32 devices in a mesh: dp: 8 (over y, x, core), fsdp: 4 (over z).
Axes of the slice: x: 2, y: 2, z: 4, core: 2. Of those that a mesh axis runs over, the one named last changes fastest.
Arguments:
- tokens: bfloat16 [16384, 768], P(('dp', 'fsdp')), may hold values from -6 to 6
- cotangent: bfloat16 [16384, 768], P(('dp', 'fsdp')), may hold values from -6 to 6
- params: bfloat16 [7087104], P(('dp', 'fsdp'))
- lengths: int32 [64, 2], P(('dp', 'fsdp')), may hold values from 39 to 98, as said below
Outputs:
- block_out: bfloat16 [16384, 768], P(('dp', 'fsdp'))
- input_grad: float32 [16384, 768], P(('dp', 'fsdp'))
- param_grad: float32 [7087104], P(('dp', 'fsdp'))
The draws below stay inside these ranges and needn't reach their ends.
Inputs may be any that keep to these rules, and one draw needn't show every extreme that they name: `lengths`: row b gives, in order, the visible patches of the 2 images packed from row 0 of buffer b; rows past their sum are padding. Every buffer holds one image of exactly 98 patches.
All inputs are finite; a program needn't handle non-finite values.
Results may differ from the reference program's by a relative error of at most 0.012.
Values may be sent and summed in bfloat16 or wider, within the bound.
A program may use at most 192 MiB of HBM per device.

```python
import math
import jax
import jax.numpy as jnp
from jax import lax

D = 768
HEADS = 12
HEAD_DIM = 64
FF = 3072
ROWS = 256
LMIN = 39
LMAX = 98
IMGS = 2
NBUF = 64
TOKENS = 16384
PARAMS = 7087104


def draw_params(key, part):
    base_draw = jnp.clip(jax.random.normal(key, (PARAMS,), jnp.float32), -3.0, 3.0)
    mean_len = 0.5 * (LMIN + LMAX)
    layout = (('gain', D, 0.15), ('shift', D, 0.3), ('matrix', 3 * D * D, 1.2 / math.sqrt(D)), ('shift', D, 0.3), ('shift', D, 0.3), ('matrix', D * D, 0.7 * math.sqrt(mean_len / D)), ('shift', D, 0.3), ('gain', D, 0.15), ('shift', D, 0.3), ('matrix', D * FF, 1.0 / math.sqrt(D)), ('shift', FF, 0.3), ('matrix', FF * D, 1.5 / math.sqrt(FF)), ('shift', D, 0.3))
    pieces = []
    offset = 0
    for piece_kind, entries, piece_scale in layout:
        segment = base_draw[offset:offset + entries]
        if piece_kind == 'gain':
            pieces.append(1.0 + piece_scale * segment)
        else:
            pieces.append(piece_scale * segment)
        offset += entries
    return jnp.concatenate(pieces).astype(jnp.bfloat16)


def draw_lengths(key, part):
    key_len, key_slot = jax.random.split(key)
    drawn_len = jax.random.randint(key_len, (NBUF, IMGS), LMIN, LMAX + 1, dtype=jnp.int32)
    chosen = jax.random.randint(key_slot, (NBUF, 1), 0, IMGS, dtype=jnp.int32)
    slot_ids = jnp.arange(IMGS, dtype=jnp.int32)[None, :]
    return jnp.where(slot_ids == chosen, LMAX, drawn_len).astype(jnp.int32)


def steps_of(rng, extent, cuts, least, top_value):
    factor_of, own = 1.0, jax.random.fold_in(rng, 6)
    for dim, parts in cuts:
        draws = jnp.exp(jax.random.uniform(jax.random.fold_in(own, dim), (parts,), jnp.float32, least / len(cuts), top_value / len(cuts)))
        factor_of = factor_of * jnp.repeat(draws, extent[dim] // parts).reshape([-1 if axis == dim else 1 for axis in range(len(extent))])
    return factor_of


def noise(own_key, shape, width, bound, cuts=(), held_as=jnp.bfloat16):
    array = width * jax.random.normal(own_key, shape, jnp.float32)
    if cuts:
        array = array * steps_of(own_key, shape, cuts, -0.22, 0.18)
    return jnp.clip(array, -bound, bound).astype(held_as)


def setup_inputs(seed: int = 0) -> dict:
    splits = jax.random.split(jax.random.key(seed), 5)
    return {
        "tokens": noise(splits[0], (TOKENS, D), 1.0, 6.0, ((0, 32),)),
        "cotangent": noise(splits[1], (TOKENS, D), 1.0, 6.0, ((0, 32),)),
        "params": draw_params(jax.random.fold_in(splits[4], 71), 0),
        "lengths": draw_lengths(jax.random.fold_in(splits[4], 71), 0),
    }


PRECISE = lax.Precision.HIGHEST
EPSILON = 1e-06
NEG_FILL = -1e+30

@jax.custom_vjp
def low(v):
    return lax.optimization_barrier(v.astype(jnp.bfloat16)).astype(jnp.float32)

@jax.custom_vjp
def low_back(v):
    return v

def low_keep(v):
    return (low(v), None)

def low_pass(kept, grad):
    return (grad,)

def back_keep(v):
    return (v, None)

def back_low(kept, grad):
    return (low(grad),)
low.defvjp(low_keep, low_pass)
low_back.defvjp(back_keep, back_low)

def layout_shapes():
    return ((D,), (D,), (D, 3 * D), (D,), (D,), (D, D), (D,), (D,), (D,), (D, FF), (FF,), (FF, D), (D,))

def unpack(flat_params):
    pieces = []
    offset = 0
    for piece_shape in layout_shapes():
        entries = math.prod(piece_shape)
        pieces.append(flat_params[offset:offset + entries].reshape(piece_shape))
        offset += entries
    return tuple(pieces)

def matmul(left, right):
    return jnp.dot(left, right, precision=PRECISE, preferred_element_type=jnp.float32)

def layer_norm(values, scale_vec, shift_vec):
    centred = values - lax.optimization_barrier(jnp.mean(values, axis=-1, keepdims=True))
    inv_std = lax.rsqrt(lax.optimization_barrier(jnp.mean(centred * centred, axis=-1, keepdims=True)) + EPSILON)
    return centred * inv_std * scale_vec + shift_vec

def one_buffer(weights, block_x, block_len):
    ln1_gain, ln1_bias, w_qkv, q_bias, v_bias, w_proj, proj_bias, ln2_gain, ln2_bias, w_fc1, fc1_bias, w_fc2, fc2_bias = weights
    seg_end = jnp.cumsum(block_len)
    positions = jnp.arange(ROWS, dtype=jnp.int32)
    segment_id = lax.optimization_barrier(jnp.sum((positions[:, None] >= seg_end[None, :]).astype(jnp.int32), axis=1))
    valid_row = (segment_id < IMGS).astype(jnp.float32)[:, None]
    allowed = segment_id[:, None] == segment_id[None, :]
    attn_in = low(layer_norm(block_x, ln1_gain, ln1_bias))
    qkv_bias = jnp.concatenate([q_bias, jnp.zeros_like(q_bias), v_bias])
    packed_qkv = low(low_back(matmul(attn_in, w_qkv) + qkv_bias))
    queries = packed_qkv[:, :D].reshape(ROWS, HEADS, HEAD_DIM)
    keys_all = packed_qkv[:, D:2 * D].reshape(ROWS, HEADS, HEAD_DIM)
    values_all = packed_qkv[:, 2 * D:].reshape(ROWS, HEADS, HEAD_DIM)
    raw_scores = jnp.einsum('rhd,chd->hrc', queries, keys_all, precision=PRECISE)
    scores = low_back(jnp.where(allowed[None], raw_scores * (1.0 / math.sqrt(HEAD_DIM)), NEG_FILL))
    row_top = lax.optimization_barrier(jnp.max(scores, axis=-1, keepdims=True))
    exp_scores = jnp.exp(scores - row_top)
    attn_probs = low(exp_scores / lax.optimization_barrier(jnp.sum(exp_scores, axis=-1, keepdims=True)))
    attn_mix = jnp.einsum('hrc,chd->rhd', attn_probs, values_all, precision=PRECISE).reshape(ROWS, D)
    attn_mix = low(low_back(attn_mix))
    resid_mid = block_x + low_back(matmul(attn_mix, w_proj) + proj_bias)
    mlp_in = low(layer_norm(resid_mid, ln2_gain, ln2_bias))
    pre_act = low_back(matmul(mlp_in, w_fc1) + fc1_bias)
    act_low = low(jax.nn.gelu(pre_act, approximate=False))
    branch = low_back(matmul(act_low, w_fc2) + fc2_bias)
    return valid_row * (resid_mid + branch)

def reference(tokens, cotangent, params, lengths):
    tok_blocks = tokens.astype(jnp.float32).reshape(NBUF, ROWS, D)
    cot_blocks = cotangent.astype(jnp.float32).reshape(NBUF, ROWS, D)
    checked = jax.checkpoint(one_buffer)

    def forward(blocks, flat_params):
        weights = unpack(flat_params)

        def step_fn(scan_carry, scan_item):
            return (scan_carry, checked(weights, scan_item[0], scan_item[1]))
        _, outputs = lax.scan(step_fn, jnp.zeros((), jnp.float32), (blocks, lengths))
        return outputs
    outputs, pullback = jax.vjp(forward, tok_blocks, params.astype(jnp.float32))
    grad_tokens, grad_params = pullback(cot_blocks)
    return (outputs.reshape(TOKENS, D).astype(jnp.bfloat16), grad_tokens.reshape(TOKENS, D), grad_params)
```

```python
import functools
import math

import jax
import jax.numpy as jnp
from jax import lax
from jax.experimental import pallas as pl
from jax.experimental.pallas import tpu as pltpu
from jax.sharding import PartitionSpec as P

AXES = ("dp", "fsdp")
LANES = 128
CORE = 3


class Place:
    def __init__(self, mesh):
        devs = mesh.devices
        spot = lambda d: (*d.coords, d.core_on_chip)
        self.shape = devs.shape
        self.digits = []
        for axis in range(2):
            line = [spot(devs[i, 0] if axis == 0 else devs[0, i]) for i in range(devs.shape[axis])]
            found, stride = [], 1
            while stride < len(line):
                delta = [b - a for a, b in zip(line[0], line[stride])]
                phys = [p for p in range(4) if delta[p]][0]
                step, size = delta[phys], 1
                while (
                    size * stride < len(line)
                    and line[size * stride][phys] - line[0][phys] == size * step
                    and all(line[size * stride][q] == line[0][q] for q in range(4) if q != phys)
                ):
                    size += 1
                found.append((phys, step, size, stride))
                stride *= size
            self.digits.append(found)
        self.size = [1, 1, 1, 1]
        for found in self.digits:
            for phys, _, size, _ in found:
                self.size[phys] *= size
        self.devices = devs.size
        self.chips = math.prod(self.size[:3])
        long = max(range(3), key=lambda p: self.size[p])
        a, b = [p for p in range(3) if p != long]
        self.orders = ((long, a, b), (long, b, a))
        self.shares = (1, 1)
        if self.chips <= 16:
            self.orders += ((a, long, b), (b, long, a))
            self.shares += (2, 2)
        self.classes = len(self.orders)

    def coords(self):
        index = [lax.axis_index(name) for name in AXES]
        out = [0, 0, 0, 0]
        for axis in range(2):
            for phys, step, size, stride in self.digits[axis]:
                out[phys] = out[phys] + ((index[axis] // stride) % size) * step
        return out

    def device(self, coords):
        out = []
        for axis in range(2):
            total = 0
            for phys, step, size, stride in self.digits[axis]:
                total = total + ((coords[phys] // step) % size) * stride
            out.append(total)
        return tuple(out)

    def flat(self, coords):
        dp, fsdp = self.device(coords)
        return dp * self.shape[1] + fsdp

    def chip(self, coords):
        return (coords[0] * self.size[1] + coords[1]) * self.size[2] + coords[2]

    def class_rows(self, rows):
        units = rows // 16
        counts = [units * share // sum(self.shares) for share in self.shares]
        counts[-1] += units - sum(counts)
        out, start = [], 0
        for count in counts:
            out.append((start * 16, count * 16))
            start += count
        return out


def flipped(mine, rel, size):
    total, bit = 0, 1
    while bit < size:
        total = total + bit * (((mine // bit) % 2 + (rel // bit) % 2) % 2)
        bit *= 2
    return total


def both(*conds):
    known = [c for c in conds if isinstance(c, bool)]
    if not all(known):
        return False
    rest = [c for c in conds if not isinstance(c, bool)]
    return functools.reduce(jnp.logical_and, rest) if rest else True


def when(cond, fn):
    if isinstance(cond, bool):
        if cond:
            fn()
    else:
        pl.when(cond)(fn)


def moved(coords, dim, by):
    out = list(coords)
    out[dim] = out[dim] + by
    return out


def partner(coords):
    out = list(coords)
    out[CORE] = 1 - out[CORE]
    return out


def neighbours(place, me):
    out = [(True, partner(me))]
    for dim in range(3):
        if place.size[dim] == 1:
            continue
        if place.size[dim] == 2:
            other = list(me)
            other[dim] = 1 - other[dim]
            out.append((True, other))
        else:
            out.append((me[dim] < place.size[dim] - 1, moved(me, dim, 1)))
            out.append((me[dim] > 0, moved(me, dim, -1)))
    return out


def greet(place, me):
    barrier = pltpu.get_barrier_semaphore()
    nbrs = neighbours(place, me)
    for cond, who in nbrs:
        when(
            cond,
            lambda who=who: pl.semaphore_signal(
                barrier, inc=1, device_id=place.device(who), device_id_type=pl.DeviceIdType.MESH
            ),
        )
    peers = sum(1 if cond is True else jnp.where(cond, 1, 0) for cond, _ in nbrs)
    pl.semaphore_wait(barrier, peers)


def onward(place, order, me, rel, src):
    out = []
    for pos in range(3):
        dim = order[pos]
        size = place.size[dim]
        if size == 1:
            continue
        later = [rel[d] == 0 for d in order[pos + 1 :]]
        if size == 2:
            other = list(me)
            other[dim] = 1 - other[dim]
            out.append((both(*later, rel[dim] == 0), pos, 0, other))
        else:
            for way, by in ((0, 1), (1, -1)):
                if by == 1:
                    here = both(me[dim] >= src[dim], me[dim] < size - 1)
                else:
                    here = both(me[dim] <= src[dim], me[dim] > 0)
                cond = both(*later, here)
                out.append((cond, pos, way, moved(me, dim, by)))
    return out


def walk(place, body, reverse=False):
    sizes = place.size[:3]
    if place.chips <= 16:
        rels = [
            (x, y, z) for x in range(sizes[0]) for y in range(sizes[1]) for z in range(sizes[2])
        ]
        rels.sort(key=lambda r: (sum(r), r), reverse=reverse)
        for rel in rels:
            body(rel)
        return

    def step(i, carry):
        i = place.chips - 1 - i if reverse else i
        body((i % sizes[0], (i // sizes[0]) % sizes[1], i // (sizes[0] * sizes[1])))
        return carry

    lax.fori_loop(0, place.chips, step, 0)


def source_of(place, me, rel):
    return [flipped(me[d], rel[d], place.size[d]) for d in range(3)] + [me[CORE]]


def gather_all(place, me, held, send, recv, cross):
    rows = held.shape[1]
    parts = place.class_rows(rows)

    def copy(k, src, slot, sem, who):
        start, count = parts[k]
        ref = held.at[place.flat(src), pl.ds(start, count), :]
        return pltpu.make_async_remote_copy(
            src_ref=ref,
            dst_ref=ref,
            send_sem=send.at[k, place.chip(src), slot],
            recv_sem=sem.at[k, place.chip(src)],
            device_id=place.device(who),
            device_id_type=pl.DeviceIdType.MESH,
        )

    def sends(k, rel, src, act):
        for cond, pos, way, who in onward(place, place.orders[k], me, rel, src):
            when(cond, lambda: act(copy(k, src, pos * 2 + way, recv, who)))
        act(copy(k, src, 6, cross, partner(me)))

    def go(rel):
        src = source_of(place, me, rel)
        first = [r == 0 for r in rel]
        for k in range(place.classes):
            if all(isinstance(f, bool) for f in first):
                if not all(first):
                    copy(k, src, 0, recv, me).wait_recv()
            else:
                when(
                    jnp.logical_not(both(*first)),
                    lambda: copy(k, src, 0, recv, me).wait_recv(),
                )
            sends(k, rel, src, lambda c: c.start())

    walk(place, go)

    def drain(rel):
        src = source_of(place, me, rel)
        theirs = partner(src)
        for k in range(place.classes):
            sends(k, rel, src, lambda c: c.wait_send())
            copy(k, theirs, 0, cross, me).wait_recv()

    walk(place, drain)


def gather_sems(place):
    return [
        pltpu.SemaphoreType.DMA((place.classes, place.chips, 7)),
        pltpu.SemaphoreType.DMA((place.classes, place.chips)),
        pltpu.SemaphoreType.DMA((place.classes, place.chips)),
    ]


def slot_plan(place, rows):
    plan = []
    for order in place.orders:
        starts, total = [], 0
        for pos in range(3):
            before = math.prod(place.size[d] for d in order[:pos])
            size = place.size[order[pos]]
            starts.append(total)
            total += before * (1 if size == 2 else size + 1 if size > 1 else 0)
        plan.append((starts, total))
    return plan


def slot_of(place, plan, k, pos, way, at, dest):
    order = place.orders[k]
    index = 0
    for d in order[:pos]:
        index = index * place.size[d] + dest[d]
    dim = order[pos]
    size = place.size[dim]
    if size > 2:
        spot = dest[dim]
        if way == 1:
            spot = spot + jnp.where(at[dim] == dest[dim], size - dest[dim], 0)
        index = index * (size + 1) + spot
    return plan[k][0][pos] + index


def add_rows(dst, a, b, count, step=16):
    def body(i, carry):
        r = pl.ds(pl.multiple_of(i * step, step), step)
        dst(r, a(r).astype(jnp.float32) + b(r).astype(jnp.float32))
        return carry

    lax.fori_loop(0, count // step, body, 0)


def scatter_all(place, me, own, cross, slots, total, sems):
    cross_send, cross_recv, send, recv = sems
    rows = own.shape[1]
    parts = place.class_rows(rows)
    plan = slot_plan(place, rows)

    def swap(dest):
        return pltpu.make_async_remote_copy(
            src_ref=own.at[place.flat(partner(dest))],
            dst_ref=cross.at[place.chip(dest)],
            send_sem=cross_send.at[place.chip(dest)],
            recv_sem=cross_recv.at[place.chip(dest)],
            device_id=place.device(partner(me)),
            device_id_type=pl.DeviceIdType.MESH,
        )

    def pass_on(k, pos, way, dest, to):
        start, count = parts[k]
        slot = slot_of(place, plan, k, pos, way, to, dest)
        return pltpu.make_async_remote_copy(
            src_ref=own.at[place.flat(dest), pl.ds(start, count), :],
            dst_ref=slots[k].at[slot],
            send_sem=send.at[k, place.chip(dest)],
            recv_sem=recv[k].at[slot],
            device_id=place.device(to),
            device_id_type=pl.DeviceIdType.MESH,
        )

    def parents(k, rel, dest):
        order = place.orders[k]
        out = []
        for pos in range(3):
            dim = order[pos]
            size = place.size[dim]
            if size == 1:
                continue
            later = both(*[rel[d] == 0 for d in order[pos + 1 :]])
            if size == 2:
                other = list(me)
                other[dim] = 1 - other[dim]
                away = rel[dim] == 1
                out.append((both(later, away), pos, 0, other))
            else:
                out.append((both(later, me[dim] > dest[dim]), pos, 0, moved(me, dim, -1)))
                out.append((both(later, me[dim] < dest[dim]), pos, 1, moved(me, dim, 1)))
        return out

    walk(place, lambda rel: swap(source_of(place, me, rel)).start(), reverse=True)

    def go(rel):
        dest = source_of(place, me, rel)
        home = both(*[r == 0 for r in rel])
        flat, chip = place.flat(dest), place.chip(dest)
        swap(dest).wait_recv()

        def mix(final):
            for k in range(place.classes):
                start, count = parts[k]

                def rows_of(r):
                    return pl.ds(r.start + start, r.size)

                if final:

                    def put(r, v):
                        total[rows_of(r), :] = v

                    def held(r):
                        return total[rows_of(r), :]

                else:

                    def put(r, v):
                        own[flat, rows_of(r), :] = v.astype(own.dtype)

                    def held(r):
                        return own[flat, rows_of(r), :]

                add_rows(
                    put,
                    lambda r: own[flat, rows_of(r), :],
                    lambda r: cross[chip, rows_of(r), :],
                    count,
                )
                for cond, pos, way, who in onward(place, place.orders[k], me, rel, dest):

                    def take():
                        slot = slot_of(place, plan, k, pos, way, me, dest)
                        pass_on(k, pos, way, dest, me).wait_recv()
                        add_rows(put, held, lambda r: slots[k][slot, r, :], count)

                    when(cond, take)
                if not final:
                    for cond, pos, way, who in parents(k, rel, dest):
                        when(cond, lambda: pass_on(k, pos, way, dest, who).start())

        if isinstance(home, bool):
            mix(home)
        else:
            pl.when(home)(lambda: mix(True))
            pl.when(jnp.logical_not(home))(lambda: mix(False))

    walk(place, go, reverse=True)

    def drain(rel):
        dest = source_of(place, me, rel)
        swap(dest).wait_send()
        for k in range(place.classes):
            for cond, pos, way, who in parents(k, rel, dest):
                when(cond, lambda: pass_on(k, pos, way, dest, who).wait_send())

    walk(place, drain)


def scatter_scratch(place, rows):
    parts = place.class_rows(rows)
    plan = slot_plan(place, rows)
    dma = pltpu.SemaphoreType.DMA
    return (
        [pltpu.VMEM((place.chips, rows, LANES), jnp.bfloat16)],
        [pltpu.VMEM((plan[k][1], parts[k][1], LANES), jnp.bfloat16) for k in range(place.classes)],
        [dma((place.chips,)), dma((place.chips,)), dma((place.classes, place.chips))],
        [dma((plan[k][1],)) for k in range(place.classes)],
    )


D = 768
HEAD_DIM = 64
FF = 3072
EPSILON = 1e-06
NEG_FILL = -1e30
ROOT_HALF = 0.7071067811865476
INV_ROOT_TWO_PI = 0.3989422804014327

PIECES = (
    ("ln1_gain", (D,)),
    ("ln1_bias", (D,)),
    ("w_qkv", (D, 3 * D)),
    ("q_bias", (D,)),
    ("v_bias", (D,)),
    ("w_proj", (D, D)),
    ("proj_bias", (D,)),
    ("ln2_gain", (D,)),
    ("ln2_bias", (D,)),
    ("w_fc1", (D, FF)),
    ("fc1_bias", (FF,)),
    ("w_fc2", (FF, D)),
    ("fc2_bias", (D,)),
)
MATRICES = tuple(name for name, shape in PIECES if len(shape) == 2)
VECTORS = tuple(name for name, shape in PIECES if len(shape) == 1)
SHAPES = dict(PIECES)


def row_bases():
    bases, row = {}, 0
    for name, shape in PIECES:
        bases[name] = row
        row += math.prod(shape) // LANES
    return bases, row


BASES, TOTAL_ROWS = row_bases()
VECTOR_ROWS = sum(SHAPES[name][0] // LANES for name in VECTORS)
MESH = pl.DeviceIdType.MESH


def part_rows(entries):
    return -(-((LANES - 1 + entries - 1) // LANES + 1) // 16) * 16


def tile(i):
    return pl.ds(pl.multiple_of(i * 16, 16), 16)


def loop(count, body):
    def step(i, carry):
        body(i)
        return carry

    lax.fori_loop(0, count, step, 0)


def aligned(raw, held, stage, which, entries):
    rows = held.shape[1]
    shift = (entries * which) % LANES
    stage[0:8, :] = jnp.zeros((8, LANES), jnp.float32)

    def turn(i):
        stage[pl.ds(pl.multiple_of(i * 16 + 8, 8), 16), :] = pltpu.roll(
            raw[tile(i), :].astype(jnp.float32), shift, 1
        )

    loop(rows // 16, turn)

    def merge(i):
        lane = lax.broadcasted_iota(jnp.int32, (16, LANES), 1)
        now = stage[pl.ds(i * 16 + 8, 16), :]
        before = stage[pl.ds(i * 16 + 7, 16), :]
        held[which, tile(i), :] = jnp.where(lane < shift, before, now).astype(held.dtype)

    loop(rows // 16, merge)


def spread(held, stage, entries):
    rows = held.shape[1]

    def one(d):
        base = (entries * d) // LANES
        cut = (entries * d) % LANES
        first = stage[pl.ds(base, 1), :]

        def body(i):
            stage[pl.ds(base + i * 16, 16), :] = held[d, tile(i), :].astype(jnp.float32)

        loop(rows // 16, body)
        row = stage[pl.ds(base, 1), :]
        stage[pl.ds(base, 1), :] = jnp.where(cut != 0, row + first, row)

    loop(held.shape[0], one)


def form(stage, name, out):
    depth, width = SHAPES[name]
    blocks = width // LANES

    def body(i):
        for j in range(blocks):
            start = BASES[name] + i * 16 * blocks + j
            out[tile(i), j * LANES : (j + 1) * LANES] = stage[
                pl.ds(start, 16, stride=blocks), :
            ].astype(out.dtype)

    loop(depth // 16, body)


def gather_kernel(place, entries, raw, *refs):
    mats, vecs = refs[:4], refs[4]
    held, stage = refs[5:7]
    forms = refs[7:11]
    send, recv, cross, done = refs[11:]
    me = place.coords()
    aligned(raw, held, stage, place.flat(me), entries)
    greet(place, me)
    gather_all(place, me, held, send, recv, cross)
    spread(held, stage, entries)
    for i, name in enumerate(MATRICES):
        form(stage, name, forms[i])
        pltpu.make_async_copy(forms[i], mats[i], done.at[i]).start()
    row = 0
    for name in VECTORS:
        count = SHAPES[name][0] // LANES
        vecs[row : row + count, :] = stage[BASES[name] : BASES[name] + count, :]
        row += count
    for i in range(4):
        pltpu.make_async_copy(forms[i], mats[i], done.at[i]).wait()


def gathered(place, params):
    entries = params.shape[0]
    rows = part_rows(entries)
    raw = jnp.pad(params, (0, rows * LANES - entries)).reshape(rows, LANES)
    any_spec = pl.BlockSpec(memory_space=pl.ANY)
    vmem = pl.BlockSpec(memory_space=pltpu.VMEM)
    *mats, vecs = pl.pallas_call(
        functools.partial(gather_kernel, place, entries),
        out_shape=[jax.ShapeDtypeStruct(SHAPES[n], jnp.bfloat16) for n in MATRICES]
        + [jax.ShapeDtypeStruct((VECTOR_ROWS, LANES), jnp.float32)],
        in_specs=[vmem],
        out_specs=[any_spec] * 4 + [vmem],
        scratch_shapes=[
            pltpu.VMEM((place.devices, rows, LANES), jnp.bfloat16),
            pltpu.VMEM((TOTAL_ROWS + 32, LANES), jnp.float32),
        ]
        + [pltpu.VMEM(SHAPES[n], jnp.bfloat16) for n in MATRICES]
        + gather_sems(place)
        + [pltpu.SemaphoreType.DMA((4,))],
        compiler_params=pltpu.CompilerParams(
            collective_id=0, has_side_effects=True, vmem_limit_bytes=66 * 10**6
        ),
        name="gather",
    )(raw)
    out = dict(zip(MATRICES, mats))
    flat, row = vecs.reshape(-1), 0
    for name in VECTORS:
        out[name] = flat[row : row + SHAPES[name][0]]
        row += SHAPES[name][0]
    return out


def chunk_depth(name):
    return 96 if SHAPES[name][0] == D else 384


def scatter_kernel(place, entries, *refs):
    grads, vecs, out = refs[:4], refs[4], refs[5]
    own, cross = refs[6:8]
    n = place.classes
    slots, refs = refs[8 : 8 + n], refs[8 + n :]
    cross_send, cross_recv, send = refs[:3]
    recv, refs = refs[3 : 3 + n], refs[3 + n :]
    stage, total = refs[:2]
    bufs = refs[2:6]
    load = refs[6]
    rows = own.shape[1]
    me = place.coords()

    row = 0
    for name in VECTORS:
        count = SHAPES[name][0] // LANES
        stage[BASES[name] : BASES[name] + count, :] = vecs[row : row + count, :]
        row += count
    stage[TOTAL_ROWS : TOTAL_ROWS + 32, :] = jnp.zeros((32, LANES), jnp.float32)

    for m, name in enumerate(MATRICES):
        depth, width = SHAPES[name]
        blocks = width // LANES
        chunk = chunk_depth(name)
        count = depth // chunk

        def fetch(c, slot):
            return pltpu.make_async_copy(
                grads[m].at[pl.ds(pl.multiple_of(c * chunk, chunk), chunk), :],
                bufs[m].at[slot],
                load.at[slot],
            )

        fetch(0, 0).start()

        def body(c):
            slot = c % 2
            fetch(c, slot).wait()

            @pl.when(c + 1 < count)
            def _():
                fetch(c + 1, 1 - slot).start()

            def lay(i):
                for j in range(blocks):
                    start = BASES[name] + (c * chunk + i * 16) * blocks + j
                    stage[pl.ds(start, 16, stride=blocks), :] = bufs[m][
                        slot, tile(i), j * LANES : (j + 1) * LANES
                    ].astype(jnp.float32)

            loop(chunk // 16, lay)

        loop(count, body)

    def cut(d):
        base = (entries * d) // LANES

        def body(i):
            own[d, tile(i), :] = stage[pl.ds(base + i * 16, 16), :].astype(own.dtype)

        loop(rows // 16, body)

    loop(place.devices, cut)
    greet(place, me)
    scatter_all(place, me, own, cross, slots, total, (cross_send, cross_recv, send, recv))

    shift = (entries * place.flat(me)) % LANES
    back = (LANES - shift) % LANES

    def turn(i):
        total[tile(i), :] = pltpu.roll(total[tile(i), :], back, 1)

    loop(rows // 16, turn)

    def merge(i):
        lane = lax.broadcasted_iota(jnp.int32, (16, LANES), 1)
        now = total[pl.ds(i * 16, 16), :]
        after = total[pl.ds(i * 16 + 1, 16), :]
        out[tile(i), :] = jnp.where(lane < LANES - shift, now, after)

    loop(rows // 16, merge)


def scattered(place, grads, entries):
    rows = part_rows(entries)
    vecs = jnp.concatenate([grads[n] for n in VECTORS]).reshape(VECTOR_ROWS, LANES)
    mats = [grads[n].astype(jnp.bfloat16) for n in MATRICES]
    cross, slots, sems, recv = scatter_scratch(place, rows)
    any_spec = pl.BlockSpec(memory_space=pl.ANY)
    vmem = pl.BlockSpec(memory_space=pltpu.VMEM)
    out = pl.pallas_call(
        functools.partial(scatter_kernel, place, entries),
        out_shape=jax.ShapeDtypeStruct((rows, LANES), jnp.float32),
        in_specs=[any_spec] * 4 + [vmem],
        out_specs=vmem,
        scratch_shapes=[pltpu.VMEM((place.devices, rows, LANES), jnp.bfloat16)]
        + cross
        + slots
        + sems
        + recv
        + [
            pltpu.VMEM((TOTAL_ROWS + 32, LANES), jnp.float32),
            pltpu.VMEM((rows + 16, LANES), jnp.float32),
        ]
        + [pltpu.VMEM((2, chunk_depth(n), SHAPES[n][1]), jnp.bfloat16) for n in MATRICES]
        + [pltpu.SemaphoreType.DMA((2,))],
        compiler_params=pltpu.CompilerParams(
            collective_id=1, has_side_effects=True, vmem_limit_bytes=67 * 10**6
        ),
        name="scatter",
    )(*mats, vecs)
    return out.reshape(-1)[:entries]


def norm_rows(values, gain, bias):
    centred = values - jnp.mean(values, axis=-1, keepdims=True)
    inv_std = lax.rsqrt(jnp.mean(centred * centred, axis=-1, keepdims=True) + EPSILON)
    normed = centred * inv_std
    return normed * gain + bias, normed, inv_std


def norm_back(grad_out, normed, inv_std, gain):
    grad_norm = grad_out * gain
    return inv_std * (
        grad_norm
        - jnp.mean(grad_norm, axis=-1, keepdims=True)
        - normed * jnp.mean(grad_norm * normed, axis=-1, keepdims=True)
    )


def dot(a, b, dims):
    return lax.dot_general(a, b, (dims, ((), ())), preferred_element_type=jnp.float32)


def block(w, tokens, cotangent, lengths):
    low = lambda v: v.astype(jnp.bfloat16)
    buffers = lengths.shape[0]
    total, width = tokens.shape
    rows = total // buffers
    heads = width // HEAD_DIM
    seg_end = jnp.cumsum(lengths, axis=1)
    positions = jnp.arange(rows, dtype=jnp.int32)
    segment = jnp.sum((positions[None, :, None] >= seg_end[:, None, :]).astype(jnp.int32), axis=2)
    valid = (segment < lengths.shape[1]).astype(jnp.float32).reshape(total, 1)
    allowed = (segment[:, :, None] == segment[:, None, :])[:, None]

    x = tokens.astype(jnp.float32)
    attn_full, normed1, inv1 = norm_rows(x, w["ln1_gain"], w["ln1_bias"])
    attn_in = low(attn_full)
    bias = jnp.concatenate([w["q_bias"], jnp.zeros_like(w["q_bias"]), w["v_bias"]])
    qkv = low(dot(attn_in, w["w_qkv"], ((1,), (0,))) + bias)
    q, k, v = (
        qkv[:, i * width : (i + 1) * width].reshape(buffers, rows, heads, HEAD_DIM)
        for i in range(3)
    )
    ein = functools.partial(jnp.einsum, preferred_element_type=jnp.float32)
    scale = 1.0 / math.sqrt(HEAD_DIM)
    scores = jnp.where(allowed, ein("brhd,bchd->bhrc", q, k) * scale, NEG_FILL)
    exps = jnp.exp(scores - jnp.max(scores, axis=-1, keepdims=True))
    probs = exps / jnp.sum(exps, axis=-1, keepdims=True)
    probs_low = low(probs)
    mix = low(ein("bhrc,bchd->brhd", probs_low, v).reshape(total, width))
    mid = x + dot(mix, w["w_proj"], ((1,), (0,))) + w["proj_bias"]
    mlp_full, normed2, inv2 = norm_rows(mid, w["ln2_gain"], w["ln2_bias"])
    mlp_in = low(mlp_full)
    pre = dot(mlp_in, w["w_fc1"], ((1,), (0,))) + w["fc1_bias"]
    phi = 0.5 * (1.0 + lax.erf(pre * ROOT_HALF))
    act = low(pre * phi)
    slope = phi + pre * jnp.exp(-0.5 * pre * pre) * INV_ROOT_TWO_PI
    out = valid * (mid + dot(act, w["w_fc2"], ((1,), (0,))) + w["fc2_bias"])

    g = {}
    g_full = cotangent.astype(jnp.float32) * valid
    g_low = low(g_full)
    g["w_fc2"] = dot(act, g_low, ((0,), (0,)))
    g["fc2_bias"] = jnp.sum(g_low, axis=0, dtype=jnp.float32)
    g_pre = low(dot(g_low, w["w_fc2"], ((1,), (1,))) * slope)
    g["w_fc1"] = dot(mlp_in, g_pre, ((0,), (0,)))
    g["fc1_bias"] = jnp.sum(g_pre, axis=0, dtype=jnp.float32)
    g_mlp = dot(g_pre, w["w_fc1"], ((1,), (1,)))
    g["ln2_gain"] = jnp.sum(g_mlp * normed2, axis=0)
    g["ln2_bias"] = jnp.sum(g_mlp, axis=0)
    g_mid = g_full + norm_back(g_mlp, normed2, inv2, w["ln2_gain"])
    g_mid_low = low(g_mid)
    g["w_proj"] = dot(mix, g_mid_low, ((0,), (0,)))
    g["proj_bias"] = jnp.sum(g_mid_low, axis=0, dtype=jnp.float32)
    g_mix = low(dot(g_mid_low, w["w_proj"], ((1,), (1,)))).reshape(buffers, rows, heads, HEAD_DIM)
    g_probs = ein("brhd,bchd->bhrc", g_mix, v)
    g_v = ein("bhrc,brhd->bchd", probs_low, g_mix)
    g_scores = low(probs * (g_probs - jnp.sum(probs * g_probs, axis=-1, keepdims=True)))
    g_q = ein("bhrc,bchd->brhd", g_scores, k) * scale
    g_k = ein("bhrc,brhd->bchd", g_scores, q) * scale
    g_qkv = low(jnp.concatenate([t.reshape(total, width) for t in (g_q, g_k, g_v)], axis=1))
    g["w_qkv"] = dot(attn_in, g_qkv, ((0,), (0,)))
    sums = jnp.sum(g_qkv, axis=0, dtype=jnp.float32)
    g["q_bias"], g["v_bias"] = sums[:width], sums[2 * width :]
    g_attn = dot(g_qkv, w["w_qkv"], ((1,), (1,)))
    g["ln1_gain"] = jnp.sum(g_attn * normed1, axis=0)
    g["ln1_bias"] = jnp.sum(g_attn, axis=0)
    g_x = g_mid + norm_back(g_attn, normed1, inv1, w["ln1_gain"])
    return low(out), g_x, g


def solution(mesh):
    place = Place(mesh)

    def shards(tokens, cotangent, params, lengths):
        weights = gathered(place, params)
        out, g_x, grads = block(weights, tokens, cotangent, lengths)
        return out, g_x, scattered(place, grads, params.shape[0])

    rows, flat = P(AXES, None), P(AXES)
    return jax.shard_map(
        shards,
        mesh=mesh,
        in_specs=(rows, rows, flat, rows),
        out_specs=(rows, rows, flat),
        check_vma=False,
    )
```

```python
import functools
import math

import jax
import jax.numpy as jnp
from jax import lax
from jax.experimental import pallas as pl
from jax.experimental.pallas import tpu as pltpu
from jax.sharding import PartitionSpec as P

AXES = ("dp", "fsdp")
LANES = 128
CORE = 3


class Place:
    def __init__(self, mesh):
        devs = mesh.devices
        spot = lambda d: (*d.coords, d.core_on_chip)
        self.shape = devs.shape
        self.digits = []
        for axis in range(2):
            line = [spot(devs[i, 0] if axis == 0 else devs[0, i]) for i in range(devs.shape[axis])]
            found, stride = [], 1
            while stride < len(line):
                delta = [b - a for a, b in zip(line[0], line[stride])]
                phys = [p for p in range(4) if delta[p]][0]
                step, size = delta[phys], 1
                while (
                    size * stride < len(line)
                    and line[size * stride][phys] - line[0][phys] == size * step
                    and all(line[size * stride][q] == line[0][q] for q in range(4) if q != phys)
                ):
                    size += 1
                found.append((phys, step, size, stride))
                stride *= size
            self.digits.append(found)
        self.size = [1, 1, 1, 1]
        for found in self.digits:
            for phys, _, size, _ in found:
                self.size[phys] *= size
        self.devices = devs.size
        self.chips = math.prod(self.size[:3])
        long = max(range(3), key=lambda p: self.size[p])
        a, b = [p for p in range(3) if p != long]
        self.orders = ((long, a, b), (long, b, a))
        self.shares = (1, 1)
        if self.chips <= 16:
            self.orders += ((a, long, b), (b, long, a))
            self.shares += (2, 2)
        self.classes = len(self.orders)

    def coords(self):
        index = [lax.axis_index(name) for name in AXES]
        out = [0, 0, 0, 0]
        for axis in range(2):
            for phys, step, size, stride in self.digits[axis]:
                out[phys] = out[phys] + ((index[axis] // stride) % size) * step
        return out

    def device(self, coords):
        out = []
        for axis in range(2):
            total = 0
            for phys, step, size, stride in self.digits[axis]:
                total = total + ((coords[phys] // step) % size) * stride
            out.append(total)
        return tuple(out)

    def flat(self, coords):
        dp, fsdp = self.device(coords)
        return dp * self.shape[1] + fsdp

    def chip(self, coords):
        return (coords[0] * self.size[1] + coords[1]) * self.size[2] + coords[2]

    def class_rows(self, rows):
        units = rows // 16
        counts = [units * share // sum(self.shares) for share in self.shares]
        counts[-1] += units - sum(counts)
        out, start = [], 0
        for count in counts:
            out.append((start * 16, count * 16))
            start += count
        return out


def flipped(mine, rel, size):
    total, bit = 0, 1
    while bit < size:
        total = total + bit * (((mine // bit) % 2 + (rel // bit) % 2) % 2)
        bit *= 2
    return total


def both(*conds):
    known = [c for c in conds if isinstance(c, bool)]
    if not all(known):
        return False
    rest = [c for c in conds if not isinstance(c, bool)]
    return functools.reduce(jnp.logical_and, rest) if rest else True


def when(cond, fn):
    if isinstance(cond, bool):
        if cond:
            fn()
    else:
        pl.when(cond)(fn)


def moved(coords, dim, by):
    out = list(coords)
    out[dim] = out[dim] + by
    return out


def partner(coords):
    out = list(coords)
    out[CORE] = 1 - out[CORE]
    return out


def neighbours(place, me):
    out = [(True, partner(me))]
    for dim in range(3):
        if place.size[dim] == 1:
            continue
        if place.size[dim] == 2:
            other = list(me)
            other[dim] = 1 - other[dim]
            out.append((True, other))
        else:
            out.append((me[dim] < place.size[dim] - 1, moved(me, dim, 1)))
            out.append((me[dim] > 0, moved(me, dim, -1)))
    return out


def greet(place, me):
    barrier = pltpu.get_barrier_semaphore()
    nbrs = neighbours(place, me)
    for cond, who in nbrs:
        when(
            cond,
            lambda who=who: pl.semaphore_signal(
                barrier, inc=1, device_id=place.device(who), device_id_type=pl.DeviceIdType.MESH
            ),
        )
    peers = sum(1 if cond is True else jnp.where(cond, 1, 0) for cond, _ in nbrs)
    pl.semaphore_wait(barrier, peers)


def onward(place, order, me, rel, src):
    out = []
    for pos in range(3):
        dim = order[pos]
        size = place.size[dim]
        if size == 1:
            continue
        later = [rel[d] == 0 for d in order[pos + 1 :]]
        if size == 2:
            other = list(me)
            other[dim] = 1 - other[dim]
            out.append((both(*later, rel[dim] == 0), pos, 0, other))
        else:
            for way, by in ((0, 1), (1, -1)):
                if by == 1:
                    here = both(me[dim] >= src[dim], me[dim] < size - 1)
                else:
                    here = both(me[dim] <= src[dim], me[dim] > 0)
                cond = both(*later, here)
                out.append((cond, pos, way, moved(me, dim, by)))
    return out


PASSES = (
    0, 16, 32, 48, 1, 17, 40, 33, 52, 49, 41, 56, 3, 8, 2, 20, 35, 34, 10, 53, 18, 28,
    11, 5, 51, 36, 12, 19, 45, 57, 50, 9, 7, 21, 55, 54, 60, 25, 44, 6, 22, 29, 24, 42,
    58, 27, 37, 26, 59, 43, 15, 23, 4, 39, 61, 14, 30, 13, 62, 38, 63, 31, 47, 46,
)


def walk_parts(place, body, reverse=False, after=None):
    if place.size[:3] == [2, 2, 4]:
        for i, code in enumerate(PASSES[::-1] if reverse else PASSES):
            body(code // 16, ((code // 8) % 2, (code // 4) % 2, code % 4))
            if after is not None:
                after(i)
        return

    def each(rel):
        for k in range(place.classes):
            body(k, rel)

    walk(place, each, reverse)
    if after is not None:
        after(None)


def walk(place, body, reverse=False):
    sizes = place.size[:3]
    if place.chips <= 16:
        rels = [
            (x, y, z) for x in range(sizes[0]) for y in range(sizes[1]) for z in range(sizes[2])
        ]
        rels.sort(key=lambda r: (sum(r), r), reverse=reverse)
        for rel in rels:
            body(rel)
        return

    def step(i, carry):
        i = place.chips - 1 - i if reverse else i
        body((i % sizes[0], (i // sizes[0]) % sizes[1], i // (sizes[0] * sizes[1])))
        return carry

    lax.fori_loop(0, place.chips, step, 0)


def source_of(place, me, rel):
    return [flipped(me[d], rel[d], place.size[d]) for d in range(3)] + [me[CORE]]


def gather_all(place, me, held, send, recv, cross, after=None):
    rows = held.shape[1]
    parts = place.class_rows(rows)

    def copy(k, src, slot, sem, who):
        start, count = parts[k]
        ref = held.at[place.flat(src), pl.ds(start, count), :]
        return pltpu.make_async_remote_copy(
            src_ref=ref,
            dst_ref=ref,
            send_sem=send.at[k, place.chip(src), slot],
            recv_sem=sem.at[k, place.chip(src)],
            device_id=place.device(who),
            device_id_type=pl.DeviceIdType.MESH,
        )

    def sends(k, rel, src, act):
        for cond, pos, way, who in onward(place, place.orders[k], me, rel, src):
            when(cond, lambda: act(copy(k, src, pos * 2 + way, recv, who)))
        act(copy(k, src, 6, cross, partner(me)))

    def go(k, rel):
        src = source_of(place, me, rel)
        home = both(*[r == 0 for r in rel])
        if home is not True:
            away = True if home is False else jnp.logical_not(home)
            when(away, lambda: copy(k, src, 0, recv, me).wait_recv())
        sends(k, rel, src, lambda c: c.start())

    walk_parts(place, go, after=after)

    def drain(rel):
        src = source_of(place, me, rel)
        theirs = partner(src)
        for k in range(place.classes):
            sends(k, rel, src, lambda c: c.wait_send())
            copy(k, theirs, 0, cross, me).wait_recv()

    walk(place, drain)


def gather_sems(place):
    return [
        pltpu.SemaphoreType.DMA((place.classes, place.chips, 7)),
        pltpu.SemaphoreType.DMA((place.classes, place.chips)),
        pltpu.SemaphoreType.DMA((place.classes, place.chips)),
    ]


def slot_plan(place, rows):
    plan = []
    for order in place.orders:
        starts, total = [], 0
        for pos in range(3):
            before = math.prod(place.size[d] for d in order[:pos])
            size = place.size[order[pos]]
            starts.append(total)
            total += before * (1 if size == 2 else size + 1 if size > 1 else 0)
        plan.append((starts, total))
    return plan


def slot_of(place, plan, k, pos, way, at, dest):
    order = place.orders[k]
    index = 0
    for d in order[:pos]:
        index = index * place.size[d] + dest[d]
    dim = order[pos]
    size = place.size[dim]
    if size > 2:
        spot = dest[dim]
        if way == 1:
            spot = spot + jnp.where(at[dim] == dest[dim], size - dest[dim], 0)
        index = index * (size + 1) + spot
    return plan[k][0][pos] + index


def add_rows(dst, a, b, count, step=16):
    def body(i, carry):
        r = pl.ds(pl.multiple_of(i * step, step), step)
        dst(r, a(r).astype(jnp.float32) + b(r).astype(jnp.float32))
        return carry

    lax.fori_loop(0, count // step, body, 0)


def scatter_all(place, me, own, cross, slots, total, sems):
    cross_send, cross_recv, send, recv = sems
    rows = own.shape[1]
    parts = place.class_rows(rows)
    plan = slot_plan(place, rows)

    def swap(dest):
        return pltpu.make_async_remote_copy(
            src_ref=own.at[place.flat(partner(dest))],
            dst_ref=cross.at[place.chip(dest)],
            send_sem=cross_send.at[place.chip(dest)],
            recv_sem=cross_recv.at[place.chip(dest)],
            device_id=place.device(partner(me)),
            device_id_type=pl.DeviceIdType.MESH,
        )

    def pass_on(k, pos, way, dest, to):
        start, count = parts[k]
        slot = slot_of(place, plan, k, pos, way, to, dest)
        return pltpu.make_async_remote_copy(
            src_ref=own.at[place.flat(dest), pl.ds(start, count), :],
            dst_ref=slots[k].at[slot],
            send_sem=send.at[k, place.chip(dest)],
            recv_sem=recv[k].at[slot],
            device_id=place.device(to),
            device_id_type=pl.DeviceIdType.MESH,
        )

    def parents(k, rel, dest):
        order = place.orders[k]
        out = []
        for pos in range(3):
            dim = order[pos]
            size = place.size[dim]
            if size == 1:
                continue
            later = both(*[rel[d] == 0 for d in order[pos + 1 :]])
            if size == 2:
                other = list(me)
                other[dim] = 1 - other[dim]
                away = rel[dim] == 1
                out.append((both(later, away), pos, 0, other))
            else:
                out.append((both(later, me[dim] > dest[dim]), pos, 0, moved(me, dim, -1)))
                out.append((both(later, me[dim] < dest[dim]), pos, 1, moved(me, dim, 1)))
        return out

    walk(place, lambda rel: swap(source_of(place, me, rel)).start(), reverse=True)

    def go(rel):
        dest = source_of(place, me, rel)
        home = both(*[r == 0 for r in rel])
        flat, chip = place.flat(dest), place.chip(dest)
        swap(dest).wait_recv()

        def mix(final):
            for k in range(place.classes):
                start, count = parts[k]

                def rows_of(r):
                    return pl.ds(r.start + start, r.size)

                if final:

                    def put(r, v):
                        total[rows_of(r), :] = v

                    def held(r):
                        return total[rows_of(r), :]

                else:

                    def put(r, v):
                        own[flat, rows_of(r), :] = v.astype(own.dtype)

                    def held(r):
                        return own[flat, rows_of(r), :]

                add_rows(
                    put,
                    lambda r: own[flat, rows_of(r), :],
                    lambda r: cross[chip, rows_of(r), :],
                    count,
                )
                for cond, pos, way, who in onward(place, place.orders[k], me, rel, dest):

                    def take():
                        slot = slot_of(place, plan, k, pos, way, me, dest)
                        pass_on(k, pos, way, dest, me).wait_recv()
                        add_rows(put, held, lambda r: slots[k][slot, r, :], count)

                    when(cond, take)
                if not final:
                    for cond, pos, way, who in parents(k, rel, dest):
                        when(cond, lambda: pass_on(k, pos, way, dest, who).start())

        if isinstance(home, bool):
            mix(home)
        else:
            pl.when(home)(lambda: mix(True))
            pl.when(jnp.logical_not(home))(lambda: mix(False))

    walk(place, go, reverse=True)

    def drain(rel):
        dest = source_of(place, me, rel)
        swap(dest).wait_send()
        for k in range(place.classes):
            for cond, pos, way, who in parents(k, rel, dest):
                when(cond, lambda: pass_on(k, pos, way, dest, who).wait_send())

    walk(place, drain)


def scatter_scratch(place, rows):
    parts = place.class_rows(rows)
    plan = slot_plan(place, rows)
    dma = pltpu.SemaphoreType.DMA
    return (
        [pltpu.VMEM((place.chips, rows, LANES), jnp.bfloat16)],
        [pltpu.VMEM((plan[k][1], parts[k][1], LANES), jnp.bfloat16) for k in range(place.classes)],
        [dma((place.chips,)), dma((place.chips,)), dma((place.classes, place.chips))],
        [dma((plan[k][1],)) for k in range(place.classes)],
    )


D = 768
HEAD_DIM = 64
FF = 3072
EPSILON = 1e-06
NEG_FILL = -1e30
ROOT_HALF = 0.7071067811865476
INV_ROOT_TWO_PI = 0.3989422804014327

PIECES = (
    ("ln1_gain", (D,)),
    ("ln1_bias", (D,)),
    ("w_qkv", (D, 3 * D)),
    ("q_bias", (D,)),
    ("v_bias", (D,)),
    ("w_proj", (D, D)),
    ("proj_bias", (D,)),
    ("ln2_gain", (D,)),
    ("ln2_bias", (D,)),
    ("w_fc1", (D, FF)),
    ("fc1_bias", (FF,)),
    ("w_fc2", (FF, D)),
    ("fc2_bias", (D,)),
)
MATRICES = tuple(name for name, shape in PIECES if len(shape) == 2)
VECTORS = tuple(name for name, shape in PIECES if len(shape) == 1)
SHAPES = dict(PIECES)


def row_bases():
    bases, row = {}, 0
    for name, shape in PIECES:
        bases[name] = row
        row += math.prod(shape) // LANES
    return bases, row


BASES, TOTAL_ROWS = row_bases()
IMAGE_MAX = 98
QKV_BIAS = len(VECTORS)
TABLE = (16, FF)


def part_rows(entries):
    return -(-((LANES - 1 + entries - 1) // LANES + 1) // 16) * 16


def tile(i):
    return pl.ds(pl.multiple_of(i * 16, 16), 16)


def loop(count, body, unroll=1):
    def step(i, carry):
        for u in range(unroll):
            body(i * unroll + u)
        return carry

    whole = count // unroll
    if whole:
        lax.fori_loop(0, whole, step, 0)
    for i in range(whole * unroll, count):
        body(i)


def aligned(raw, held, stage, which, entries):
    rows = held.shape[1]
    shift = (entries * which) % LANES
    stage[0:8, :] = jnp.zeros((8, LANES), jnp.float32)

    def turn(i):
        stage[pl.ds(pl.multiple_of(i * 16 + 8, 8), 16), :] = pltpu.roll(
            raw[tile(i), :].astype(jnp.float32), shift, 1
        )

    loop(rows // 16, turn, 8)

    def merge(i):
        lane = lax.broadcasted_iota(jnp.int32, (16, LANES), 1)
        now = stage[pl.ds(i * 16 + 8, 16), :]
        before = stage[pl.ds(i * 16 + 7, 16), :]
        held[which, tile(i), :] = jnp.where(lane < shift, before, now).astype(held.dtype)

    loop(rows // 16, merge, 8)


def round_up(value, unit):
    return -(-value // unit) * unit


class Span:
    def __init__(self, low, high, name, first, depth, vectors):
        self.low, self.high = low, high
        self.name, self.first, self.depth = name, first, depth
        self.vectors = vectors


def spans(cuts):
    out, row, early = [], 0, []
    for name, shape in PIECES:
        count = math.prod(shape) // LANES
        if len(shape) == 1:
            if out:
                out[-1].vectors.append(name)
                out[-1].high = row + count
            else:
                early.append(name)
        else:
            depth = shape[0] // cuts[name]
            blocks = shape[1] // LANES
            for c in range(cuts[name]):
                start = row + c * depth * blocks
                span = Span(start, start + depth * blocks, name, c * depth, depth, [])
                if not out:
                    span.low, span.vectors = 0, early
                out.append(span)
        row += count
    return out


GATHER_SPANS = spans({name: 1 for name in MATRICES})
SCATTER_SPANS = spans({"w_qkv": 2, "w_proj": 1, "w_fc1": 2, "w_fc2": 2})


def stage_rows(spans_, rows):
    return round_up(max(s.high - s.low for s in spans_), 16) + 2 * rows + 32


def owners(span, entries):
    return (span.low * LANES) // entries, (span.high * LANES - 1) // entries


def spread(held, stage, span, entries):
    rows = held.shape[1]
    low, high = owners(span, entries)

    def one(i):
        d = low + i
        base = (entries * d) // LANES - span.low + rows
        cut = (entries * d) % LANES
        first = stage[pl.ds(base, 1), :]

        def body(t):
            stage[pl.ds(base + t * 16, 16), :] = held[d, tile(t), :].astype(jnp.float32)

        loop(rows // 16, body, 8)
        row = stage[pl.ds(base, 1), :]
        stage[pl.ds(base, 1), :] = jnp.where(cut != 0, row + first, row)

    loop(high - low + 1, one)


def form(stage, span, margin, out):
    blocks = SHAPES[span.name][1] // LANES
    base = margin + BASES[span.name] + span.first * blocks - span.low

    def body(i):
        for j in range(blocks):
            out[tile(i + span.first // 16), j * LANES : (j + 1) * LANES] = stage[
                pl.ds(base + i * 16 * blocks + j, 16, stride=blocks), :
            ].astype(out.dtype)

    loop(span.depth // 16, body, max(1, 24 // blocks))


def vector_rows(stage, span, margin, table):
    for name in span.vectors:
        at = margin + BASES[name] - span.low
        row = VECTORS.index(name)
        for j in range(SHAPES[name][0] // LANES):
            table[row : row + 1, j * LANES : (j + 1) * LANES] = stage[at + j : at + j + 1, :]


def vector(table, name):
    row = VECTORS.index(name)
    return table[row : row + 1, 0 : SHAPES[name][0]]


def lay(stage, span, margin, first, value):
    blocks = SHAPES[span.name][1] // LANES
    base = margin + BASES[span.name] - span.low + first * blocks
    for i in range(value.shape[0] // 16):
        for j in range(blocks):
            stage[pl.ds(base + i * 16 * blocks + j, 16, stride=blocks), :] = value[
                i * 16 : (i + 1) * 16, j * LANES : (j + 1) * LANES
            ]


def lay_vectors(stage, span, margin, table):
    for name in span.vectors:
        at = margin + BASES[name] - span.low
        row = VECTORS.index(name)
        for j in range(SHAPES[name][0] // LANES):
            stage[at + j : at + j + 1, :] = table[row : row + 1, j * LANES : (j + 1) * LANES]


def cut(stage, span, own, entries):
    rows = own.shape[1]
    low, high = owners(span, entries)

    def whole(d):
        base = (entries * d) // LANES - span.low + rows

        def body(t):
            own[d, tile(t), :] = stage[pl.ds(base + t * 16, 16), :].astype(own.dtype)

        loop(rows // 16, body, 8)

    def edge(d):
        base = (entries * d) // LANES - span.low + rows

        def body(t):
            now = stage[pl.ds(base + t * 16, 16), :]
            row = base + t * 16 - rows + lax.broadcasted_iota(jnp.int32, (16, LANES), 0)
            inside = jnp.logical_and(row >= 0, row < span.high - span.low)
            before = own[d, tile(t), :].astype(jnp.float32)
            own[d, tile(t), :] = jnp.where(inside, now, before).astype(own.dtype)

        loop(rows // 16, body, 8)

    edge(low)
    if high - low > 1:
        loop(high - low - 1, lambda i: whole(low + 1 + i))
    if high > low:
        edge(high)


def mean_of(v):
    return jnp.sum(v, axis=-1, keepdims=True) * (1.0 / v.shape[-1])


def normalize(v):
    centred = v - mean_of(v)
    inv_std = lax.rsqrt(mean_of(centred * centred) + EPSILON)
    return centred * inv_std, inv_std


def norm_back(grad_out, normed, inv_std, gain):
    grad_norm = grad_out * gain
    return inv_std * (grad_norm - mean_of(grad_norm) - normed * mean_of(grad_norm * normed))


def dot(a, b, left=1, right=0):
    return lax.dot_general(
        a, b, (((left,), (right,)), ((), ())), preferred_element_type=jnp.float32
    )


def columns(width, block, body):
    loop(width // block, lambda i: body(pl.ds(pl.multiple_of(i * block, block), block)))


def segments(lengths, b, images, shape, dim):
    position = lax.broadcasted_iota(jnp.int32, shape, dim)
    total, seg = 0, jnp.zeros(shape, jnp.int32)
    for i in range(images):
        total = total + lengths[b, i]
        seg = seg + jnp.where(position >= total, 1, 0)
    return seg


def valid_rows(lengths, b, images, count):
    return jnp.where(segments(lengths, b, images, (count, 1), 0) < images, 1.0, 0.0)


class Sizes:
    def __init__(self, tokens, lengths):
        self.buffers, self.images = lengths.shape
        self.full = tokens.shape[0] // self.buffers
        self.rows = min(self.full, round_up(self.images * IMAGE_MAX, 16))
        self.total = self.rows * self.buffers
        self.pairs = D // LANES

    def at(self, b):
        return slice(b * self.rows, (b + 1) * self.rows)

    def given(self, b):
        return slice(b * self.full, b * self.full + self.rows)


def low(v):
    return v.astype(jnp.bfloat16)


def half_lanes(rows):
    lane = lax.broadcasted_iota(jnp.int32, (rows, LANES), 1)
    first = low(jnp.where(lane < HEAD_DIM, 1.0, 0.0))
    return first, low(jnp.where(lane < HEAD_DIM, 0.0, 1.0))


SCALE = 1.0 / math.sqrt(HEAD_DIM)
SAVED = ("attn_in", "qkv", "probs", "mix", "mid", "mlp_in", "act", "slope")


def saved_shapes(sz):
    t = sz.total
    bf = jnp.bfloat16
    return {
        "attn_in": ((t, D), bf),
        "qkv": ((t, 3 * D), bf),
        "probs": ((sz.buffers * sz.pairs * 2, sz.rows, sz.rows), bf),
        "mix": ((t, D), bf),
        "mid": ((t, D), jnp.float32),
        "mlp_in": ((t, D), bf),
        "act": ((t, FF), bf),
        "slope": ((t, FF), bf),
    }


def forward_kernel(place, entries, sz, raw, tokens, lengths, *refs):
    mats, refs = dict(zip(MATRICES, refs[:4])), refs[4:]
    out_saved, refs = dict(zip(SAVED, refs[:8])), refs[8:]
    table, block_out, refs = refs[0], refs[1], refs[2:]
    held, stage, refs = refs[0], refs[1], refs[2:]
    w, refs = dict(zip(MATRICES, refs[:4])), refs[4:]
    a, refs = dict(zip(SAVED, refs[:8])), refs[8:]
    normed = refs[0]
    send, recv, cross, done_w, done_a = refs[1:]
    me = place.coords()
    margin = held.shape[1]

    aligned(raw, held, stage, place.flat(me), entries)
    greet(place, me)

    def norm_first(i):
        for b in range(sz.buffers):
            x = tokens[pl.ds(pl.multiple_of(b * sz.full + i * 16, 16), 16), :].astype(jnp.float32)
            normed[pl.ds(pl.multiple_of(b * sz.rows + i * 16, 16), 16), :] = normalize(x)[0]

    def after(i):
        if i is None or i == 8:
            loop(sz.rows // 16, norm_first)

    gather_all(place, me, held, send, recv, cross, after)

    def keep(name):
        pltpu.make_async_copy(a[name], out_saved[name], done_a.at[SAVED.index(name)]).start()

    for span in GATHER_SPANS:
        name = span.name
        spread(held, stage, span, entries)
        form(stage, span, margin, w[name])
        vector_rows(stage, span, margin, table)
        m = MATRICES.index(name)
        pltpu.make_async_copy(w[name], mats[name], done_w.at[m]).start()
    table[QKV_BIAS : QKV_BIAS + 1, 0:D] = vector(table, "q_bias")
    table[QKV_BIAS : QKV_BIAS + 1, D : 2 * D] = jnp.zeros((1, D), jnp.float32)
    table[QKV_BIAS : QKV_BIAS + 1, 2 * D : 3 * D] = vector(table, "v_bias")

    def scale_first(i):
        a["attn_in"][tile(i), :] = low(
            normed[tile(i), :] * vector(table, "ln1_gain") + vector(table, "ln1_bias")
        )

    loop(sz.total // 16, scale_first)
    keep("attn_in")

    def to_qkv(c):
        a["qkv"][:, c] = low(
            dot(a["attn_in"][...], w["w_qkv"][:, c]) + table[QKV_BIAS : QKV_BIAS + 1, c]
        )

    columns(3 * D, 256, to_qkv)
    keep("qkv")

    qkv, probs, mix = a["qkv"], a["probs"], a["mix"]
    for b in range(sz.buffers):
        rows = sz.at(b)
        seg_r = segments(lengths, b, sz.images, (sz.rows, 1), 0)
        seg_c = segments(lengths, b, sz.images, (1, sz.rows), 1)

        def attend(p):
            halves = half_lanes(sz.rows)
            at = lambda part: pl.ds(pl.multiple_of(part * D + p * LANES, LANES), LANES)
            q, k, v = (qkv[rows, at(part)] for part in range(3))
            mixed = None
            for h in range(2):
                s = dot(q * (halves[h] * SCALE).astype(q.dtype), k, 1, 1)
                s = jnp.where(seg_r == seg_c, s, NEG_FILL)
                e = jnp.exp(s - jnp.max(s, axis=-1, keepdims=True))
                pr = low(e * (1.0 / jnp.sum(e, axis=-1, keepdims=True)))
                probs[(b * sz.pairs + p) * 2 + h] = pr
                part = dot(pr, v * halves[h])
                mixed = part if mixed is None else mixed + part
            mix[rows, at(0)] = low(mixed)

        loop(sz.pairs, attend)
    keep("probs")
    keep("mix")

    def to_mid(c):
        made = dot(mix[...], w["w_proj"][:, c]) + table[
            VECTORS.index("proj_bias") : VECTORS.index("proj_bias") + 1, c
        ]
        for b in range(sz.buffers):
            a["mid"][sz.at(b), c] = (
                tokens[sz.given(b), c].astype(jnp.float32) + made[sz.at(b), :]
            )

    columns(D, 256, to_mid)
    keep("mid")

    def norm_second(i):
        a["mlp_in"][tile(i), :] = low(
            normalize(a["mid"][tile(i), :])[0] * vector(table, "ln2_gain")
            + vector(table, "ln2_bias")
        )

    loop(sz.total // 16, norm_second)
    keep("mlp_in")

    def to_act(c):
        at = VECTORS.index("fc1_bias")
        pre = dot(a["mlp_in"][...], w["w_fc1"][:, c]) + table[at : at + 1, c]
        phi = 0.5 * (1.0 + lax.erf(pre * ROOT_HALF))
        a["act"][:, c] = low(pre * phi)
        a["slope"][:, c] = low(phi + pre * jnp.exp(-0.5 * pre * pre) * INV_ROOT_TWO_PI)

    columns(FF, 256, to_act)
    keep("act")
    keep("slope")

    def to_out(c):
        at = VECTORS.index("fc2_bias")
        made = dot(a["act"][...], w["w_fc2"][:, c]) + table[at : at + 1, c]
        for b in range(sz.buffers):
            valid = valid_rows(lengths, b, sz.images, sz.rows)
            block_out[sz.given(b), c] = low(valid * (a["mid"][sz.at(b), c] + made[sz.at(b), :]))
            if sz.full > sz.rows:
                block_out[b * sz.full + sz.rows : (b + 1) * sz.full, c] = jnp.zeros(
                    (sz.full - sz.rows, made.shape[1]), jnp.bfloat16
                )

    columns(D, 256, to_out)
    for m, name in enumerate(MATRICES):
        pltpu.make_async_copy(w[name], mats[name], done_w.at[m]).wait()
    for i, name in enumerate(SAVED):
        pltpu.make_async_copy(a[name], out_saved[name], done_a.at[i]).wait()


def forward(place, tokens, params, lengths):
    entries = params.shape[0]
    rows = part_rows(entries)
    sz = Sizes(tokens, lengths)
    raw = jnp.pad(params, (0, rows * LANES - entries)).reshape(rows, LANES)
    any_spec = pl.BlockSpec(memory_space=pl.ANY)
    vmem = pl.BlockSpec(memory_space=pltpu.VMEM)
    smem = pl.BlockSpec(memory_space=pltpu.SMEM)
    saved = saved_shapes(sz)
    bf = jnp.bfloat16
    outs = pl.pallas_call(
        functools.partial(forward_kernel, place, entries, sz),
        out_shape=[jax.ShapeDtypeStruct(SHAPES[n], bf) for n in MATRICES]
        + [jax.ShapeDtypeStruct(*saved[n]) for n in SAVED]
        + [jax.ShapeDtypeStruct(TABLE, jnp.float32), jax.ShapeDtypeStruct(tokens.shape, bf)],
        in_specs=[vmem, vmem, smem],
        out_specs=[any_spec] * 12 + [vmem, vmem],
        scratch_shapes=[
            pltpu.VMEM((place.devices, rows, LANES), bf),
            pltpu.VMEM((stage_rows(GATHER_SPANS, rows), LANES), jnp.float32),
        ]
        + [pltpu.VMEM(SHAPES[n], bf) for n in MATRICES]
        + [pltpu.VMEM(*saved[n]) for n in SAVED]
        + [pltpu.VMEM((sz.total, D), jnp.float32)]
        + gather_sems(place)
        + [pltpu.SemaphoreType.DMA((4,)), pltpu.SemaphoreType.DMA((8,))],
        compiler_params=pltpu.CompilerParams(
            collective_id=0, has_side_effects=True, vmem_limit_bytes=67 * 10**6
        ),
        name="forward",
    )(raw, tokens, lengths)
    return dict(zip(MATRICES, outs[:4])), dict(zip(SAVED, outs[4:12])), outs[12], outs[13]


SUMS = tuple(VECTORS)


def backward_kernel(place, entries, sz, tokens, cotangent, lengths, table, *refs):
    mats, refs = dict(zip(MATRICES, refs[:4])), refs[4:]
    given, refs = dict(zip(SAVED, refs[:8])), refs[8:]
    out, input_grad, refs = refs[0], refs[1], refs[2:]
    own, cross, refs = refs[0], refs[1], refs[2:]
    n = place.classes
    slots, refs = refs[:n], refs[n:]
    cross_send, cross_recv, send = refs[:3]
    recv, refs = refs[3 : 3 + n], refs[3 + n :]
    stage, total, sums, refs = refs[0], refs[1], refs[2], refs[3:]
    big_a, big_b, refs = refs[0], refs[1], refs[2:]
    wide, slope, qkv, probs, mix, mid, narrow, x, g, temp, blank, load, done = refs
    me = place.coords()
    margin = own.shape[1]
    count = sz.total
    order = ("g", "act", "w_fc2", "slope", "mlp_in", "w_fc1", "mid", "mix", "x", "qkv", "probs")

    def fetches(name):
        sem = load.at[order.index(name)]
        if name in ("g", "x"):
            src, dst = (cotangent, g) if name == "g" else (tokens, x)
            return [
                pltpu.make_async_copy(
                    src.at[sz.given(b)],
                    dst.at[sz.at(b)],
                    load.at[order.index(name) if b == 0 else len(order) + 10 + 2 * b + (name == "g")],
                )
                for b in range(sz.buffers)
            ]
        return [pltpu.make_async_copy(*places[name], sem)]

    places = {
        "act": (given["act"], wide),
        "slope": (given["slope"], slope),
        "mlp_in": (given["mlp_in"], narrow),
        "mid": (given["mid"], mid),
        "mix": (given["mix"], mix),
        "qkv": (given["qkv"], qkv),
        "probs": (given["probs"], probs),
        "w_fc2": (mats["w_fc2"], big_a),
        "w_fc1": (mats["w_fc1"], big_b),
    }

    def begin(name):
        for c in fetches(name):
            c.start()

    def ready(name):
        for c in fetches(name):
            c.wait()

    for name in order:
        begin(name)
    greet(place, me)

    def sum_to(name, c, value):
        at = SUMS.index(name)
        sums[at : at + 1, c] = value

    def ones():
        return jnp.ones((8, count), jnp.bfloat16)

    def column_sums(name, ref, width):
        def body(c):
            sum_to(name, c, dot(ones(), ref[:, c])[0:1, :])

        columns(width, 256, body)

    def pieces(name, left, right, block):
        for span in [s for s in SCATTER_SPANS if s.name == name]:

            def body(i):
                first = pl.multiple_of(span.first + i * block, block)
                lay(stage, span, margin, first, dot(left[:, pl.ds(first, block)], right(), 0, 0))

            loop(span.depth // block, body)
            yield span

    def finish(span):
        lay_vectors(stage, span, margin, sums)
        cut(stage, span, own, entries)

    ready("g")
    for b in range(sz.buffers):
        rows = sz.at(b)
        valid = valid_rows(lengths, b, sz.images, sz.rows)
        g[rows, :] = low(g[rows, :].astype(jnp.float32) * valid)
    ready("act")
    column_sums("fc2_bias", g, D)
    for span in pieces("w_fc2", wide, lambda: g[...], 256):
        finish(span)

    ready("w_fc2")
    ready("slope")

    def to_pre(i):
        c = pl.ds(pl.multiple_of(i * 256, 256), 256)
        made = dot(g[...], big_a[c, :], 1, 1)
        wide[:, c] = low(made * slope[:, c].astype(jnp.float32))

    loop(FF // 256, to_pre)
    late = [
        pltpu.make_async_copy(
            mats["w_qkv"].at[:, i * D : (i + 1) * D],
            big_a.at[i * D : (i + 1) * D],
            load.at[len(order) + 8 + i],
        )
        for i in range(3)
    ]
    late.append(
        pltpu.make_async_copy(mats["w_proj"], big_a.at[3 * D : 4 * D], load.at[len(order) + 11])
    )
    for c in reversed(late):
        c.start()
    ready("mlp_in")
    column_sums("fc1_bias", wide, FF)
    for span in pieces("w_fc1", narrow, lambda: wide[...], 128):
        finish(span)

    attn_load = pltpu.make_async_copy(given["attn_in"], narrow, load.at[len(order) + 7])
    attn_load.start()
    ready("w_fc1")

    def to_mlp(i):
        c = pl.ds(pl.multiple_of(i * 256, 256), 256)
        temp[:, c] = dot(wide[...], big_b[c, :], 1, 1)

    loop(D // 256, to_mlp)
    ready("mid")

    def column_add(name, value, first):
        at = SUMS.index(name)
        part = jnp.sum(value, axis=0, keepdims=True)
        before = sums[at : at + 1, 0:D]
        sums[at : at + 1, 0:D] = part if first else before + part

    def clear(name):
        at = SUMS.index(name)
        sums[at : at + 1, 0:D] = jnp.zeros((1, D), jnp.float32)

    clear("ln2_gain")
    clear("ln2_bias")

    def back_second(i):
        normed, inv = normalize(mid[tile(i), :])
        d = temp[tile(i), :]
        column_add("ln2_gain", d * normed, False)
        column_add("ln2_bias", d, False)
        v = g[tile(i), :].astype(jnp.float32) + norm_back(d, normed, inv, vector(table, "ln2_gain"))
        mid[tile(i), :] = v
        g[tile(i), :] = low(v)

    loop(count // 16, back_second)
    ready("mix")
    column_sums("proj_bias", g, D)
    for span in pieces("w_proj", mix, lambda: g[...], 256):
        finish(span)
    late[3].wait()

    def to_mix(i):
        c = pl.ds(pl.multiple_of(i * 256, 256), 256)
        rows = pl.ds(pl.multiple_of(3 * D + i * 256, 256), 256)
        slope[:, c] = low(dot(g[...], big_a[rows, :], 1, 1))

    loop(D // 256, to_mix)
    ready("qkv")
    ready("probs")
    for b in range(sz.buffers):
        rows = sz.at(b)

        def attend(p):
            halves = half_lanes(sz.rows)
            at = lambda part: pl.ds(pl.multiple_of(part * D + p * LANES, LANES), LANES)
            q, k, v = (qkv[rows, at(part)] for part in range(3))
            dm = slope[rows, at(0)]
            dq = dk = dv = 0.0
            for h in range(2):
                pr = probs[(b * sz.pairs + p) * 2 + h]
                dmh = dm * halves[h]
                dp = dot(dmh, v, 1, 1)
                prf = pr.astype(jnp.float32)
                ds = low(prf * (dp - jnp.sum(prf * dp, axis=-1, keepdims=True)))
                dv = dv + dot(pr, dmh, 0, 0)
                dq = dq + dot(ds, k * halves[h])
                dk = dk + dot(ds, q * halves[h], 0, 0)
            wide[rows, at(0)] = low(dq * SCALE)
            wide[rows, at(1)] = low(dk * SCALE)
            wide[rows, at(2)] = low(dv)

        loop(sz.pairs, attend)
    for c in late[:3]:
        c.wait()

    def to_attn(i):
        c = pl.ds(pl.multiple_of(i * 256, 256), 256)
        made = None
        for part in range(3):
            rows = pl.ds(pl.multiple_of(part * D + i * 256, 256), 256)
            term = dot(wide[:, part * D : (part + 1) * D], big_a[rows, :], 1, 1)
            made = term if made is None else made + term
        temp[:, c] = made

    loop(D // 256, to_attn)
    ready("x")
    clear("ln1_gain")
    clear("ln1_bias")

    def back_first(i):
        normed, inv = normalize(x[tile(i), :].astype(jnp.float32))
        d = temp[tile(i), :]
        column_add("ln1_gain", d * normed, False)
        column_add("ln1_bias", d, False)
        mid[tile(i), :] = mid[tile(i), :] + norm_back(d, normed, inv, vector(table, "ln1_gain"))

    loop(count // 16, back_first)
    outs = []
    for b in range(sz.buffers):
        outs.append(
            pltpu.make_async_copy(mid.at[sz.at(b)], input_grad.at[sz.given(b)], done.at[2 * b])
        )
        if sz.full > sz.rows:
            blank[...] = jnp.zeros(blank.shape, blank.dtype)
            outs.append(
                pltpu.make_async_copy(
                    blank,
                    input_grad.at[b * sz.full + sz.rows : (b + 1) * sz.full],
                    done.at[2 * b + 1],
                )
            )
    for c in outs:
        c.start()

    attn_load.wait()

    def qv_sums(c):
        wide_sum = dot(ones(), wide[:, c])[0:1, :]
        sums[len(SUMS) : len(SUMS) + 1, c] = wide_sum

    columns(3 * D, 256, qv_sums)
    for name, part in (("q_bias", 0), ("v_bias", 2)):
        at = SUMS.index(name)
        sums[at : at + 1, 0:D] = sums[len(SUMS) : len(SUMS) + 1, part * D : (part + 1) * D]
    for span in pieces("w_qkv", narrow, lambda: wide[:, 0 : 3 * D], 128):
        finish(span)

    scatter_all(place, me, own, cross, slots, total, (cross_send, cross_recv, send, recv))
    shift = (entries * place.flat(me)) % LANES
    back = (LANES - shift) % LANES
    rows = own.shape[1]

    def turn(i):
        total[tile(i), :] = pltpu.roll(total[tile(i), :], back, 1)

    loop(rows // 16, turn, 8)

    def merge(i):
        lane = lax.broadcasted_iota(jnp.int32, (16, LANES), 1)
        now = total[pl.ds(i * 16, 16), :]
        after = total[pl.ds(i * 16 + 1, 16), :]
        out[tile(i), :] = jnp.where(lane < LANES - shift, now, after)

    loop(rows // 16, merge, 8)
    for c in outs:
        c.wait()


def backward(place, tokens, cotangent, lengths, mats, saved, table, entries):
    rows = part_rows(entries)
    sz = Sizes(tokens, lengths)
    cross, slots, sems, recv = scatter_scratch(place, rows)
    any_spec = pl.BlockSpec(memory_space=pl.ANY)
    vmem = pl.BlockSpec(memory_space=pltpu.VMEM)
    smem = pl.BlockSpec(memory_space=pltpu.SMEM)
    bf, f32 = jnp.bfloat16, jnp.float32
    shapes = saved_shapes(sz)
    scratch = lambda name: pltpu.VMEM(*shapes[name])
    out, input_grad = pl.pallas_call(
        functools.partial(backward_kernel, place, entries, sz),
        out_shape=[
            jax.ShapeDtypeStruct((rows, LANES), f32),
            jax.ShapeDtypeStruct(tokens.shape, f32),
        ],
        in_specs=[any_spec, any_spec, smem, vmem] + [any_spec] * 12,
        out_specs=[vmem, any_spec],
        scratch_shapes=[pltpu.VMEM((place.devices, rows, LANES), bf)]
        + cross
        + slots
        + sems
        + recv
        + [
            pltpu.VMEM((stage_rows(SCATTER_SPANS, rows), LANES), f32),
            pltpu.VMEM((rows + 16, LANES), f32),
            pltpu.VMEM(TABLE, f32),
            pltpu.VMEM((FF, D), bf),
            pltpu.VMEM((D, FF), bf),
            scratch("act"),
            scratch("slope"),
            scratch("qkv"),
            scratch("probs"),
            scratch("mix"),
            scratch("mid"),
            scratch("mlp_in"),
            pltpu.VMEM((sz.total, D), bf),
            pltpu.VMEM((sz.total, D), bf),
            pltpu.VMEM((sz.total, D), f32),
            pltpu.VMEM((max(8, sz.full - sz.rows), D), f32),
            pltpu.SemaphoreType.DMA((24 + 2 * sz.buffers,)),
            pltpu.SemaphoreType.DMA((2 * sz.buffers,)),
        ],
        compiler_params=pltpu.CompilerParams(
            collective_id=1, has_side_effects=True, vmem_limit_bytes=67 * 10**6
        ),
        name="backward",
    )(tokens, cotangent, lengths, table, *[mats[m] for m in MATRICES], *[saved[s] for s in SAVED])
    return input_grad, out.reshape(-1)[:entries]


def solution(mesh):
    place = Place(mesh)

    def shards(tokens, cotangent, params, lengths):
        mats, saved, table, out = forward(place, tokens, params, lengths)
        input_grad, grad = backward(
            place, tokens, cotangent, lengths, mats, saved, table, params.shape[0]
        )
        return out, input_grad, grad

    rows, flat = P(AXES, None), P(AXES)
    return jax.shard_map(
        shards,
        mesh=mesh,
        in_specs=(rows, rows, flat, rows),
        out_specs=(rows, rows, flat),
        check_vma=False,
    )
```

```python
import functools
import math

import jax
import jax.numpy as jnp
from jax import lax
from jax.experimental import pallas as pl
from jax.experimental.pallas import tpu as pltpu
from jax.sharding import PartitionSpec as P

AXES = ("dp", "fsdp")
LANES = 128
CORE = 3


class Place:
    def __init__(self, mesh):
        devs = mesh.devices
        spot = lambda d: (*d.coords, d.core_on_chip)
        self.shape = devs.shape
        self.digits = []
        for axis in range(2):
            line = [spot(devs[i, 0] if axis == 0 else devs[0, i]) for i in range(devs.shape[axis])]
            found, stride = [], 1
            while stride < len(line):
                delta = [b - a for a, b in zip(line[0], line[stride])]
                phys = [p for p in range(4) if delta[p]][0]
                step, size = delta[phys], 1
                while (
                    size * stride < len(line)
                    and line[size * stride][phys] - line[0][phys] == size * step
                    and all(line[size * stride][q] == line[0][q] for q in range(4) if q != phys)
                ):
                    size += 1
                found.append((phys, step, size, stride))
                stride *= size
            self.digits.append(found)
        self.size = [1, 1, 1, 1]
        for found in self.digits:
            for phys, _, size, _ in found:
                self.size[phys] *= size
        self.devices = devs.size
        self.chips = math.prod(self.size[:3])
        long = max(range(3), key=lambda p: self.size[p])
        a, b = [p for p in range(3) if p != long]
        self.orders = ((long, a, b), (long, b, a))
        self.shares = (1, 1)
        if self.chips <= 16:
            self.orders += ((a, long, b), (b, long, a))
            self.shares += (2, 2)
        self.classes = len(self.orders)

    def coords(self):
        index = [lax.axis_index(name) for name in AXES]
        out = [0, 0, 0, 0]
        for axis in range(2):
            for phys, step, size, stride in self.digits[axis]:
                out[phys] = out[phys] + ((index[axis] // stride) % size) * step
        return out

    def device(self, coords):
        out = []
        for axis in range(2):
            total = 0
            for phys, step, size, stride in self.digits[axis]:
                total = total + ((coords[phys] // step) % size) * stride
            out.append(total)
        return tuple(out)

    def flat(self, coords):
        dp, fsdp = self.device(coords)
        return dp * self.shape[1] + fsdp

    def chip(self, coords):
        return (coords[0] * self.size[1] + coords[1]) * self.size[2] + coords[2]

    def class_rows(self, rows):
        units = rows // 16
        counts = [units * share // sum(self.shares) for share in self.shares]
        counts[-1] += units - sum(counts)
        out, start = [], 0
        for count in counts:
            out.append((start * 16, count * 16))
            start += count
        return out


def flipped(mine, rel, size):
    total, bit = 0, 1
    while bit < size:
        total = total + bit * (((mine // bit) % 2 + (rel // bit) % 2) % 2)
        bit *= 2
    return total


def both(*conds):
    known = [c for c in conds if isinstance(c, bool)]
    if not all(known):
        return False
    rest = [c for c in conds if not isinstance(c, bool)]
    return functools.reduce(jnp.logical_and, rest) if rest else True


def when(cond, fn):
    if isinstance(cond, bool):
        if cond:
            fn()
    else:
        pl.when(cond)(fn)


def moved(coords, dim, by):
    out = list(coords)
    out[dim] = out[dim] + by
    return out


def partner(coords):
    out = list(coords)
    out[CORE] = 1 - out[CORE]
    return out


def neighbours(place, me):
    out = [(True, partner(me))]
    for dim in range(3):
        if place.size[dim] == 1:
            continue
        if place.size[dim] == 2:
            other = list(me)
            other[dim] = 1 - other[dim]
            out.append((True, other))
        else:
            out.append((me[dim] < place.size[dim] - 1, moved(me, dim, 1)))
            out.append((me[dim] > 0, moved(me, dim, -1)))
    return out


def greet(place, me):
    barrier = pltpu.get_barrier_semaphore()
    nbrs = neighbours(place, me)
    for cond, who in nbrs:
        when(
            cond,
            lambda who=who: pl.semaphore_signal(
                barrier, inc=1, device_id=place.device(who), device_id_type=pl.DeviceIdType.MESH
            ),
        )
    peers = sum(1 if cond is True else jnp.where(cond, 1, 0) for cond, _ in nbrs)
    pl.semaphore_wait(barrier, peers)


def onward(place, order, me, rel, src):
    out = []
    for pos in range(3):
        dim = order[pos]
        size = place.size[dim]
        if size == 1:
            continue
        later = [rel[d] == 0 for d in order[pos + 1 :]]
        if size == 2:
            other = list(me)
            other[dim] = 1 - other[dim]
            out.append((both(*later, rel[dim] == 0), pos, 0, other))
        else:
            for way, by in ((0, 1), (1, -1)):
                if by == 1:
                    here = both(me[dim] >= src[dim], me[dim] < size - 1)
                else:
                    here = both(me[dim] <= src[dim], me[dim] > 0)
                cond = both(*later, here)
                out.append((cond, pos, way, moved(me, dim, by)))
    return out


PASSES = (
    0, 16, 32, 48, 1, 17, 40, 33, 52, 49, 41, 56, 3, 8, 2, 20, 35, 34, 10, 53, 18, 28,
    11, 5, 51, 36, 12, 19, 45, 57, 50, 9, 7, 21, 55, 54, 60, 25, 44, 6, 22, 29, 24, 42,
    58, 27, 37, 26, 59, 43, 15, 23, 4, 39, 61, 14, 30, 13, 62, 38, 63, 31, 47, 46,
)


def walk_parts(place, body, reverse=False, after=None):
    if place.size[:3] == [2, 2, 4]:
        for i, code in enumerate(PASSES[::-1] if reverse else PASSES):
            body(code // 16, ((code // 8) % 2, (code // 4) % 2, code % 4))
            if after is not None:
                after(i)
        return

    def each(rel):
        for k in range(place.classes):
            body(k, rel)

    walk(place, each, reverse)
    if after is not None:
        after(None)


def walk(place, body, reverse=False):
    sizes = place.size[:3]
    if place.chips <= 16:
        rels = [
            (x, y, z) for x in range(sizes[0]) for y in range(sizes[1]) for z in range(sizes[2])
        ]
        rels.sort(key=lambda r: (sum(r), r), reverse=reverse)
        for rel in rels:
            body(rel)
        return

    def step(i, carry):
        i = place.chips - 1 - i if reverse else i
        body((i % sizes[0], (i // sizes[0]) % sizes[1], i // (sizes[0] * sizes[1])))
        return carry

    lax.fori_loop(0, place.chips, step, 0)


def source_of(place, me, rel):
    return [flipped(me[d], rel[d], place.size[d]) for d in range(3)] + [me[CORE]]


def gather_all(place, me, held, send, recv, cross, after=None):
    rows = held.shape[1]
    parts = place.class_rows(rows)

    def copy(k, src, slot, sem, who):
        start, count = parts[k]
        ref = held.at[place.flat(src), pl.ds(start, count), :]
        return pltpu.make_async_remote_copy(
            src_ref=ref,
            dst_ref=ref,
            send_sem=send.at[k, place.chip(src), slot],
            recv_sem=sem.at[k, place.chip(src)],
            device_id=place.device(who),
            device_id_type=pl.DeviceIdType.MESH,
        )

    def sends(k, rel, src, act):
        for cond, pos, way, who in onward(place, place.orders[k], me, rel, src):
            when(cond, lambda: act(copy(k, src, pos * 2 + way, recv, who)))
        act(copy(k, src, 6, cross, partner(me)))

    def go(k, rel):
        src = source_of(place, me, rel)
        home = both(*[r == 0 for r in rel])
        if home is not True:
            away = True if home is False else jnp.logical_not(home)
            when(away, lambda: copy(k, src, 0, recv, me).wait_recv())
        sends(k, rel, src, lambda c: c.start())

    walk_parts(place, go, after=after)

    def drain(rel):
        src = source_of(place, me, rel)
        theirs = partner(src)
        for k in range(place.classes):
            sends(k, rel, src, lambda c: c.wait_send())
            copy(k, theirs, 0, cross, me).wait_recv()

    walk(place, drain)


def gather_sems(place):
    return [
        pltpu.SemaphoreType.DMA((place.classes, place.chips, 7)),
        pltpu.SemaphoreType.DMA((place.classes, place.chips)),
        pltpu.SemaphoreType.DMA((place.classes, place.chips)),
    ]


def slot_plan(place, rows):
    plan = []
    for order in place.orders:
        starts, total = [], 0
        for pos in range(3):
            before = math.prod(place.size[d] for d in order[:pos])
            size = place.size[order[pos]]
            starts.append(total)
            total += before * (1 if size == 2 else size + 1 if size > 1 else 0)
        plan.append((starts, total))
    return plan


def slot_of(place, plan, k, pos, way, at, dest):
    order = place.orders[k]
    index = 0
    for d in order[:pos]:
        index = index * place.size[d] + dest[d]
    dim = order[pos]
    size = place.size[dim]
    if size > 2:
        spot = dest[dim]
        if way == 1:
            spot = spot + jnp.where(at[dim] == dest[dim], size - dest[dim], 0)
        index = index * (size + 1) + spot
    return plan[k][0][pos] + index


def add_rows(dst, terms, count):
    def body(i):
        r = tile(i)
        value = terms[0](r).astype(jnp.float32)
        for term in terms[1:]:
            value = value + term(r).astype(jnp.float32)
        dst(r, value)

    loop(count // 16, body, 4)


def scatter_all(place, me, own, cross, slots, total, sems):
    cross_send, cross_recv, send, recv = sems
    rows = own.shape[1]
    parts = place.class_rows(rows)
    plan = slot_plan(place, rows)

    def swap(dest):
        return pltpu.make_async_remote_copy(
            src_ref=own.at[place.flat(partner(dest))],
            dst_ref=cross.at[place.chip(dest)],
            send_sem=cross_send.at[place.chip(dest)],
            recv_sem=cross_recv.at[place.chip(dest)],
            device_id=place.device(partner(me)),
            device_id_type=pl.DeviceIdType.MESH,
        )

    def pass_on(k, pos, way, dest, to):
        start, count = parts[k]
        slot = slot_of(place, plan, k, pos, way, to, dest)
        return pltpu.make_async_remote_copy(
            src_ref=own.at[place.flat(dest), pl.ds(start, count), :],
            dst_ref=slots[k].at[slot],
            send_sem=send.at[k, place.chip(dest)],
            recv_sem=recv[k].at[slot],
            device_id=place.device(to),
            device_id_type=pl.DeviceIdType.MESH,
        )

    def parents(k, rel, dest):
        order = place.orders[k]
        out = []
        for pos in range(3):
            dim = order[pos]
            size = place.size[dim]
            if size == 1:
                continue
            later = both(*[rel[d] == 0 for d in order[pos + 1 :]])
            if size == 2:
                other = list(me)
                other[dim] = 1 - other[dim]
                away = rel[dim] == 1
                out.append((both(later, away), pos, 0, other))
            else:
                out.append((both(later, me[dim] > dest[dim]), pos, 0, moved(me, dim, -1)))
                out.append((both(later, me[dim] < dest[dim]), pos, 1, moved(me, dim, 1)))
        return out

    walk(place, lambda rel: swap(source_of(place, me, rel)).start(), reverse=True)

    swapped = set()

    def go(k, rel):
        dest = source_of(place, me, rel)
        home = both(*[r == 0 for r in rel])
        flat, chip = place.flat(dest), place.chip(dest)
        if isinstance(home, bool):
            if rel not in swapped:
                swap(dest).wait_recv()
            swapped.add(rel)
        elif k == 0:
            swap(dest).wait_recv()

        def mix(final):
            start, count = parts[k]

            def rows_of(r):
                return pl.ds(r.start + start, r.size)

            if final:

                def put(r, v):
                    total[rows_of(r), :] = v

                def held(r):
                    return total[rows_of(r), :]

            else:

                def put(r, v):
                    own[flat, rows_of(r), :] = v.astype(own.dtype)

                def held(r):
                    return own[flat, rows_of(r), :]

            def kid(pos, way):
                slot = slot_of(place, plan, k, pos, way, me, dest)
                pass_on(k, pos, way, dest, me).wait_recv()
                return lambda r: slots[k][slot, r, :]

            kids = onward(place, place.orders[k], me, rel, dest)
            terms = [lambda r: own[flat, rows_of(r), :], lambda r: cross[chip, rows_of(r), :]]
            terms += [kid(pos, way) for cond, pos, way, _ in kids if cond is True]
            add_rows(put, terms, count)
            for cond, pos, way, _ in kids:
                if isinstance(cond, bool):
                    continue
                pl.when(cond)(lambda: add_rows(put, [held, kid(pos, way)], count))
            if not final:
                for cond, pos, way, who in parents(k, rel, dest):
                    when(cond, lambda: pass_on(k, pos, way, dest, who).start())

        if isinstance(home, bool):
            mix(home)
        else:
            pl.when(home)(lambda: mix(True))
            pl.when(jnp.logical_not(home))(lambda: mix(False))

    walk_parts(place, go, reverse=True)

    def drain(rel):
        dest = source_of(place, me, rel)
        swap(dest).wait_send()
        for k in range(place.classes):
            for cond, pos, way, who in parents(k, rel, dest):
                when(cond, lambda: pass_on(k, pos, way, dest, who).wait_send())

    walk(place, drain)


def scatter_scratch(place, rows):
    parts = place.class_rows(rows)
    plan = slot_plan(place, rows)
    dma = pltpu.SemaphoreType.DMA
    return (
        [pltpu.VMEM((place.chips, rows, LANES), jnp.bfloat16)],
        [pltpu.VMEM((plan[k][1], parts[k][1], LANES), jnp.bfloat16) for k in range(place.classes)],
        [dma((place.chips,)), dma((place.chips,)), dma((place.classes, place.chips))],
        [dma((plan[k][1],)) for k in range(place.classes)],
    )


D = 768
HEAD_DIM = 64
FF = 3072
EPSILON = 1e-06
NEG_FILL = -1e30
ROOT_HALF = 0.7071067811865476
INV_ROOT_TWO_PI = 0.3989422804014327

PIECES = (
    ("ln1_gain", (D,)),
    ("ln1_bias", (D,)),
    ("w_qkv", (D, 3 * D)),
    ("q_bias", (D,)),
    ("v_bias", (D,)),
    ("w_proj", (D, D)),
    ("proj_bias", (D,)),
    ("ln2_gain", (D,)),
    ("ln2_bias", (D,)),
    ("w_fc1", (D, FF)),
    ("fc1_bias", (FF,)),
    ("w_fc2", (FF, D)),
    ("fc2_bias", (D,)),
)
MATRICES = tuple(name for name, shape in PIECES if len(shape) == 2)
VECTORS = tuple(name for name, shape in PIECES if len(shape) == 1)
SHAPES = dict(PIECES)


def row_bases():
    bases, row = {}, 0
    for name, shape in PIECES:
        bases[name] = row
        row += math.prod(shape) // LANES
    return bases, row


BASES, TOTAL_ROWS = row_bases()
IMAGE_MAX = 98
QKV_BIAS = len(VECTORS)
TABLE = (16, FF)


def part_rows(entries):
    return -(-((LANES - 1 + entries - 1) // LANES + 1) // 16) * 16


def tile(i):
    return pl.ds(pl.multiple_of(i * 16, 16), 16)


def loop(count, body, unroll=1):
    def step(i, carry):
        for u in range(unroll):
            body(i * unroll + u)
        return carry

    whole = count // unroll
    if whole:
        lax.fori_loop(0, whole, step, 0)
    for i in range(whole * unroll, count):
        body(i)


def aligned(raw, held, stage, which, entries):
    rows = held.shape[1]
    shift = (entries * which) % LANES
    stage[0:8, :] = jnp.zeros((8, LANES), jnp.float32)

    def turn(i):
        stage[pl.ds(pl.multiple_of(i * 16 + 8, 8), 16), :] = pltpu.roll(
            raw[tile(i), :].astype(jnp.float32), shift, 1
        )

    loop(rows // 16, turn, 8)

    def merge(i):
        lane = lax.broadcasted_iota(jnp.int32, (16, LANES), 1)
        now = stage[pl.ds(i * 16 + 8, 16), :]
        before = stage[pl.ds(i * 16 + 7, 16), :]
        held[which, tile(i), :] = jnp.where(lane < shift, before, now).astype(held.dtype)

    loop(rows // 16, merge, 8)


def round_up(value, unit):
    return -(-value // unit) * unit


class Span:
    def __init__(self, low, high, name, first, depth, vectors):
        self.low, self.high = low, high
        self.name, self.first, self.depth = name, first, depth
        self.vectors = vectors


def spans(cuts):
    out, row, early = [], 0, []
    for name, shape in PIECES:
        count = math.prod(shape) // LANES
        if len(shape) == 1:
            if out:
                out[-1].vectors.append(name)
                out[-1].high = row + count
            else:
                early.append(name)
        else:
            depth = shape[0] // cuts[name]
            blocks = shape[1] // LANES
            for c in range(cuts[name]):
                start = row + c * depth * blocks
                span = Span(start, start + depth * blocks, name, c * depth, depth, [])
                if not out:
                    span.low, span.vectors = 0, early
                out.append(span)
        row += count
    return out


GATHER_SPANS = spans({name: 1 for name in MATRICES})
SCATTER_SPANS = spans({"w_qkv": 2, "w_proj": 1, "w_fc1": 2, "w_fc2": 2})


def stage_rows(spans_, rows):
    return round_up(max(s.high - s.low for s in spans_), 16) + 2 * rows + 32


def owners(span, entries):
    return (span.low * LANES) // entries, (span.high * LANES - 1) // entries


def spread(held, stage, span, entries):
    rows = held.shape[1]
    low, high = owners(span, entries)

    def one(i):
        d = low + i
        base = (entries * d) // LANES - span.low + rows
        cut = (entries * d) % LANES
        first = stage[pl.ds(base, 1), :]

        def body(t):
            stage[pl.ds(base + t * 16, 16), :] = held[d, tile(t), :].astype(jnp.float32)

        loop(rows // 16, body, 8)
        row = stage[pl.ds(base, 1), :]
        stage[pl.ds(base, 1), :] = jnp.where(cut != 0, row + first, row)

    loop(high - low + 1, one)


def form(stage, span, margin, out):
    blocks = SHAPES[span.name][1] // LANES
    base = margin + BASES[span.name] + span.first * blocks - span.low

    def body(i):
        for j in range(blocks):
            out[tile(i + span.first // 16), j * LANES : (j + 1) * LANES] = stage[
                pl.ds(base + i * 16 * blocks + j, 16, stride=blocks), :
            ].astype(out.dtype)

    loop(span.depth // 16, body, max(1, 24 // blocks))


def vector_rows(stage, span, margin, table):
    for name in span.vectors:
        at = margin + BASES[name] - span.low
        row = VECTORS.index(name)
        for j in range(SHAPES[name][0] // LANES):
            table[row : row + 1, j * LANES : (j + 1) * LANES] = stage[at + j : at + j + 1, :]


def vector(table, name):
    row = VECTORS.index(name)
    return table[row : row + 1, 0 : SHAPES[name][0]]


def lay(stage, span, margin, first, value):
    blocks = SHAPES[span.name][1] // LANES
    base = margin + BASES[span.name] - span.low + first * blocks
    for i in range(value.shape[0] // 16):
        for j in range(blocks):
            stage[pl.ds(base + i * 16 * blocks + j, 16, stride=blocks), :] = value[
                i * 16 : (i + 1) * 16, j * LANES : (j + 1) * LANES
            ]


def lay_vectors(stage, span, margin, table):
    for name in span.vectors:
        at = margin + BASES[name] - span.low
        row = VECTORS.index(name)
        for j in range(SHAPES[name][0] // LANES):
            stage[at + j : at + j + 1, :] = table[row : row + 1, j * LANES : (j + 1) * LANES]


def cut(stage, span, own, entries):
    rows = own.shape[1]
    low, high = owners(span, entries)

    def whole(d):
        base = (entries * d) // LANES - span.low + rows

        def body(t):
            own[d, tile(t), :] = stage[pl.ds(base + t * 16, 16), :].astype(own.dtype)

        loop(rows // 16, body, 8)

    def edge(d):
        base = (entries * d) // LANES - span.low + rows

        def body(t):
            now = stage[pl.ds(base + t * 16, 16), :]
            row = base + t * 16 - rows + lax.broadcasted_iota(jnp.int32, (16, LANES), 0)
            inside = jnp.logical_and(row >= 0, row < span.high - span.low)
            before = own[d, tile(t), :].astype(jnp.float32)
            own[d, tile(t), :] = jnp.where(inside, now, before).astype(own.dtype)

        loop(rows // 16, body, 8)

    edge(low)
    if high - low > 1:
        loop(high - low - 1, lambda i: whole(low + 1 + i))
    if high > low:
        edge(high)


def mean_of(v):
    return jnp.sum(v, axis=-1, keepdims=True) * (1.0 / v.shape[-1])


def normalize(v):
    centred = v - mean_of(v)
    inv_std = lax.rsqrt(mean_of(centred * centred) + EPSILON)
    return centred * inv_std, inv_std


def norm_back(grad_out, normed, inv_std, gain):
    grad_norm = grad_out * gain
    return inv_std * (grad_norm - mean_of(grad_norm) - normed * mean_of(grad_norm * normed))


def dot(a, b, left=1, right=0):
    return lax.dot_general(
        a, b, (((left,), (right,)), ((), ())), preferred_element_type=jnp.float32
    )


def columns(width, block, body):
    loop(width // block, lambda i: body(pl.ds(pl.multiple_of(i * block, block), block)))


def segments(lengths, b, images, shape, dim):
    position = lax.broadcasted_iota(jnp.int32, shape, dim)
    total, seg = 0, jnp.zeros(shape, jnp.int32)
    for i in range(images):
        total = total + lengths[b, i]
        seg = seg + jnp.where(position >= total, 1, 0)
    return seg


def valid_rows(lengths, b, images, count):
    return jnp.where(segments(lengths, b, images, (count, 1), 0) < images, 1.0, 0.0)


class Sizes:
    def __init__(self, tokens, lengths):
        self.buffers, self.images = lengths.shape
        self.full = tokens.shape[0] // self.buffers
        self.rows = min(self.full, round_up(self.images * IMAGE_MAX, 16))
        self.total = self.rows * self.buffers
        self.pairs = D // LANES

    def at(self, b):
        return slice(b * self.rows, (b + 1) * self.rows)

    def given(self, b):
        return slice(b * self.full, b * self.full + self.rows)


def low(v):
    return v.astype(jnp.bfloat16)


def half_lanes(rows):
    lane = lax.broadcasted_iota(jnp.int32, (rows, LANES), 1)
    first = low(jnp.where(lane < HEAD_DIM, 1.0, 0.0))
    return first, low(jnp.where(lane < HEAD_DIM, 0.0, 1.0))


SCALE = 1.0 / math.sqrt(HEAD_DIM)
SAVED = ("attn_in", "qkv", "probs", "mix", "mid", "mlp_in", "act", "slope")


def saved_shapes(sz):
    t = sz.total
    bf = jnp.bfloat16
    return {
        "attn_in": ((t, D), bf),
        "qkv": ((t, 3 * D), bf),
        "probs": ((sz.buffers * sz.pairs * 2, sz.rows, sz.rows), bf),
        "mix": ((t, D), bf),
        "mid": ((t, D), jnp.float32),
        "mlp_in": ((t, D), bf),
        "act": ((t, FF), bf),
        "slope": ((t, FF), bf),
    }


def forward_kernel(place, entries, sz, raw, tokens, lengths, *refs):
    mats, refs = dict(zip(MATRICES, refs[:4])), refs[4:]
    out_saved, refs = dict(zip(SAVED, refs[:8])), refs[8:]
    table, block_out, refs = refs[0], refs[1], refs[2:]
    held, stage, refs = refs[0], refs[1], refs[2:]
    w, refs = dict(zip(MATRICES, refs[:4])), refs[4:]
    a, refs = dict(zip(SAVED, refs[:8])), refs[8:]
    normed = refs[0]
    send, recv, cross, done_w, done_a = refs[1:]
    me = place.coords()
    margin = held.shape[1]

    aligned(raw, held, stage, place.flat(me), entries)
    greet(place, me)

    def norm_first(i):
        for b in range(sz.buffers):
            x = tokens[pl.ds(pl.multiple_of(b * sz.full + i * 16, 16), 16), :].astype(jnp.float32)
            normed[pl.ds(pl.multiple_of(b * sz.rows + i * 16, 16), 16), :] = normalize(x)[0]

    def after(i):
        if i is None or i == 8:
            loop(sz.rows // 16, norm_first)

    gather_all(place, me, held, send, recv, cross, after)

    def keep(name):
        pltpu.make_async_copy(a[name], out_saved[name], done_a.at[SAVED.index(name)]).start()

    for span in GATHER_SPANS:
        name = span.name
        spread(held, stage, span, entries)
        form(stage, span, margin, w[name])
        vector_rows(stage, span, margin, table)
        m = MATRICES.index(name)
        pltpu.make_async_copy(w[name], mats[name], done_w.at[m]).start()
    table[QKV_BIAS : QKV_BIAS + 1, 0:D] = vector(table, "q_bias")
    table[QKV_BIAS : QKV_BIAS + 1, D : 2 * D] = jnp.zeros((1, D), jnp.float32)
    table[QKV_BIAS : QKV_BIAS + 1, 2 * D : 3 * D] = vector(table, "v_bias")

    def scale_first(i):
        a["attn_in"][tile(i), :] = low(
            normed[tile(i), :] * vector(table, "ln1_gain") + vector(table, "ln1_bias")
        )

    loop(sz.total // 16, scale_first)
    keep("attn_in")

    def to_qkv(c):
        a["qkv"][:, c] = low(
            dot(a["attn_in"][...], w["w_qkv"][:, c]) + table[QKV_BIAS : QKV_BIAS + 1, c]
        )

    columns(3 * D, 256, to_qkv)
    keep("qkv")

    qkv, probs, mix = a["qkv"], a["probs"], a["mix"]
    for b in range(sz.buffers):
        rows = sz.at(b)
        seg_r = segments(lengths, b, sz.images, (sz.rows, 1), 0)
        seg_c = segments(lengths, b, sz.images, (1, sz.rows), 1)

        def attend(p):
            halves = half_lanes(sz.rows)
            at = lambda part: pl.ds(pl.multiple_of(part * D + p * LANES, LANES), LANES)
            q, k, v = (qkv[rows, at(part)] for part in range(3))
            mixed = None
            for h in range(2):
                s = dot(q * (halves[h] * SCALE).astype(q.dtype), k, 1, 1)
                s = jnp.where(seg_r == seg_c, s, NEG_FILL)
                e = jnp.exp(s - jnp.max(s, axis=-1, keepdims=True))
                pr = low(e * (1.0 / jnp.sum(e, axis=-1, keepdims=True)))
                probs[(b * sz.pairs + p) * 2 + h] = pr
                part = dot(pr, v * halves[h])
                mixed = part if mixed is None else mixed + part
            mix[rows, at(0)] = low(mixed)

        loop(sz.pairs, attend)
    keep("probs")
    keep("mix")

    def to_mid(c):
        made = dot(mix[...], w["w_proj"][:, c]) + table[
            VECTORS.index("proj_bias") : VECTORS.index("proj_bias") + 1, c
        ]
        for b in range(sz.buffers):
            a["mid"][sz.at(b), c] = (
                tokens[sz.given(b), c].astype(jnp.float32) + made[sz.at(b), :]
            )

    columns(D, 256, to_mid)
    keep("mid")

    def norm_second(i):
        a["mlp_in"][tile(i), :] = low(
            normalize(a["mid"][tile(i), :])[0] * vector(table, "ln2_gain")
            + vector(table, "ln2_bias")
        )

    loop(sz.total // 16, norm_second)
    keep("mlp_in")

    def to_act(c):
        at = VECTORS.index("fc1_bias")
        pre = dot(a["mlp_in"][...], w["w_fc1"][:, c]) + table[at : at + 1, c]
        phi = 0.5 * (1.0 + lax.erf(pre * ROOT_HALF))
        a["act"][:, c] = low(pre * phi)
        a["slope"][:, c] = low(phi + pre * jnp.exp(-0.5 * pre * pre) * INV_ROOT_TWO_PI)

    columns(FF, 256, to_act)
    keep("act")
    keep("slope")

    def to_out(c):
        at = VECTORS.index("fc2_bias")
        made = dot(a["act"][...], w["w_fc2"][:, c]) + table[at : at + 1, c]
        for b in range(sz.buffers):
            valid = valid_rows(lengths, b, sz.images, sz.rows)
            block_out[sz.given(b), c] = low(valid * (a["mid"][sz.at(b), c] + made[sz.at(b), :]))
            if sz.full > sz.rows:
                block_out[b * sz.full + sz.rows : (b + 1) * sz.full, c] = jnp.zeros(
                    (sz.full - sz.rows, made.shape[1]), jnp.bfloat16
                )

    columns(D, 256, to_out)
    for m, name in enumerate(MATRICES):
        pltpu.make_async_copy(w[name], mats[name], done_w.at[m]).wait()
    for i, name in enumerate(SAVED):
        pltpu.make_async_copy(a[name], out_saved[name], done_a.at[i]).wait()


def forward(place, tokens, params, lengths):
    entries = params.shape[0]
    rows = part_rows(entries)
    sz = Sizes(tokens, lengths)
    raw = jnp.pad(params, (0, rows * LANES - entries)).reshape(rows, LANES)
    any_spec = pl.BlockSpec(memory_space=pl.ANY)
    vmem = pl.BlockSpec(memory_space=pltpu.VMEM)
    smem = pl.BlockSpec(memory_space=pltpu.SMEM)
    saved = saved_shapes(sz)
    bf = jnp.bfloat16
    outs = pl.pallas_call(
        functools.partial(forward_kernel, place, entries, sz),
        out_shape=[jax.ShapeDtypeStruct(SHAPES[n], bf) for n in MATRICES]
        + [jax.ShapeDtypeStruct(*saved[n]) for n in SAVED]
        + [jax.ShapeDtypeStruct(TABLE, jnp.float32), jax.ShapeDtypeStruct(tokens.shape, bf)],
        in_specs=[vmem, vmem, smem],
        out_specs=[any_spec] * 12 + [vmem, vmem],
        scratch_shapes=[
            pltpu.VMEM((place.devices, rows, LANES), bf),
            pltpu.VMEM((stage_rows(GATHER_SPANS, rows), LANES), jnp.float32),
        ]
        + [pltpu.VMEM(SHAPES[n], bf) for n in MATRICES]
        + [pltpu.VMEM(*saved[n]) for n in SAVED]
        + [pltpu.VMEM((sz.total, D), jnp.float32)]
        + gather_sems(place)
        + [pltpu.SemaphoreType.DMA((4,)), pltpu.SemaphoreType.DMA((8,))],
        compiler_params=pltpu.CompilerParams(
            collective_id=0, has_side_effects=True, vmem_limit_bytes=67 * 10**6
        ),
        name="forward",
    )(raw, tokens, lengths)
    return dict(zip(MATRICES, outs[:4])), dict(zip(SAVED, outs[4:12])), outs[12], outs[13]


SUMS = tuple(VECTORS)


def backward_kernel(place, entries, sz, tokens, cotangent, lengths, table, *refs):
    mats, refs = dict(zip(MATRICES, refs[:4])), refs[4:]
    given, refs = dict(zip(SAVED, refs[:8])), refs[8:]
    out, input_grad, refs = refs[0], refs[1], refs[2:]
    own, cross, refs = refs[0], refs[1], refs[2:]
    n = place.classes
    slots, refs = refs[:n], refs[n:]
    cross_send, cross_recv, send = refs[:3]
    recv, refs = refs[3 : 3 + n], refs[3 + n :]
    stage, total, sums, refs = refs[0], refs[1], refs[2], refs[3:]
    big_a, big_b, refs = refs[0], refs[1], refs[2:]
    wide, slope, qkv, probs, mix, mid, narrow, x, g, temp, blank, partial, load, done = refs
    me = place.coords()
    margin = own.shape[1]
    count = sz.total
    order = ("g", "act", "w_fc2", "slope", "mlp_in", "w_fc1", "mid", "mix", "x", "qkv", "probs")

    def fetches(name):
        sem = load.at[order.index(name)]
        if name in ("g", "x"):
            src, dst = (cotangent, g) if name == "g" else (tokens, x)
            return [
                pltpu.make_async_copy(
                    src.at[sz.given(b)],
                    dst.at[sz.at(b)],
                    load.at[order.index(name) if b == 0 else len(order) + 10 + 2 * b + (name == "g")],
                )
                for b in range(sz.buffers)
            ]
        return [pltpu.make_async_copy(*places[name], sem)]

    places = {
        "act": (given["act"], wide),
        "slope": (given["slope"], slope),
        "mlp_in": (given["mlp_in"], narrow),
        "mid": (given["mid"], mid),
        "mix": (given["mix"], mix),
        "qkv": (given["qkv"], qkv),
        "probs": (given["probs"], probs),
        "w_fc2": (mats["w_fc2"], big_a),
        "w_fc1": (mats["w_fc1"], big_b),
    }

    def begin(name):
        for c in fetches(name):
            c.start()

    def ready(name):
        for c in fetches(name):
            c.wait()

    for name in order:
        begin(name)
    greet(place, me)

    def sum_to(name, c, value):
        at = SUMS.index(name)
        sums[at : at + 1, c] = value

    def ones():
        return jnp.ones((8, count), jnp.bfloat16)

    def column_sums(name, ref, width):
        def body(c):
            sum_to(name, c, dot(ones(), ref[:, c])[0:1, :])

        columns(width, 256, body)

    def pieces(name, left, right, block):
        for span in [s for s in SCATTER_SPANS if s.name == name]:

            def body(i):
                first = pl.multiple_of(span.first + i * block, block)
                lay(stage, span, margin, first, dot(left[:, pl.ds(first, block)], right(), 0, 0))

            loop(span.depth // block, body)
            yield span

    def finish(span):
        lay_vectors(stage, span, margin, sums)
        cut(stage, span, own, entries)

    ready("g")
    for b in range(sz.buffers):
        rows = sz.at(b)
        valid = valid_rows(lengths, b, sz.images, sz.rows)
        g[rows, :] = low(g[rows, :].astype(jnp.float32) * valid)
    ready("act")
    column_sums("fc2_bias", g, D)
    for span in pieces("w_fc2", wide, lambda: g[...], 256):
        finish(span)

    ready("w_fc2")
    ready("slope")

    def to_pre(i):
        c = pl.ds(pl.multiple_of(i * 256, 256), 256)
        made = dot(g[...], big_a[c, :], 1, 1)
        wide[:, c] = low(made * slope[:, c].astype(jnp.float32))

    loop(FF // 256, to_pre)
    late = [
        pltpu.make_async_copy(
            mats["w_qkv"].at[:, i * D : (i + 1) * D],
            big_a.at[i * D : (i + 1) * D],
            load.at[len(order) + 8 + i],
        )
        for i in range(3)
    ]
    late.append(
        pltpu.make_async_copy(mats["w_proj"], big_a.at[3 * D : 4 * D], load.at[len(order) + 11])
    )
    for c in reversed(late):
        c.start()
    ready("mlp_in")
    column_sums("fc1_bias", wide, FF)
    for span in pieces("w_fc1", narrow, lambda: wide[...], 128):
        finish(span)

    attn_load = pltpu.make_async_copy(given["attn_in"], narrow, load.at[len(order) + 7])
    attn_load.start()
    ready("w_fc1")

    def to_mlp(i):
        c = pl.ds(pl.multiple_of(i * 256, 256), 256)
        temp[:, c] = dot(wide[...], big_b[c, :], 1, 1)

    loop(D // 256, to_mlp)
    ready("mid")

    def folded(v):
        return v[0:8, :] + v[8:16, :]

    def norm_sums(body, gain, bias):
        partial[...] = jnp.zeros(partial.shape, jnp.float32)

        def step(i):
            for which, value in enumerate(body(i)):
                partial[which] += folded(value)

        loop(count // 16, step, 2)
        for which, name in enumerate((gain, bias)):
            at = SUMS.index(name)
            sums[at : at + 1, 0:D] = jnp.sum(partial[which], axis=0, keepdims=True)

    def back_second(i):
        normed, inv = normalize(mid[tile(i), :])
        d = temp[tile(i), :]
        v = g[tile(i), :].astype(jnp.float32) + norm_back(d, normed, inv, vector(table, "ln2_gain"))
        mid[tile(i), :] = v
        g[tile(i), :] = low(v)
        return d * normed, d

    norm_sums(back_second, "ln2_gain", "ln2_bias")
    ready("mix")
    column_sums("proj_bias", g, D)
    for span in pieces("w_proj", mix, lambda: g[...], 256):
        finish(span)
    late[3].wait()

    def to_mix(i):
        c = pl.ds(pl.multiple_of(i * 256, 256), 256)
        rows = pl.ds(pl.multiple_of(3 * D + i * 256, 256), 256)
        slope[:, c] = low(dot(g[...], big_a[rows, :], 1, 1))

    loop(D // 256, to_mix)
    ready("qkv")
    ready("probs")
    for b in range(sz.buffers):
        rows = sz.at(b)

        def attend(p):
            halves = half_lanes(sz.rows)
            at = lambda part: pl.ds(pl.multiple_of(part * D + p * LANES, LANES), LANES)
            q, k, v = (qkv[rows, at(part)] for part in range(3))
            dm = slope[rows, at(0)]
            dq = dk = dv = 0.0
            for h in range(2):
                pr = probs[(b * sz.pairs + p) * 2 + h]
                dmh = dm * halves[h]
                dp = dot(dmh, v, 1, 1)
                prf = pr.astype(jnp.float32)
                ds = low(prf * (dp - jnp.sum(prf * dp, axis=-1, keepdims=True)))
                dv = dv + dot(pr, dmh, 0, 0)
                dq = dq + dot(ds, k * halves[h])
                dk = dk + dot(ds, q * halves[h], 0, 0)
            wide[rows, at(0)] = low(dq * SCALE)
            wide[rows, at(1)] = low(dk * SCALE)
            wide[rows, at(2)] = low(dv)

        loop(sz.pairs, attend)
    for c in late[:3]:
        c.wait()

    def to_attn(i):
        c = pl.ds(pl.multiple_of(i * 256, 256), 256)
        made = None
        for part in range(3):
            rows = pl.ds(pl.multiple_of(part * D + i * 256, 256), 256)
            term = dot(wide[:, part * D : (part + 1) * D], big_a[rows, :], 1, 1)
            made = term if made is None else made + term
        temp[:, c] = made

    loop(D // 256, to_attn)
    ready("x")

    def back_first(i):
        normed, inv = normalize(x[tile(i), :].astype(jnp.float32))
        d = temp[tile(i), :]
        mid[tile(i), :] = mid[tile(i), :] + norm_back(d, normed, inv, vector(table, "ln1_gain"))
        return d * normed, d

    norm_sums(back_first, "ln1_gain", "ln1_bias")
    outs = []
    for b in range(sz.buffers):
        outs.append(
            pltpu.make_async_copy(mid.at[sz.at(b)], input_grad.at[sz.given(b)], done.at[2 * b])
        )
        if sz.full > sz.rows:
            blank[...] = jnp.zeros(blank.shape, blank.dtype)
            outs.append(
                pltpu.make_async_copy(
                    blank,
                    input_grad.at[b * sz.full + sz.rows : (b + 1) * sz.full],
                    done.at[2 * b + 1],
                )
            )
    for c in outs:
        c.start()

    attn_load.wait()

    def qv_sums(c):
        wide_sum = dot(ones(), wide[:, c])[0:1, :]
        sums[len(SUMS) : len(SUMS) + 1, c] = wide_sum

    columns(3 * D, 256, qv_sums)
    for name, part in (("q_bias", 0), ("v_bias", 2)):
        at = SUMS.index(name)
        sums[at : at + 1, 0:D] = sums[len(SUMS) : len(SUMS) + 1, part * D : (part + 1) * D]
    for span in pieces("w_qkv", narrow, lambda: wide[:, 0 : 3 * D], 128):
        finish(span)

    scatter_all(place, me, own, cross, slots, total, (cross_send, cross_recv, send, recv))
    shift = (entries * place.flat(me)) % LANES
    back = (LANES - shift) % LANES
    rows = own.shape[1]

    def turn(i):
        total[tile(i), :] = pltpu.roll(total[tile(i), :], back, 1)

    loop(rows // 16, turn, 8)

    def merge(i):
        lane = lax.broadcasted_iota(jnp.int32, (16, LANES), 1)
        now = total[pl.ds(i * 16, 16), :]
        after = total[pl.ds(i * 16 + 1, 16), :]
        out[tile(i), :] = jnp.where(lane < LANES - shift, now, after)

    loop(rows // 16, merge, 8)
    for c in outs:
        c.wait()


def backward(place, tokens, cotangent, lengths, mats, saved, table, entries):
    rows = part_rows(entries)
    sz = Sizes(tokens, lengths)
    cross, slots, sems, recv = scatter_scratch(place, rows)
    any_spec = pl.BlockSpec(memory_space=pl.ANY)
    vmem = pl.BlockSpec(memory_space=pltpu.VMEM)
    smem = pl.BlockSpec(memory_space=pltpu.SMEM)
    bf, f32 = jnp.bfloat16, jnp.float32
    shapes = saved_shapes(sz)
    scratch = lambda name: pltpu.VMEM(*shapes[name])
    out, input_grad = pl.pallas_call(
        functools.partial(backward_kernel, place, entries, sz),
        out_shape=[
            jax.ShapeDtypeStruct((rows, LANES), f32),
            jax.ShapeDtypeStruct(tokens.shape, f32),
        ],
        in_specs=[any_spec, any_spec, smem, vmem] + [any_spec] * 12,
        out_specs=[vmem, any_spec],
        scratch_shapes=[pltpu.VMEM((place.devices, rows, LANES), bf)]
        + cross
        + slots
        + sems
        + recv
        + [
            pltpu.VMEM((stage_rows(SCATTER_SPANS, rows), LANES), f32),
            pltpu.VMEM((rows + 16, LANES), f32),
            pltpu.VMEM(TABLE, f32),
            pltpu.VMEM((FF, D), bf),
            pltpu.VMEM((D, FF), bf),
            scratch("act"),
            scratch("slope"),
            scratch("qkv"),
            scratch("probs"),
            scratch("mix"),
            scratch("mid"),
            scratch("mlp_in"),
            pltpu.VMEM((sz.total, D), bf),
            pltpu.VMEM((sz.total, D), bf),
            pltpu.VMEM((sz.total, D), f32),
            pltpu.VMEM((max(8, sz.full - sz.rows), D), f32),
            pltpu.VMEM((2, 8, D), f32),
            pltpu.SemaphoreType.DMA((24 + 2 * sz.buffers,)),
            pltpu.SemaphoreType.DMA((2 * sz.buffers,)),
        ],
        compiler_params=pltpu.CompilerParams(
            collective_id=1, has_side_effects=True, vmem_limit_bytes=67 * 10**6
        ),
        name="backward",
    )(tokens, cotangent, lengths, table, *[mats[m] for m in MATRICES], *[saved[s] for s in SAVED])
    return input_grad, out.reshape(-1)[:entries]


def solution(mesh):
    place = Place(mesh)

    def shards(tokens, cotangent, params, lengths):
        mats, saved, table, out = forward(place, tokens, params, lengths)
        input_grad, grad = backward(
            place, tokens, cotangent, lengths, mats, saved, table, params.shape[0]
        )
        return out, input_grad, grad

    rows, flat = P(AXES, None), P(AXES)
    return jax.shard_map(
        shards,
        mesh=mesh,
        in_specs=(rows, rows, flat, rows),
        out_specs=(rows, rows, flat),
        check_vma=False,
    )
```

```python
import functools
import math

import jax
import jax.numpy as jnp
from jax import lax
from jax.experimental import pallas as pl
from jax.experimental.pallas import tpu as pltpu
from jax.sharding import PartitionSpec as P

ATTN_IN_NAME = "attn_in"
QKV_NAME = "qkv"
PROBS_NAME = "probs"
MIX_NAME = "mix"
MID_NAME = "mid"
MLP_IN_NAME = "mlp_in"
ACT_NAME = "act"
SLOPE_NAME = "slope"
LN1_GAIN_NAME = "ln1_gain"
LN1_BIAS_NAME = "ln1_bias"
W_QKV_NAME = "w_qkv"
Q_BIAS_NAME = "q_bias"
V_BIAS_NAME = "v_bias"
W_PROJ_NAME = "w_proj"
PROJ_BIAS_NAME = "proj_bias"
LN2_GAIN_NAME = "ln2_gain"
LN2_BIAS_NAME = "ln2_bias"
W_FC1_NAME = "w_fc1"
FC1_BIAS_NAME = "fc1_bias"
W_FC2_NAME = "w_fc2"
FC2_BIAS_NAME = "fc2_bias"
G_NAME = "g"
X_NAME = "x"
BACKWARD_NAME = "backward"
AXES = ("dp", "fsdp")
LANES = 128
CORE = 3
MESH = pl.DeviceIdType.MESH


def quot(a, b):
    if isinstance(a, int) and isinstance(b, int):
        return a // b
    return a if isinstance(b, int) and b == 1 else lax.div(a, jnp.int32(b))


def rest(a, b):
    if isinstance(a, int) and isinstance(b, int):
        return a % b
    return lax.rem(a, jnp.int32(b))


def pick(cond, a, b):
    return lax.select(cond, lax.add(jnp.int32(0), a), lax.add(jnp.int32(0), b))


class Place:
    def __init__(self, mesh):
        devs = mesh.devices
        spot = lambda d: (*d.coords, d.core_on_chip)
        self.shape = devs.shape
        self.digits = []
        for axis in range(2):
            line = [spot(devs[i, 0] if axis == 0 else devs[0, i]) for i in range(devs.shape[axis])]
            found, stride = [], 1
            while stride < len(line):
                delta = [b - a for a, b in zip(line[0], line[stride])]
                phys = [p for p in range(4) if delta[p]][0]
                step, size = delta[phys], 1
                while (
                    size * stride < len(line)
                    and line[size * stride][phys] - line[0][phys] == size * step
                    and all(line[size * stride][q] == line[0][q] for q in range(4) if q != phys)
                ):
                    size += 1
                found.append((phys, step, size, stride))
                stride *= size
            self.digits.append(found)
        self.size = [1, 1, 1, 1]
        for found in self.digits:
            for phys, _, size, _ in found:
                self.size[phys] *= size
        self.devices = devs.size
        self.chips = math.prod(self.size[:3])
        long = max(range(3), key=lambda p: self.size[p])
        a, b = [p for p in range(3) if p != long]
        self.orders = ((long, a, b), (long, b, a))
        self.shares = (1, 1)
        if self.chips <= 16:
            self.orders += ((a, long, b), (b, long, a))
            self.shares += (2, 2)
        self.classes = len(self.orders)

    def coords(self):
        index = [lax.axis_index(name) for name in AXES]
        out = [0, 0, 0, 0]
        for axis in range(2):
            for phys, step, size, stride in self.digits[axis]:
                out[phys] = out[phys] + rest(quot(index[axis], stride), size) * step
        return out

    def device(self, coords):
        out = []
        for axis in range(2):
            total = 0
            for phys, step, size, stride in self.digits[axis]:
                total = total + rest(quot(coords[phys], step), size) * stride
            out.append(total)
        return tuple(out)

    def flat(self, coords):
        dp, fsdp = self.device(coords)
        return dp * self.shape[1] + fsdp

    def chip(self, coords):
        return (coords[0] * self.size[1] + coords[1]) * self.size[2] + coords[2]

    def class_rows(self, rows):
        units = rows // 16
        counts = [units * share // sum(self.shares) for share in self.shares]
        counts[-1] += units - sum(counts)
        out, start = [], 0
        for count in counts:
            out.append((start * 16, count * 16))
            start += count
        return out


def flipped(mine, rel, size):
    total, bit = 0, 1
    while bit < size:
        total = total + bit * rest(rest(quot(mine, bit), 2) + rest(quot(rel, bit), 2), 2)
        bit *= 2
    return total


def both(*conds):
    known = [c for c in conds if isinstance(c, bool)]
    if not all(known):
        return False
    rest = [c for c in conds if not isinstance(c, bool)]
    return functools.reduce(jnp.logical_and, rest) if rest else True


def when(cond, fn):
    if isinstance(cond, bool):
        if cond:
            fn()
    else:
        pl.when(cond)(fn)


def moved(coords, dim, by):
    out = list(coords)
    out[dim] = out[dim] + by
    return out


def partner(coords):
    out = list(coords)
    out[CORE] = 1 - out[CORE]
    return out


def neighbours(place, me):
    out = [(True, partner(me))]
    for dim in range(3):
        if place.size[dim] == 1:
            continue
        if place.size[dim] == 2:
            other = list(me)
            other[dim] = 1 - other[dim]
            out.append((True, other))
        else:
            out.append((me[dim] < place.size[dim] - 1, moved(me, dim, 1)))
            out.append((me[dim] > 0, moved(me, dim, -1)))
    return out


def greet(place, me):
    barrier = pltpu.get_barrier_semaphore()
    nbrs = neighbours(place, me)
    for cond, who in nbrs:
        when(
            cond,
            lambda who=who: pl.semaphore_signal(
                barrier, inc=1, device_id=place.device(who), device_id_type=pl.DeviceIdType.MESH
            ),
        )
    peers = sum(1 if cond is True else jnp.where(cond, 1, 0) for cond, _ in nbrs)
    pl.semaphore_wait(barrier, peers)


def onward(place, order, me, rel, src):
    out = []
    for pos in range(3):
        dim = order[pos]
        size = place.size[dim]
        if size == 1:
            continue
        later = [rel[d] == 0 for d in order[pos + 1 :]]
        if size == 2:
            other = list(me)
            other[dim] = 1 - other[dim]
            out.append((both(*later, rel[dim] == 0), pos, 0, other))
        else:
            for way, by in ((0, 1), (1, -1)):
                if by == 1:
                    here = both(me[dim] >= src[dim], me[dim] < size - 1)
                else:
                    here = both(me[dim] <= src[dim], me[dim] > 0)
                cond = both(*later, here)
                out.append((cond, pos, way, moved(me, dim, by)))
    return out


PASSES = (
    0, 16, 32, 48, 1, 17, 40, 33, 52, 49, 41, 56, 3, 8, 2, 20, 35, 34, 10, 53, 18, 28,
    11, 5, 51, 36, 12, 19, 45, 57, 50, 9, 7, 21, 55, 54, 60, 25, 44, 6, 22, 29, 24, 42,
    58, 27, 37, 26, 59, 43, 15, 23, 4, 39, 61, 14, 30, 13, 62, 38, 63, 31, 47, 46,
)


def walk_parts(place, body, reverse=False, after=None):
    if place.size[:3] == [2, 2, 4]:
        for i, code in enumerate(PASSES[::-1] if reverse else PASSES):
            body(code // 16, ((code // 8) % 2, (code // 4) % 2, code % 4))
            if after is not None:
                after(i)
        return

    def each(rel):
        for k in range(place.classes):
            body(k, rel)

    walk(place, each, reverse)
    if after is not None:
        after(None)


def walk(place, body, reverse=False):
    sizes = place.size[:3]
    if place.chips <= 16:
        rels = [
            (x, y, z) for x in range(sizes[0]) for y in range(sizes[1]) for z in range(sizes[2])
        ]
        rels.sort(key=lambda r: (sum(r), r), reverse=reverse)
        for rel in rels:
            body(rel)
        return

    def step(i, carry):
        i = place.chips - 1 - i if reverse else i
        body((i % sizes[0], (i // sizes[0]) % sizes[1], i // (sizes[0] * sizes[1])))
        return carry

    lax.fori_loop(0, place.chips, step, 0)


def source_of(place, me, rel):
    return [flipped(me[d], rel[d], place.size[d]) for d in range(3)] + [me[CORE]]


def gather_all(place, me, held, send, recv, cross, after=None):
    rows = held.shape[1]
    parts = place.class_rows(rows)

    def copy(k, src, slot, sem, who):
        start, count = parts[k]
        ref = held.at[place.flat(src), pl.ds(start, count), :]
        return pltpu.make_async_remote_copy(
            src_ref=ref,
            dst_ref=ref,
            send_sem=send.at[k, place.chip(src), slot],
            recv_sem=sem.at[k, place.chip(src)],
            device_id=place.device(who),
            device_id_type=pl.DeviceIdType.MESH,
        )

    def sends(k, rel, src, act):
        for cond, pos, way, who in onward(place, place.orders[k], me, rel, src):
            when(cond, lambda: act(copy(k, src, pos * 2 + way, recv, who)))
        act(copy(k, src, 6, cross, partner(me)))

    def go(k, rel):
        src = source_of(place, me, rel)
        home = both(*[r == 0 for r in rel])
        if home is not True:
            away = True if home is False else jnp.logical_not(home)
            when(away, lambda: copy(k, src, 0, recv, me).wait_recv())
        sends(k, rel, src, lambda c: c.start())

    walk_parts(place, go, after=after)

    def drain(rel):
        src = source_of(place, me, rel)
        theirs = partner(src)
        for k in range(place.classes):
            sends(k, rel, src, lambda c: c.wait_send())
            copy(k, theirs, 0, cross, me).wait_recv()

    walk(place, drain)


def gather_sems(place):
    return [
        pltpu.SemaphoreType.DMA((place.classes, place.chips, 7)),
        pltpu.SemaphoreType.DMA((place.classes, place.chips)),
        pltpu.SemaphoreType.DMA((place.classes, place.chips)),
    ]


def slot_plan(place, rows):
    plan = []
    for order in place.orders:
        starts, total = [], 0
        for pos in range(3):
            before = math.prod(place.size[d] for d in order[:pos])
            size = place.size[order[pos]]
            starts.append(total)
            total += before * (1 if size == 2 else size + 1 if size > 1 else 0)
        plan.append((starts, total))
    return plan


def slot_of(place, plan, k, pos, way, at, dest):
    order = place.orders[k]
    index = 0
    for d in order[:pos]:
        index = index * place.size[d] + dest[d]
    dim = order[pos]
    size = place.size[dim]
    if size > 2:
        spot = dest[dim]
        if way == 1:
            spot = spot + pick(at[dim] == dest[dim], size - dest[dim], 0)
        index = index * (size + 1) + spot
    return plan[k][0][pos] + index


def add_rows(dst, a, b, count, step=16):
    def body(i, carry):
        r = pl.ds(pl.multiple_of(i * step, step), step)
        dst(r, a(r).astype(jnp.float32) + b(r).astype(jnp.float32))
        return carry

    lax.fori_loop(0, count // step, body, 0)


def scatter_all(place, me, own, cross, slots, total, sems):
    cross_send, cross_recv, send, recv = sems
    rows = own.shape[1]
    parts = place.class_rows(rows)
    plan = slot_plan(place, rows)

    def swap(dest):
        return pltpu.make_async_remote_copy(
            src_ref=own.at[place.flat(partner(dest))],
            dst_ref=cross.at[place.chip(dest)],
            send_sem=cross_send.at[place.chip(dest)],
            recv_sem=cross_recv.at[place.chip(dest)],
            device_id=place.device(partner(me)),
            device_id_type=pl.DeviceIdType.MESH,
        )

    def pass_on(k, pos, way, dest, to):
        start, count = parts[k]
        slot = slot_of(place, plan, k, pos, way, to, dest)
        return pltpu.make_async_remote_copy(
            src_ref=own.at[place.flat(dest), pl.ds(start, count), :],
            dst_ref=slots[k].at[slot],
            send_sem=send.at[k, place.chip(dest)],
            recv_sem=recv[k].at[slot],
            device_id=place.device(to),
            device_id_type=pl.DeviceIdType.MESH,
        )

    def parents(k, rel, dest):
        order = place.orders[k]
        out = []
        for pos in range(3):
            dim = order[pos]
            size = place.size[dim]
            if size == 1:
                continue
            later = both(*[rel[d] == 0 for d in order[pos + 1 :]])
            if size == 2:
                other = list(me)
                other[dim] = 1 - other[dim]
                away = rel[dim] == 1
                out.append((both(later, away), pos, 0, other))
            else:
                out.append((both(later, me[dim] > dest[dim]), pos, 0, moved(me, dim, -1)))
                out.append((both(later, me[dim] < dest[dim]), pos, 1, moved(me, dim, 1)))
        return out

    walk(place, lambda rel: swap(source_of(place, me, rel)).start(), reverse=True)

    def go(rel):
        dest = source_of(place, me, rel)
        home = both(*[r == 0 for r in rel])
        flat, chip = place.flat(dest), place.chip(dest)
        swap(dest).wait_recv()

        def mix(final):
            for k in range(place.classes):
                start, count = parts[k]

                def rows_of(r):
                    return pl.ds(r.start + start, r.size)

                if final:

                    def put(r, v):
                        total[rows_of(r), :] = v

                    def held(r):
                        return total[rows_of(r), :]

                else:

                    def put(r, v):
                        own[flat, rows_of(r), :] = v.astype(own.dtype)

                    def held(r):
                        return own[flat, rows_of(r), :]

                add_rows(
                    put,
                    lambda r: own[flat, rows_of(r), :],
                    lambda r: cross[chip, rows_of(r), :],
                    count,
                )
                for cond, pos, way, who in onward(place, place.orders[k], me, rel, dest):

                    def take():
                        slot = slot_of(place, plan, k, pos, way, me, dest)
                        pass_on(k, pos, way, dest, me).wait_recv()
                        add_rows(put, held, lambda r: slots[k][slot, r, :], count)

                    when(cond, take)
                if not final:
                    for cond, pos, way, who in parents(k, rel, dest):
                        when(cond, lambda: pass_on(k, pos, way, dest, who).start())

        if isinstance(home, bool):
            mix(home)
        else:
            pl.when(home)(lambda: mix(True))
            pl.when(jnp.logical_not(home))(lambda: mix(False))

    walk(place, go, reverse=True)

    def drain(rel):
        dest = source_of(place, me, rel)
        swap(dest).wait_send()
        for k in range(place.classes):
            for cond, pos, way, who in parents(k, rel, dest):
                when(cond, lambda: pass_on(k, pos, way, dest, who).wait_send())

    walk(place, drain)


def scatter_scratch(place, rows):
    parts = place.class_rows(rows)
    plan = slot_plan(place, rows)
    dma = pltpu.SemaphoreType.DMA
    return (
        [pltpu.VMEM((place.chips, rows, LANES), jnp.bfloat16)],
        [pltpu.VMEM((plan[k][1], parts[k][1], LANES), jnp.bfloat16) for k in range(place.classes)],
        [dma((place.chips,)), dma((place.chips,)), dma((place.classes, place.chips))],
        [dma((plan[k][1],)) for k in range(place.classes)],
    )


D = 768
HEAD_DIM = 64
FF = 3072
EPSILON = 1e-06
NEG_FILL = -1e30
ROOT_HALF = 0.7071067811865476
INV_ROOT_TWO_PI = 0.3989422804014327

PIECES = (
    (LN1_GAIN_NAME, (D,)),
    (LN1_BIAS_NAME, (D,)),
    (W_QKV_NAME, (D, 3 * D)),
    (Q_BIAS_NAME, (D,)),
    (V_BIAS_NAME, (D,)),
    (W_PROJ_NAME, (D, D)),
    (PROJ_BIAS_NAME, (D,)),
    (LN2_GAIN_NAME, (D,)),
    (LN2_BIAS_NAME, (D,)),
    (W_FC1_NAME, (D, FF)),
    (FC1_BIAS_NAME, (FF,)),
    (W_FC2_NAME, (FF, D)),
    (FC2_BIAS_NAME, (D,)),
)
MATRICES = tuple(name for name, shape in PIECES if len(shape) == 2)
VECTORS = tuple(name for name, shape in PIECES if len(shape) == 1)
SHAPES = dict(PIECES)


def row_bases():
    bases, row = {}, 0
    for name, shape in PIECES:
        bases[name] = row
        row += math.prod(shape) // LANES
    return bases, row


BASES, TOTAL_ROWS = row_bases()
IMAGE_MAX = 98
QKV_BIAS = len(VECTORS)
TABLE = (16, FF)


def part_rows(entries):
    return -(-((LANES - 1 + entries - 1) // LANES + 1) // 16) * 16


def tile(i):
    return pl.ds(pl.multiple_of(i * 16, 16), 16)


def loop(count, body, unroll=1):
    def step(i, carry):
        for u in range(unroll):
            body(i * unroll + u)
        return carry

    whole = count // unroll
    if whole:
        lax.fori_loop(0, whole, step, 0)
    for i in range(whole * unroll, count):
        body(i)


def aligned(raw, held, stage, which, entries):
    rows = held.shape[1]
    shift = (entries * which) % LANES
    stage[0:8, :] = jnp.zeros((8, LANES), jnp.float32)

    def turn(i):
        stage[pl.ds(pl.multiple_of(i * 16 + 8, 8), 16), :] = pltpu.roll(
            raw[tile(i), :].astype(jnp.float32), shift, 1
        )

    loop(rows // 16, turn, 8)

    def merge(i):
        lane = lax.broadcasted_iota(jnp.int32, (16, LANES), 1)
        now = stage[pl.ds(i * 16 + 8, 16), :]
        before = stage[pl.ds(i * 16 + 7, 16), :]
        held[which, tile(i), :] = jnp.where(lane < shift, before, now).astype(held.dtype)

    loop(rows // 16, merge, 8)


def round_up(value, unit):
    return -(-value // unit) * unit


class Span:
    def __init__(self, low, high, name, first, depth, vectors):
        self.low, self.high = low, high
        self.name, self.first, self.depth = name, first, depth
        self.vectors = vectors


def spans(cuts):
    out, row, early = [], 0, []
    for name, shape in PIECES:
        count = math.prod(shape) // LANES
        if len(shape) == 1:
            if out:
                out[-1].vectors.append(name)
                out[-1].high = row + count
            else:
                early.append(name)
        else:
            depth = shape[0] // cuts[name]
            blocks = shape[1] // LANES
            for c in range(cuts[name]):
                start = row + c * depth * blocks
                span = Span(start, start + depth * blocks, name, c * depth, depth, [])
                if not out:
                    span.low, span.vectors = 0, early
                out.append(span)
        row += count
    return out


GATHER_SPANS = spans({name: 1 for name in MATRICES})
SCATTER_SPANS = spans({W_QKV_NAME: 2, W_PROJ_NAME: 1, W_FC1_NAME: 2, W_FC2_NAME: 2})


def stage_rows(spans_, rows):
    return round_up(max(s.high - s.low for s in spans_), 16) + 2 * rows + 32


def owners(span, entries):
    return (span.low * LANES) // entries, (span.high * LANES - 1) // entries


def spread(held, stage, span, entries):
    rows = held.shape[1]
    low, high = owners(span, entries)

    def one(i):
        d = low + i
        base = (entries * d) // LANES - span.low + rows
        cut = (entries * d) % LANES
        first = stage[pl.ds(base, 1), :]

        def body(t):
            stage[pl.ds(base + t * 16, 16), :] = held[d, tile(t), :].astype(jnp.float32)

        loop(rows // 16, body, 8)
        row = stage[pl.ds(base, 1), :]
        stage[pl.ds(base, 1), :] = jnp.where(cut != 0, row + first, row)

    loop(high - low + 1, one)


def form(stage, span, margin, out):
    blocks = SHAPES[span.name][1] // LANES
    base = margin + BASES[span.name] + span.first * blocks - span.low

    def body(i):
        for j in range(blocks):
            out[tile(i + span.first // 16), j * LANES : (j + 1) * LANES] = stage[
                pl.ds(base + i * 16 * blocks + j, 16, stride=blocks), :
            ].astype(out.dtype)

    loop(span.depth // 16, body, max(1, 24 // blocks))


def vector_rows(stage, span, margin, table):
    for name in span.vectors:
        at = margin + BASES[name] - span.low
        row = VECTORS.index(name)
        for j in range(SHAPES[name][0] // LANES):
            table[row : row + 1, j * LANES : (j + 1) * LANES] = stage[at + j : at + j + 1, :]


def vector(table, name):
    row = VECTORS.index(name)
    return table[row : row + 1, 0 : SHAPES[name][0]]


def lay(stage, span, margin, first, value):
    blocks = SHAPES[span.name][1] // LANES
    base = margin + BASES[span.name] - span.low + first * blocks
    for i in range(value.shape[0] // 16):
        for j in range(blocks):
            stage[pl.ds(base + i * 16 * blocks + j, 16, stride=blocks), :] = value[
                i * 16 : (i + 1) * 16, j * LANES : (j + 1) * LANES
            ]


def lay_vectors(stage, span, margin, table):
    for name in span.vectors:
        at = margin + BASES[name] - span.low
        row = VECTORS.index(name)
        for j in range(SHAPES[name][0] // LANES):
            stage[at + j : at + j + 1, :] = table[row : row + 1, j * LANES : (j + 1) * LANES]


def cut(stage, span, own, entries):
    rows = own.shape[1]
    low, high = owners(span, entries)

    def whole(d):
        base = (entries * d) // LANES - span.low + rows

        def body(t):
            own[d, tile(t), :] = stage[pl.ds(base + t * 16, 16), :].astype(own.dtype)

        loop(rows // 16, body, 8)

    def edge(d):
        base = (entries * d) // LANES - span.low + rows

        def body(t):
            now = stage[pl.ds(base + t * 16, 16), :]
            row = base + t * 16 - rows + lax.broadcasted_iota(jnp.int32, (16, LANES), 0)
            inside = jnp.logical_and(row >= 0, row < span.high - span.low)
            before = own[d, tile(t), :].astype(jnp.float32)
            own[d, tile(t), :] = jnp.where(inside, now, before).astype(own.dtype)

        loop(rows // 16, body, 8)

    edge(low)
    if high - low > 1:
        loop(high - low - 1, lambda i: whole(low + 1 + i))
    if high > low:
        edge(high)


def mean_of(v):
    return jnp.sum(v, axis=-1, keepdims=True) * (1.0 / v.shape[-1])


def normalize(v):
    centred = v - mean_of(v)
    inv_std = lax.rsqrt(mean_of(centred * centred) + EPSILON)
    return centred * inv_std, inv_std


def norm_back(grad_out, normed, inv_std, gain):
    grad_norm = grad_out * gain
    return inv_std * (grad_norm - mean_of(grad_norm) - normed * mean_of(grad_norm * normed))


def dot(a, b, left=1, right=0):
    return lax.dot_general(
        a, b, (((left,), (right,)), ((), ())), preferred_element_type=jnp.float32
    )


def columns(width, block, body):
    loop(width // block, lambda i: body(pl.ds(pl.multiple_of(i * block, block), block)))


def segments(lengths, b, images, shape, dim):
    position = lax.broadcasted_iota(jnp.int32, shape, dim)
    total, seg = 0, jnp.zeros(shape, jnp.int32)
    for i in range(images):
        total = total + lengths[b, i]
        seg = seg + jnp.where(position >= total, 1, 0)
    return seg


def valid_rows(lengths, b, images, count):
    return jnp.where(segments(lengths, b, images, (count, 1), 0) < images, 1.0, 0.0)


class Sizes:
    def __init__(self, tokens, lengths):
        self.buffers, self.images = lengths.shape
        self.full = tokens.shape[0] // self.buffers
        self.rows = min(self.full, round_up(self.images * IMAGE_MAX, 16))
        self.total = self.rows * self.buffers
        self.pairs = D // LANES

    def at(self, b):
        return slice(b * self.rows, (b + 1) * self.rows)

    def given(self, b):
        return slice(b * self.full, b * self.full + self.rows)


def low(v):
    return v.astype(jnp.bfloat16)


def half_lanes(rows):
    lane = lax.broadcasted_iota(jnp.int32, (rows, LANES), 1)
    first = low(jnp.where(lane < HEAD_DIM, 1.0, 0.0))
    return first, low(jnp.where(lane < HEAD_DIM, 0.0, 1.0))


SCALE = 1.0 / math.sqrt(HEAD_DIM)
SAVED = (ATTN_IN_NAME, QKV_NAME, PROBS_NAME, MIX_NAME, MID_NAME, MLP_IN_NAME, ACT_NAME, SLOPE_NAME)


def saved_shapes(sz):
    t = sz.total
    bf = jnp.bfloat16
    return {
        ATTN_IN_NAME: ((t, D), bf),
        QKV_NAME: ((t, 3 * D), bf),
        PROBS_NAME: ((sz.buffers * sz.pairs * 2, sz.rows, sz.rows), bf),
        MIX_NAME: ((t, D), bf),
        MID_NAME: ((t, D), jnp.float32),
        MLP_IN_NAME: ((t, D), bf),
        ACT_NAME: ((t, FF), bf),
        SLOPE_NAME: ((t, FF), bf),
    }


def forward_kernel(place, entries, sz, raw, tokens, lengths, *refs):
    mats, refs = dict(zip(MATRICES, refs[:4])), refs[4:]
    out_saved, refs = dict(zip(SAVED, refs[:8])), refs[8:]
    table, block_out, refs = refs[0], refs[1], refs[2:]
    held, stage, refs = refs[0], refs[1], refs[2:]
    w, refs = dict(zip(MATRICES, refs[:4])), refs[4:]
    a, refs = dict(zip(SAVED, refs[:8])), refs[8:]
    normed = refs[0]
    send, recv, cross, done_w, done_a = refs[1:]
    me = place.coords()
    margin = held.shape[1]

    aligned(raw, held, stage, place.flat(me), entries)
    greet(place, me)

    def norm_first(i):
        for b in range(sz.buffers):
            x = tokens[pl.ds(pl.multiple_of(b * sz.full + i * 16, 16), 16), :].astype(jnp.float32)
            normed[pl.ds(pl.multiple_of(b * sz.rows + i * 16, 16), 16), :] = normalize(x)[0]

    def after(i):
        if i is None or i == 8:
            loop(sz.rows // 16, norm_first)

    gather_all(place, me, held, send, recv, cross, after)

    def keep(name):
        pltpu.make_async_copy(a[name], out_saved[name], done_a.at[SAVED.index(name)]).start()

    for span in GATHER_SPANS:
        name = span.name
        spread(held, stage, span, entries)
        form(stage, span, margin, w[name])
        vector_rows(stage, span, margin, table)
        m = MATRICES.index(name)
        pltpu.make_async_copy(w[name], mats[name], done_w.at[m]).start()
    table[QKV_BIAS : QKV_BIAS + 1, 0:D] = vector(table, Q_BIAS_NAME)
    table[QKV_BIAS : QKV_BIAS + 1, D : 2 * D] = jnp.zeros((1, D), jnp.float32)
    table[QKV_BIAS : QKV_BIAS + 1, 2 * D : 3 * D] = vector(table, V_BIAS_NAME)

    def scale_first(i):
        a[ATTN_IN_NAME][tile(i), :] = low(
            normed[tile(i), :] * vector(table, LN1_GAIN_NAME) + vector(table, LN1_BIAS_NAME)
        )

    loop(sz.total // 16, scale_first)
    keep(ATTN_IN_NAME)

    def to_qkv(c):
        a[QKV_NAME][:, c] = low(
            dot(a[ATTN_IN_NAME][...], w[W_QKV_NAME][:, c]) + table[QKV_BIAS : QKV_BIAS + 1, c]
        )

    columns(3 * D, 256, to_qkv)
    keep(QKV_NAME)

    qkv, probs, mix = a[QKV_NAME], a[PROBS_NAME], a[MIX_NAME]
    for b in range(sz.buffers):
        rows = sz.at(b)
        seg_r = segments(lengths, b, sz.images, (sz.rows, 1), 0)
        seg_c = segments(lengths, b, sz.images, (1, sz.rows), 1)

        def attend(p):
            halves = half_lanes(sz.rows)
            at = lambda part: pl.ds(pl.multiple_of(part * D + p * LANES, LANES), LANES)
            q, k, v = (qkv[rows, at(part)] for part in range(3))
            mixed = None
            for h in range(2):
                s = dot(q * (halves[h] * SCALE).astype(q.dtype), k, 1, 1)
                s = jnp.where(seg_r == seg_c, s, NEG_FILL)
                e = jnp.exp(s - jnp.max(s, axis=-1, keepdims=True))
                pr = low(e * (1.0 / jnp.sum(e, axis=-1, keepdims=True)))
                probs[(b * sz.pairs + p) * 2 + h] = pr
                part = dot(pr, v * halves[h])
                mixed = part if mixed is None else mixed + part
            mix[rows, at(0)] = low(mixed)

        loop(sz.pairs, attend)
    keep(PROBS_NAME)
    keep(MIX_NAME)

    def to_mid(c):
        made = dot(mix[...], w[W_PROJ_NAME][:, c]) + table[
            VECTORS.index(PROJ_BIAS_NAME) : VECTORS.index(PROJ_BIAS_NAME) + 1, c
        ]
        for b in range(sz.buffers):
            a[MID_NAME][sz.at(b), c] = (
                tokens[sz.given(b), c].astype(jnp.float32) + made[sz.at(b), :]
            )

    columns(D, 256, to_mid)
    keep(MID_NAME)

    def norm_second(i):
        a[MLP_IN_NAME][tile(i), :] = low(
            normalize(a[MID_NAME][tile(i), :])[0] * vector(table, LN2_GAIN_NAME)
            + vector(table, LN2_BIAS_NAME)
        )

    loop(sz.total // 16, norm_second)
    keep(MLP_IN_NAME)

    def to_act(c):
        at = VECTORS.index(FC1_BIAS_NAME)
        pre = dot(a[MLP_IN_NAME][...], w[W_FC1_NAME][:, c]) + table[at : at + 1, c]
        phi = 0.5 * (1.0 + lax.erf(pre * ROOT_HALF))
        a[ACT_NAME][:, c] = low(pre * phi)
        a[SLOPE_NAME][:, c] = low(phi + pre * jnp.exp(-0.5 * pre * pre) * INV_ROOT_TWO_PI)

    columns(FF, 256, to_act)
    keep(ACT_NAME)
    keep(SLOPE_NAME)

    def to_out(c):
        at = VECTORS.index(FC2_BIAS_NAME)
        made = dot(a[ACT_NAME][...], w[W_FC2_NAME][:, c]) + table[at : at + 1, c]
        for b in range(sz.buffers):
            valid = valid_rows(lengths, b, sz.images, sz.rows)
            block_out[sz.given(b), c] = low(valid * (a[MID_NAME][sz.at(b), c] + made[sz.at(b), :]))
            if sz.full > sz.rows:
                block_out[b * sz.full + sz.rows : (b + 1) * sz.full, c] = jnp.zeros(
                    (sz.full - sz.rows, made.shape[1]), jnp.bfloat16
                )

    columns(D, 256, to_out)
    for m, name in enumerate(MATRICES):
        pltpu.make_async_copy(w[name], mats[name], done_w.at[m]).wait()
    for i, name in enumerate(SAVED):
        pltpu.make_async_copy(a[name], out_saved[name], done_a.at[i]).wait()


def forward(place, tokens, params, lengths):
    entries = params.shape[0]
    rows = part_rows(entries)
    sz = Sizes(tokens, lengths)
    raw = jnp.pad(params, (0, rows * LANES - entries)).reshape(rows, LANES)
    any_spec = pl.BlockSpec(memory_space=pl.ANY)
    vmem = pl.BlockSpec(memory_space=pltpu.VMEM)
    smem = pl.BlockSpec(memory_space=pltpu.SMEM)
    saved = saved_shapes(sz)
    bf = jnp.bfloat16
    outs = pl.pallas_call(
        functools.partial(forward_kernel, place, entries, sz),
        out_shape=[jax.ShapeDtypeStruct(SHAPES[n], bf) for n in MATRICES]
        + [jax.ShapeDtypeStruct(*saved[n]) for n in SAVED]
        + [jax.ShapeDtypeStruct(TABLE, jnp.float32), jax.ShapeDtypeStruct(tokens.shape, bf)],
        in_specs=[vmem, vmem, smem],
        out_specs=[any_spec] * 12 + [vmem, vmem],
        scratch_shapes=[
            pltpu.VMEM((place.devices, rows, LANES), bf),
            pltpu.VMEM((stage_rows(GATHER_SPANS, rows), LANES), jnp.float32),
        ]
        + [pltpu.VMEM(SHAPES[n], bf) for n in MATRICES]
        + [pltpu.VMEM(*saved[n]) for n in SAVED]
        + [pltpu.VMEM((sz.total, D), jnp.float32)]
        + gather_sems(place)
        + [pltpu.SemaphoreType.DMA((4,)), pltpu.SemaphoreType.DMA((8,))],
        compiler_params=pltpu.CompilerParams(
            collective_id=0, has_side_effects=True, vmem_limit_bytes=67 * 10**6
        ),
        name="forward",
    )(raw, tokens, lengths)
    return dict(zip(MATRICES, outs[:4])), dict(zip(SAVED, outs[4:12])), outs[12], outs[13]


SUMS = tuple(VECTORS)


def backward_kernel(place, entries, sz, tokens, cotangent, lengths, table, *refs):
    mats, refs = dict(zip(MATRICES, refs[:4])), refs[4:]
    given, refs = dict(zip(SAVED, refs[:8])), refs[8:]
    out, input_grad, refs = refs[0], refs[1], refs[2:]
    own, cross, refs = refs[0], refs[1], refs[2:]
    n = place.classes
    slots, refs = refs[:n], refs[n:]
    cross_send, cross_recv, send = refs[:3]
    recv, refs = refs[3 : 3 + n], refs[3 + n :]
    stage, total, sums, refs = refs[0], refs[1], refs[2], refs[3:]
    big_a, big_b, refs = refs[0], refs[1], refs[2:]
    wide, slope, qkv, probs, mix, mid, narrow, x, g, temp, blank, load, done = refs
    me = place.coords()
    margin = own.shape[1]
    count = sz.total
    order = (G_NAME, ACT_NAME, W_FC2_NAME, SLOPE_NAME, MLP_IN_NAME, W_FC1_NAME, MID_NAME, MIX_NAME, X_NAME, QKV_NAME, PROBS_NAME)

    def fetches(name):
        sem = load.at[order.index(name)]
        if name in (G_NAME, X_NAME):
            src, dst = (cotangent, g) if name == G_NAME else (tokens, x)
            return [
                pltpu.make_async_copy(
                    src.at[sz.given(b)],
                    dst.at[sz.at(b)],
                    load.at[order.index(name) if b == 0 else len(order) + 10 + 2 * b + (name == G_NAME)],
                )
                for b in range(sz.buffers)
            ]
        return [pltpu.make_async_copy(*places[name], sem)]

    places = {
        ACT_NAME: (given[ACT_NAME], wide),
        SLOPE_NAME: (given[SLOPE_NAME], slope),
        MLP_IN_NAME: (given[MLP_IN_NAME], narrow),
        MID_NAME: (given[MID_NAME], mid),
        MIX_NAME: (given[MIX_NAME], mix),
        QKV_NAME: (given[QKV_NAME], qkv),
        PROBS_NAME: (given[PROBS_NAME], probs),
        W_FC2_NAME: (mats[W_FC2_NAME], big_a),
        W_FC1_NAME: (mats[W_FC1_NAME], big_b),
    }

    def begin(name):
        for c in fetches(name):
            c.start()

    def ready(name):
        for c in fetches(name):
            c.wait()

    for name in order:
        begin(name)
    greet(place, me)

    def sum_to(name, c, value):
        at = SUMS.index(name)
        sums[at : at + 1, c] = value

    def ones():
        return jnp.ones((8, count), jnp.bfloat16)

    def column_sums(name, ref, width):
        def body(c):
            sum_to(name, c, dot(ones(), ref[:, c])[0:1, :])

        columns(width, 256, body)

    def pieces(name, left, right, block):
        for span in [s for s in SCATTER_SPANS if s.name == name]:

            def body(i):
                first = pl.multiple_of(span.first + i * block, block)
                lay(stage, span, margin, first, dot(left[:, pl.ds(first, block)], right(), 0, 0))

            loop(span.depth // block, body)
            yield span

    def finish(span):
        lay_vectors(stage, span, margin, sums)
        cut(stage, span, own, entries)

    ready(G_NAME)
    for b in range(sz.buffers):
        rows = sz.at(b)
        valid = valid_rows(lengths, b, sz.images, sz.rows)
        g[rows, :] = low(g[rows, :].astype(jnp.float32) * valid)
    ready(ACT_NAME)
    column_sums(FC2_BIAS_NAME, g, D)
    for span in pieces(W_FC2_NAME, wide, lambda: g[...], 256):
        finish(span)

    ready(W_FC2_NAME)
    ready(SLOPE_NAME)

    def to_pre(i):
        c = pl.ds(pl.multiple_of(i * 256, 256), 256)
        made = dot(g[...], big_a[c, :], 1, 1)
        wide[:, c] = low(made * slope[:, c].astype(jnp.float32))

    loop(FF // 256, to_pre)
    late = [
        pltpu.make_async_copy(
            mats[W_QKV_NAME].at[:, i * D : (i + 1) * D],
            big_a.at[i * D : (i + 1) * D],
            load.at[len(order) + 8 + i],
        )
        for i in range(3)
    ]
    late.append(
        pltpu.make_async_copy(mats[W_PROJ_NAME], big_a.at[3 * D : 4 * D], load.at[len(order) + 11])
    )
    for c in reversed(late):
        c.start()
    ready(MLP_IN_NAME)
    column_sums(FC1_BIAS_NAME, wide, FF)
    for span in pieces(W_FC1_NAME, narrow, lambda: wide[...], 128):
        finish(span)

    attn_load = pltpu.make_async_copy(given[ATTN_IN_NAME], narrow, load.at[len(order) + 7])
    attn_load.start()
    ready(W_FC1_NAME)

    def to_mlp(i):
        c = pl.ds(pl.multiple_of(i * 256, 256), 256)
        temp[:, c] = dot(wide[...], big_b[c, :], 1, 1)

    loop(D // 256, to_mlp)
    ready(MID_NAME)

    def column_add(name, value, first):
        at = SUMS.index(name)
        part = jnp.sum(value, axis=0, keepdims=True)
        before = sums[at : at + 1, 0:D]
        sums[at : at + 1, 0:D] = part if first else before + part

    def clear(name):
        at = SUMS.index(name)
        sums[at : at + 1, 0:D] = jnp.zeros((1, D), jnp.float32)

    clear(LN2_GAIN_NAME)
    clear(LN2_BIAS_NAME)

    def back_second(i):
        normed, inv = normalize(mid[tile(i), :])
        d = temp[tile(i), :]
        column_add(LN2_GAIN_NAME, d * normed, False)
        column_add(LN2_BIAS_NAME, d, False)
        v = g[tile(i), :].astype(jnp.float32) + norm_back(d, normed, inv, vector(table, LN2_GAIN_NAME))
        mid[tile(i), :] = v
        g[tile(i), :] = low(v)

    loop(count // 16, back_second)
    ready(MIX_NAME)
    column_sums(PROJ_BIAS_NAME, g, D)
    for span in pieces(W_PROJ_NAME, mix, lambda: g[...], 256):
        finish(span)
    late[3].wait()

    def to_mix(i):
        c = pl.ds(pl.multiple_of(i * 256, 256), 256)
        rows = pl.ds(pl.multiple_of(3 * D + i * 256, 256), 256)
        slope[:, c] = low(dot(g[...], big_a[rows, :], 1, 1))

    loop(D // 256, to_mix)
    ready(QKV_NAME)
    ready(PROBS_NAME)
    for b in range(sz.buffers):
        rows = sz.at(b)

        def attend(p):
            halves = half_lanes(sz.rows)
            at = lambda part: pl.ds(pl.multiple_of(part * D + p * LANES, LANES), LANES)
            q, k, v = (qkv[rows, at(part)] for part in range(3))
            dm = slope[rows, at(0)]
            dq = dk = dv = 0.0
            for h in range(2):
                pr = probs[(b * sz.pairs + p) * 2 + h]
                dmh = dm * halves[h]
                dp = dot(dmh, v, 1, 1)
                prf = pr.astype(jnp.float32)
                ds = low(prf * (dp - jnp.sum(prf * dp, axis=-1, keepdims=True)))
                dv = dv + dot(pr, dmh, 0, 0)
                dq = dq + dot(ds, k * halves[h])
                dk = dk + dot(ds, q * halves[h], 0, 0)
            wide[rows, at(0)] = low(dq * SCALE)
            wide[rows, at(1)] = low(dk * SCALE)
            wide[rows, at(2)] = low(dv)

        loop(sz.pairs, attend)
    for c in late[:3]:
        c.wait()

    def to_attn(i):
        c = pl.ds(pl.multiple_of(i * 256, 256), 256)
        made = None
        for part in range(3):
            rows = pl.ds(pl.multiple_of(part * D + i * 256, 256), 256)
            term = dot(wide[:, part * D : (part + 1) * D], big_a[rows, :], 1, 1)
            made = term if made is None else made + term
        temp[:, c] = made

    loop(D // 256, to_attn)
    ready(X_NAME)
    clear(LN1_GAIN_NAME)
    clear(LN1_BIAS_NAME)

    def back_first(i):
        normed, inv = normalize(x[tile(i), :].astype(jnp.float32))
        d = temp[tile(i), :]
        column_add(LN1_GAIN_NAME, d * normed, False)
        column_add(LN1_BIAS_NAME, d, False)
        mid[tile(i), :] = mid[tile(i), :] + norm_back(d, normed, inv, vector(table, LN1_GAIN_NAME))

    loop(count // 16, back_first)
    outs = []
    for b in range(sz.buffers):
        outs.append(
            pltpu.make_async_copy(mid.at[sz.at(b)], input_grad.at[sz.given(b)], done.at[2 * b])
        )
        if sz.full > sz.rows:
            blank[...] = jnp.zeros(blank.shape, blank.dtype)
            outs.append(
                pltpu.make_async_copy(
                    blank,
                    input_grad.at[b * sz.full + sz.rows : (b + 1) * sz.full],
                    done.at[2 * b + 1],
                )
            )
    for c in outs:
        c.start()

    attn_load.wait()

    def qv_sums(c):
        wide_sum = dot(ones(), wide[:, c])[0:1, :]
        sums[len(SUMS) : len(SUMS) + 1, c] = wide_sum

    columns(3 * D, 256, qv_sums)
    for name, part in ((Q_BIAS_NAME, 0), (V_BIAS_NAME, 2)):
        at = SUMS.index(name)
        sums[at : at + 1, 0:D] = sums[len(SUMS) : len(SUMS) + 1, part * D : (part + 1) * D]
    for span in pieces(W_QKV_NAME, narrow, lambda: wide[:, 0 : 3 * D], 128):
        finish(span)

    scatter_all(place, me, own, cross, slots, total, (cross_send, cross_recv, send, recv))
    shift = (entries * place.flat(me)) % LANES
    back = (LANES - shift) % LANES
    rows = own.shape[1]

    def turn(i):
        total[tile(i), :] = pltpu.roll(total[tile(i), :], back, 1)

    loop(rows // 16, turn, 8)

    def merge(i):
        lane = lax.broadcasted_iota(jnp.int32, (16, LANES), 1)
        now = total[pl.ds(i * 16, 16), :]
        after = total[pl.ds(i * 16 + 1, 16), :]
        out[tile(i), :] = jnp.where(lane < LANES - shift, now, after)

    loop(rows // 16, merge, 8)
    for c in outs:
        c.wait()


def backward(place, tokens, cotangent, lengths, mats, saved, table, entries):
    rows = part_rows(entries)
    sz = Sizes(tokens, lengths)
    cross, slots, sems, recv = scatter_scratch(place, rows)
    any_spec = pl.BlockSpec(memory_space=pl.ANY)
    vmem = pl.BlockSpec(memory_space=pltpu.VMEM)
    smem = pl.BlockSpec(memory_space=pltpu.SMEM)
    bf, f32 = jnp.bfloat16, jnp.float32
    shapes = saved_shapes(sz)
    scratch = lambda name: pltpu.VMEM(*shapes[name])
    out, input_grad = pl.pallas_call(
        functools.partial(backward_kernel, place, entries, sz),
        out_shape=[
            jax.ShapeDtypeStruct((rows, LANES), f32),
            jax.ShapeDtypeStruct(tokens.shape, f32),
        ],
        in_specs=[any_spec, any_spec, smem, vmem] + [any_spec] * 12,
        out_specs=[vmem, any_spec],
        scratch_shapes=[pltpu.VMEM((place.devices, rows, LANES), bf)]
        + cross
        + slots
        + sems
        + recv
        + [
            pltpu.VMEM((stage_rows(SCATTER_SPANS, rows), LANES), f32),
            pltpu.VMEM((rows + 16, LANES), f32),
            pltpu.VMEM(TABLE, f32),
            pltpu.VMEM((FF, D), bf),
            pltpu.VMEM((D, FF), bf),
            scratch(ACT_NAME),
            scratch(SLOPE_NAME),
            scratch(QKV_NAME),
            scratch(PROBS_NAME),
            scratch(MIX_NAME),
            scratch(MID_NAME),
            scratch(MLP_IN_NAME),
            pltpu.VMEM((sz.total, D), bf),
            pltpu.VMEM((sz.total, D), bf),
            pltpu.VMEM((sz.total, D), f32),
            pltpu.VMEM((max(8, sz.full - sz.rows), D), f32),
            pltpu.SemaphoreType.DMA((24 + 2 * sz.buffers,)),
            pltpu.SemaphoreType.DMA((2 * sz.buffers,)),
        ],
        compiler_params=pltpu.CompilerParams(
            collective_id=1, has_side_effects=True, vmem_limit_bytes=67 * 10**6
        ),
        name=BACKWARD_NAME,
    )(tokens, cotangent, lengths, table, *[mats[m] for m in MATRICES], *[saved[s] for s in SAVED])
    return input_grad, out.reshape(-1)[:entries]


class Share:
    def __init__(self, place, name, depth, width, low):
        self.name, self.depth, self.half = name, depth, width // 2
        self.high = depth // place.chips
        self.low = low
        self.rows = self.high * (width // LANES)
        third = self.high // 3
        if name is None:
            self.parts = {2: (0, self.high, 0, self.half)}
        elif third % 32:
            first = -(-self.half // LANES // 2) * LANES
            self.parts = {
                2: (0, third, 0, self.half),
                3: (third, third, 0, self.half),
                0: (2 * third, third, 0, first),
                1: (2 * third, third, first, self.half - first),
            }
        else:
            self.parts = {
                2: (0, third, 0, self.half),
                3: (third, third, 0, self.half),
                0: (2 * third, third // 2, 0, self.half),
                1: (2 * third + third // 2, third // 2, 0, self.half),
            }


def shares(place):
    out = [Share(place, n, *SHAPES[n], BASES[n]) for n in MATRICES]
    return out + [Share(place, None, 16 * place.chips, 2 * LANES, None)]


VECTOR_LIST = [(n, j) for n in VECTORS for j in range(SHAPES[n][0] // LANES)]


def fits(place):
    return place.size == [2, 2, 4, 2]


def block_of(place, coords):
    return (coords[1] * 2 + coords[0]) * 4 + coords[2]


def chip_of(block):
    return [rest(quot(block, 4), 2), quot(block, 8), rest(block, 4)]


class Summing:
    def __init__(self, place, me, parts, own, cross, slots, send, recv, cross_send, cross_recv):
        self.place, self.me, self.parts = place, me, parts
        self.own, self.cross, self.slots = own, cross, slots
        self.send, self.recv = send, recv
        self.cross_send, self.cross_recv = cross_send, cross_recv
        self.plan = slot_plan(place, 16 * sum(place.shares))
        self.slot, self.sent = 0, []
        self.waits, self.then, self.left = {}, {}, {}

    def rect(self, p, k, dest):
        top, high, left, wide = self.parts[p].parts[k]
        row = block_of(self.place, dest) * self.parts[p].high + top
        return pl.multiple_of(row, 16), high, left, wide

    def swap(self, p, first, count, chunk):
        rows = pl.ds(pl.multiple_of(first, 16), count)
        return pltpu.make_async_remote_copy(
            src_ref=self.own[p].at[1 - self.me[CORE], rows, :],
            dst_ref=self.cross[p].at[rows, :],
            send_sem=self.cross_send.at[p, chunk],
            recv_sem=self.cross_recv.at[p, chunk],
            device_id=self.place.device(partner(self.me)),
            device_id_type=MESH,
        )

    def hand(self, p, k, pos, way, dest, to):
        row, high, left, wide = self.rect(p, k, dest)
        slot = slot_of(self.place, self.plan, k, pos, way, to, dest)
        return pltpu.make_async_remote_copy(
            src_ref=self.own[p].at[self.me[CORE], pl.ds(row, high), pl.ds(left, wide)],
            dst_ref=self.slots[p][k].at[slot],
            send_sem=self.send.at[p, k, self.place.chip(dest)],
            recv_sem=self.recv[p][k].at[slot],
            device_id=self.place.device(to),
            device_id_type=MESH,
        )

    def parents(self, k, rel, dest):
        order = self.place.orders[k]
        for pos in range(2, -1, -1):
            dim = order[pos]
            if rel[dim] == 0:
                continue
            if self.place.size[dim] == 2:
                other = list(self.me)
                other[dim] = 1 - other[dim]
                return [(True, pos, 0, other)]
            here, there = self.me[dim], dest[dim]
            return [
                (here > there, pos, 0, moved(self.me, dim, -1)),
                (here < there, pos, 1, moved(self.me, dim, 1)),
            ]
        return []

    def aim(self, x, y, turn):
        z = self.me[2]
        inner = pick(z >= 2, 3 - z, z)
        end, middle = TURNS[0][turn], TURNS[1][turn]
        at = pick(inner == 0, end, middle)
        dest = [
            1 - self.me[0] if x else self.me[0],
            1 - self.me[1] if y else self.me[1],
            pick(z >= 2, 3 - at, at),
        ]
        cond = inner == 0 if turn == 0 else inner == 1 if turn == 3 else True
        if turn == 4:
            dest[2] = z
        return cond, dest + [self.me[CORE]]

    def task(self, p, k, rel, dest):
        row, high, left, wide = self.rect(p, k, dest)
        core = self.me[CORE]
        cols = slice(left, left + wide)

        def add(terms):
            for i in range(high // 16):
                rows = pl.ds(pl.multiple_of(row + i * 16, 16), 16)
                value = self.own[p][core, rows, cols].astype(jnp.float32)
                for term in terms:
                    value = value + term(i, rows).astype(jnp.float32)
                self.own[p][core, rows, cols] = low(value)

        def kid(pos, way):
            slot = slot_of(self.place, self.plan, k, pos, way, self.me, dest)
            return lambda i, rows: self.slots[p][k][slot, i * 16 : (i + 1) * 16, :]

        kids = onward(self.place, self.place.orders[k], self.me, rel, dest)
        sure = [(pos, way) for cond, pos, way, _ in kids if cond is True]
        for pos, way in sure:
            self.hand(p, k, pos, way, dest, self.me).wait_recv()
        add([lambda i, rows: self.cross[p][rows, cols]] + [kid(*s) for s in sure])
        for cond, pos, way, _ in kids:
            if cond is True or cond is False:
                continue

            def take(pos=pos, way=way):
                self.hand(p, k, pos, way, dest, self.me).wait_recv()
                add([kid(pos, way)])

            pl.when(cond)(take)
        for cond, pos, way, to in self.parents(k, rel, dest):
            when(cond, lambda: self.hand(p, k, pos, way, dest, to).start())

    def offer(self, p, waits, then):
        self.waits[p], self.then[p] = waits, then
        self.left[p] = len(self.parts[p].parts)

    def step(self, p, k, x, y, turn):
        if p in self.waits:
            self.waits.pop(p)()
        cond, dest = self.aim(x, y, turn)
        rel = (x, y, 0 if turn == 4 else 1)
        when(cond, lambda: self.task(p, k, rel, dest))
        self.sent.append((p, k, x, y, turn))
        if x == y == 0 and turn == 4:
            self.left[p] -= 1
            if not self.left[p]:
                self.then[p]()

    def pump(self):
        self.slot += 1
        last = self.slot == len(SCHEDULE) - 1
        early, self.sent = (self.sent, []) if last else ([], self.sent)
        for code in SCHEDULE[self.slot]:
            p, k = len(MATRICES) - 1 - code // 80, (code // 20) % 4
            x, y, turn = (code // 10) % 2, (code // 5) % 2, code % 5
            self.step(p, k, x, y, turn)
            if p == 0 and k == 2:
                self.step(len(MATRICES), k, x, y, turn)
            for one in early[:4]:
                self.ended(*one)
            early = early[4:]
        self.sent = early + self.sent

    def ended(self, p, k, x, y, turn):
        known, dest = self.aim(x, y, turn)

        def wait():
            rel = (x, y, 0 if turn == 4 else 1)
            for cond, pos, way, to in self.parents(k, rel, dest):
                when(cond, lambda: self.hand(p, k, pos, way, dest, to).wait_send())

        if (x, y, turn) != (0, 0, 4):
            when(known, wait)

    def drain(self):
        for one in self.sent:
            self.ended(*one)


def most_blocks(part, entries):
    return ((entries + 2 * LANES) // LANES - 1) // part.rows + 2


def meeting(part, entries, block):
    start = (part.low + block * part.rows) * LANES
    return quot(start, entries), quot(start + part.rows * LANES - 1, entries)


def first_block(part, entries, flat):
    ahead = entries * flat - part.low * LANES
    return quot(pick(ahead > 0, ahead, 0), part.rows * LANES)


def deliver(place, me, parts, own, land, land_send, land_recv, vec_land, vec_send, vec_recv, local, entries):
    flat, core = place.flat(me), me[CORE]
    mine = block_of(place, me)
    devices = place.devices

    def device(d):
        return (quot(d, place.shape[1]), rest(d, place.shape[1]))

    def block_copy(p, block, to, which):
        part = parts[p]
        slot = block - first_block(part, entries, to)
        return pltpu.make_async_remote_copy(
            src_ref=own[p].at[core, pl.ds(pl.multiple_of(block * part.high, 16), part.high), :],
            dst_ref=land[p].at[slot, core],
            send_sem=land_send.at[p, which],
            recv_sem=land_recv[p].at[slot, core],
            device_id=device(to),
            device_id_type=MESH,
        )

    def block_local(p, block):
        part = parts[p]
        slot = block - first_block(part, entries, flat)
        return pltpu.make_async_copy(
            own[p].at[core, pl.ds(pl.multiple_of(block * part.high, 16), part.high), :],
            land[p].at[slot, core],
            local.at[p],
        )

    def sends(p):
        one, two = meeting(parts[p], entries, mine)
        return [
            (one != flat, one, 0),
            (jnp.logical_and(two != one, two != flat), two, 1),
        ], pick(one == flat, 1, pick(two == flat, 1, 0)) > 0

    def vector_pairs():
        out = []
        for v, (name, j) in enumerate(VECTOR_LIST):
            row = BASES[name] + j
            for d in range((row * LANES) // entries, ((row + 1) * LANES - 1) // entries + 1):
                if (v // 16, d) not in out:
                    out.append((v // 16, d))
        return out

    def vector_copy(n, block, d):
        return pltpu.make_async_remote_copy(
            src_ref=own[4].at[0, block * 16 : (block + 1) * 16, :],
            dst_ref=vec_land.at[block],
            send_sem=vec_send.at[n],
            recv_sem=vec_recv.at[block],
            device_id=device(d),
            device_id_type=MESH,
        )

    def start(p):
        remote, here = sends(p)
        for cond, to, which in remote:
            pl.when(cond)(lambda: block_copy(p, mine, to, which).start())
        pl.when(here)(lambda: block_local(p, mine).start())

    def start_vectors():
        for n, (block, d) in enumerate(vector_pairs()):
            home = place.flat(chip_of(block) + [0])
            if home == d:

                @pl.when(flat == d)
                def _():
                    vec_land[block] = own[4][0, block * 16 : (block + 1) * 16, :]

            else:
                pl.when(flat == home)(lambda: vector_copy(n, block, d).start())

    def expected(p):
        part = parts[p]
        low_block = first_block(part, entries, flat)
        top = part.low + part.rows * place.chips
        begins = part.low * LANES < entries * (flat + 1)
        ends = top * LANES > entries * flat
        for i in range(min(most_blocks(part, entries), place.chips)):
            block = low_block + i
            inside = (part.low + block * part.rows) * LANES < entries * (flat + 1)
            yield both_all(begins, ends, inside, block < place.chips), block, i

    def both_all(*conds):
        return functools.reduce(jnp.logical_and, conds)

    def finish(stage, margin, out):
        base = quot(entries * flat, LANES)
        for p in (3, 2, 1, 0):
            part = parts[p]
            blocks = 2 * part.half // LANES
            remote, here = sends(p)
            pl.when(here)(lambda: block_local(p, mine).wait())
            for cond, block, i in expected(p):

                def take():
                    for half in range(2):
                        source = place.flat(chip_of_traced(block) + [half])

                        @pl.when(source != flat)
                        def _():
                            pltpu.make_async_remote_copy(
                                src_ref=land[p].at[i, half],
                                dst_ref=land[p].at[i, half],
                                send_sem=land_send.at[p, 0],
                                recv_sem=land_recv[p].at[i, half],
                                device_id=device(source),
                                device_id_type=MESH,
                            ).wait_recv()

                    at = part.low + block * part.rows - base + margin
                    for r in range(part.high // 16):
                        for half in range(2):
                            for j in range(blocks // 2):
                                stage[
                                    pl.ds(
                                        at + r * 16 * blocks + half * (blocks // 2) + j,
                                        16,
                                        stride=blocks,
                                    ),
                                    :,
                                ] = land[p][
                                    i, half, r * 16 : (r + 1) * 16, j * LANES : (j + 1) * LANES
                                ].astype(jnp.float32)

                pl.when(cond)(take)
        for n, (block, d) in enumerate(vector_pairs()):
            home = place.flat(chip_of(block) + [0])

            @pl.when(flat == d)
            def _():
                if home != d:
                    vector_copy(n, block, d).wait_recv()
                for v in range(block * 16, min((block + 1) * 16, len(VECTOR_LIST))):
                    name, j = VECTOR_LIST[v]
                    row = BASES[name] + j
                    if (row * LANES) // entries <= d <= ((row + 1) * LANES - 1) // entries:
                        spot = row - (entries * d) // LANES + margin
                        stage[spot : spot + 1, :] = vec_land[block][
                            v % 16 : v % 16 + 1, :
                        ].astype(jnp.float32)

        shift = rest(entries * flat, LANES)
        back = rest(LANES - shift, LANES)
        rows = out.shape[0]

        def turn(i):
            at = pl.ds(pl.multiple_of(margin + i * 16, 16), 16)
            stage[at, :] = pltpu.roll(stage[at, :], back, 1)

        loop(rows // 16 + 1, turn, 8)

        def merge(i):
            lane = lax.broadcasted_iota(jnp.int32, (16, LANES), 1)
            now = stage[pl.ds(margin + i * 16, 16), :]
            after = stage[pl.ds(margin + i * 16 + 1, 16), :]
            out[tile(i), :] = jnp.where(lane < LANES - shift, now, after)

        loop(rows // 16, merge, 8)
        for p in range(4):
            for cond, to, which in sends(p)[0]:
                pl.when(cond)(lambda: block_copy(p, mine, to, which).wait_send())
        for n, (block, d) in enumerate(vector_pairs()):
            home = place.flat(chip_of(block) + [0])
            if home != d:
                pl.when(flat == home)(lambda: vector_copy(n, block, d).wait_send())

    return start, start_vectors, finish


def chip_of_traced(block):
    return [rest(quot(block, 4), 2), quot(block, 8), rest(block, 4)]


SCHEDULE = (
        (),
        (),
        (),
        (76, 48, 71),
        (45,),
        (75, 70),
        (55,),
        (56, 65),
        (115, 87, 136, 85),
        (46, 95, 135, 150, 126, 125, 33),
        (60, 72, 155, 86, 151, 116, 50),
        (5, 127, 40, 35, 78, 130, 97),
        (154, 51, 61, 99, 120, 128),
        (145, 32, 105, 158, 215),
        (159, 90, 49, 98, 15, 66, 112, 88),
        (210, 114, 110, 140, 59, 58, 217, 77, 156),
        (138, 195, 25, 235, 17),
        (111, 16, 73, 131, 121, 62, 96, 19, 230),
        (137, 47, 119, 216, 178, 6, 146),
        (57, 41, 7, 238, 157, 207, 237, 68, 206, 152, 205, 79),
        (141, 219, 233, 118, 122, 218, 139, 193, 225, 67, 37, 236),
        (133, 39, 30, 220, 10, 209, 9),
        (132, 147, 113, 91, 8, 231, 52, 74, 42, 80, 36),
        (53, 200, 117, 199, 92, 134, 69, 221),
        (106, 142, 173, 0, 232, 38, 108, 100, 153),
        (208, 109, 129, 12, 20, 226, 175, 93, 201, 185, 63, 211, 18, 190),
        (11, 222, 107, 223, 176, 81, 196, 26, 31, 43, 179, 168, 101, 197, 278, 191, 28, 166, 227,
     310, 277, 256, 212, 13, 255, 228, 198, 257, 82, 295, 258, 273, 275, 234, 271, 296, 1, 123, 313,
     315, 21, 270, 285, 102, 187, 103, 170, 165, 29, 318, 64, 276, 14, 300, 245, 188, 286, 316, 317,
     203, 239, 2, 169, 250, 311, 298, 252, 279, 23, 290, 192, 305, 3, 180, 83, 265, 186, 177, 202,
     171, 27, 251, 160, 89, 280, 291, 248, 148, 297, 306, 194, 260, 172, 167, 319, 259, 94, 247,
     229, 181, 281, 240, 34, 253, 288, 246, 312, 266, 307, 213, 254, 149, 22, 268, 299, 224, 143,
     274, 161, 272, 182, 301, 241, 124, 214, 292, 293, 287, 174, 261, 308, 54, 162, 267, 183, 289,
     189, 249, 24, 163, 283, 269, 302, 84, 303, 242, 104, 314, 144, 282, 243, 204, 309, 294, 262,
     263, 4, 44, 184, 164, 244, 304, 284, 264),
)
TURNS = ((3, 2, 1, 3, 0), (3, 3, 2, 0, 1))


def stage_margin(parts):
    return max(part.rows for part in parts[:4]) + 16


def even_kernel(place, entries, sz, tokens, cotangent, lengths, table, *refs):
    mats, refs = dict(zip(MATRICES, refs[:4])), refs[4:]
    given, refs = dict(zip(SAVED, refs[:8])), refs[8:]
    out, input_grad, refs = refs[0], refs[1], refs[2:]
    parts = shares(place)
    own, cross, land, refs = refs[:5], refs[5:10], refs[10:14], refs[14:]
    slots, recv = [], []
    for part in parts:
        slots.append(dict(zip(part.parts, refs)))
        refs = refs[len(part.parts) :]
    for part in parts:
        recv.append(dict(zip(part.parts, refs)))
        refs = refs[len(part.parts) :]
    send, cross_send, cross_recv, land_send, refs = *refs[:4], refs[4:]
    land_recv, refs = refs[:4], refs[4:]
    vec_land, vec_send, vec_recv, local, refs = *refs[:4], refs[4:]
    stage, sums, refs = refs[0], refs[1], refs[2:]
    big_a, big_b, refs = refs[0], refs[1], refs[2:]
    wide, slope, qkv, probs, mix, mid, narrow, x, g, temp, blank, partial, load, done = refs
    me = place.coords()
    flat = place.flat(me)
    count = sz.total
    order = (G_NAME, ACT_NAME, W_FC2_NAME, SLOPE_NAME, MLP_IN_NAME, W_FC1_NAME, MID_NAME, MIX_NAME, X_NAME, QKV_NAME, PROBS_NAME)

    def fetches(name):
        sem = load.at[order.index(name)]
        if name in (G_NAME, X_NAME):
            src, dst = (cotangent, g) if name == G_NAME else (tokens, x)
            return [
                pltpu.make_async_copy(
                    src.at[sz.given(b)],
                    dst.at[sz.at(b)],
                    load.at[order.index(name) if b == 0 else len(order) + 10 + 2 * b + (name == G_NAME)],
                )
                for b in range(sz.buffers)
            ]
        return [pltpu.make_async_copy(*places[name], sem)]

    places = {
        ACT_NAME: (given[ACT_NAME], wide),
        SLOPE_NAME: (given[SLOPE_NAME], slope),
        MLP_IN_NAME: (given[MLP_IN_NAME], narrow),
        MID_NAME: (given[MID_NAME], mid),
        MIX_NAME: (given[MIX_NAME], mix),
        QKV_NAME: (given[QKV_NAME], qkv),
        PROBS_NAME: (given[PROBS_NAME], probs),
        W_FC2_NAME: (mats[W_FC2_NAME], big_a),
        W_FC1_NAME: (mats[W_FC1_NAME], big_b),
    }

    def begin(name):
        for c in fetches(name):
            c.start()

    def ready(name):
        for c in fetches(name):
            c.wait()

    for name in order:
        begin(name)
    barrier = pltpu.get_barrier_semaphore()

    def hello(d):
        @pl.when(d != flat)
        def _():
            pl.semaphore_signal(
                barrier,
                inc=1,
                device_id=(quot(d, place.shape[1]), rest(d, place.shape[1])),
                device_id_type=MESH,
            )

    loop(place.devices, hello)
    adding = Summing(
        place, me, parts, own, cross, slots, send, recv, cross_send, cross_recv
    )
    start, start_vectors, finish = deliver(
        place, me, parts, own, land, land_send, land_recv, vec_land, vec_send, vec_recv, local, entries
    )

    def stepped(steps, body, groups):
        each = steps // groups
        for n in range(groups):
            loop(each, lambda i: body(n * each + i))
            adding.pump()

    def sum_to(name, c, value):
        at = SUMS.index(name)
        sums[at : at + 1, c] = value

    def ones():
        return jnp.ones((8, count), jnp.bfloat16)

    def column_sums(name, ref, width):
        def body(c):
            sum_to(name, c, dot(ones(), ref[:, c])[0:1, :])

        columns(width, 256, body)

    def pieces(name, left, right, block, groups):
        p = MATRICES.index(name)
        half = parts[p].half
        steps = parts[p].depth // block

        def body(i):
            first = pl.multiple_of(i * block, block)
            value = low(dot(left[:, pl.ds(first, block)], right(), 0, 0))
            own[p][0, pl.ds(first, block), :] = value[:, :half]
            own[p][1, pl.ds(first, block), :] = value[:, half:]
            adding.swap(p, first, block, i).start()

        waits = lambda: loop(steps, lambda i: adding.swap(p, i * block, block, i).wait_recv())
        adding.offer(p, waits, lambda: start(p))
        stepped(steps, body, groups)
        swaps.append((p, steps, block))

    swaps = []

    ready(G_NAME)
    for b in range(sz.buffers):
        rows = sz.at(b)
        valid = valid_rows(lengths, b, sz.images, sz.rows)
        g[rows, :] = low(g[rows, :].astype(jnp.float32) * valid)
    ready(ACT_NAME)
    column_sums(FC2_BIAS_NAME, g, D)
    pl.semaphore_wait(barrier, place.devices - 1)
    pieces(W_FC2_NAME, wide, lambda: g[...], 256, 1)

    ready(W_FC2_NAME)
    ready(SLOPE_NAME)

    def to_pre(i):
        c = pl.ds(pl.multiple_of(i * 256, 256), 256)
        made = dot(g[...], big_a[c, :], 1, 1)
        wide[:, c] = low(made * slope[:, c].astype(jnp.float32))

    stepped(FF // 256, to_pre, 3)
    late = [
        pltpu.make_async_copy(
            mats[W_QKV_NAME].at[:, i * D : (i + 1) * D],
            big_a.at[i * D : (i + 1) * D],
            load.at[len(order) + 8 + i],
        )
        for i in range(3)
    ]
    late.append(
        pltpu.make_async_copy(mats[W_PROJ_NAME], big_a.at[3 * D : 4 * D], load.at[len(order) + 11])
    )
    for c in reversed(late):
        c.start()
    ready(MLP_IN_NAME)
    column_sums(FC1_BIAS_NAME, wide, FF)
    pieces(W_FC1_NAME, narrow, lambda: wide[...], 128, 3)

    attn_load = pltpu.make_async_copy(given[ATTN_IN_NAME], narrow, load.at[len(order) + 7])
    attn_load.start()
    ready(W_FC1_NAME)

    def to_mlp(i):
        c = pl.ds(pl.multiple_of(i * 256, 256), 256)
        temp[:, c] = dot(wide[...], big_b[c, :], 1, 1)

    stepped(D // 256, to_mlp, 3)
    ready(MID_NAME)

    def folded(v):
        return v[0:8, :] + v[8:16, :]

    def norm_sums(body, gain, bias):
        partial[...] = jnp.zeros(partial.shape, jnp.float32)

        def step(i):
            for which, value in enumerate(body(i)):
                partial[which] += folded(value)

        loop(count // 16, step, 2)
        for which, name in enumerate((gain, bias)):
            at = SUMS.index(name)
            sums[at : at + 1, 0:D] = jnp.sum(partial[which], axis=0, keepdims=True)


    def back_second(i):
        normed, inv = normalize(mid[tile(i), :])
        d = temp[tile(i), :]
        v = g[tile(i), :].astype(jnp.float32) + norm_back(d, normed, inv, vector(table, LN2_GAIN_NAME))
        mid[tile(i), :] = v
        g[tile(i), :] = low(v)
        return d * normed, d

    norm_sums(back_second, LN2_GAIN_NAME, LN2_BIAS_NAME)
    ready(MIX_NAME)
    column_sums(PROJ_BIAS_NAME, g, D)
    adding.pump()
    pieces(W_PROJ_NAME, mix, lambda: g[...], 256, 1)
    late[3].wait()

    def to_mix(i):
        c = pl.ds(pl.multiple_of(i * 256, 256), 256)
        rows = pl.ds(pl.multiple_of(3 * D + i * 256, 256), 256)
        slope[:, c] = low(dot(g[...], big_a[rows, :], 1, 1))

    stepped(D // 256, to_mix, 1)
    ready(QKV_NAME)
    ready(PROBS_NAME)
    for b in range(sz.buffers):
        rows = sz.at(b)

        def attend(p):
            halves = half_lanes(sz.rows)
            at = lambda part: pl.ds(pl.multiple_of(part * D + p * LANES, LANES), LANES)
            q, k, v = (qkv[rows, at(part)] for part in range(3))
            dm = slope[rows, at(0)]
            dq = dk = dv = 0.0
            for h in range(2):
                pr = probs[(b * sz.pairs + p) * 2 + h]
                dmh = dm * halves[h]
                dp = dot(dmh, v, 1, 1)
                prf = pr.astype(jnp.float32)
                ds = low(prf * (dp - jnp.sum(prf * dp, axis=-1, keepdims=True)))
                dv = dv + dot(pr, dmh, 0, 0)
                dq = dq + dot(ds, k * halves[h])
                dk = dk + dot(ds, q * halves[h], 0, 0)
            wide[rows, at(0)] = low(dq * SCALE)
            wide[rows, at(1)] = low(dk * SCALE)
            wide[rows, at(2)] = low(dv)

        stepped(sz.pairs, attend, 3)
    for c in late[:3]:
        c.wait()

    def to_attn(i):
        c = pl.ds(pl.multiple_of(i * 256, 256), 256)
        made = None
        for part in range(3):
            rows = pl.ds(pl.multiple_of(part * D + i * 256, 256), 256)
            term = dot(wide[:, part * D : (part + 1) * D], big_a[rows, :], 1, 1)
            made = term if made is None else made + term
        temp[:, c] = made

    stepped(D // 256, to_attn, 3)
    ready(X_NAME)

    def back_first(i):
        normed, inv = normalize(x[tile(i), :].astype(jnp.float32))
        d = temp[tile(i), :]
        mid[tile(i), :] = mid[tile(i), :] + norm_back(d, normed, inv, vector(table, LN1_GAIN_NAME))
        return d * normed, d

    norm_sums(back_first, LN1_GAIN_NAME, LN1_BIAS_NAME)
    outs = []
    for b in range(sz.buffers):
        outs.append(
            pltpu.make_async_copy(mid.at[sz.at(b)], input_grad.at[sz.given(b)], done.at[2 * b])
        )
        if sz.full > sz.rows:
            blank[...] = jnp.zeros(blank.shape, blank.dtype)
            outs.append(
                pltpu.make_async_copy(
                    blank,
                    input_grad.at[b * sz.full + sz.rows : (b + 1) * sz.full],
                    done.at[2 * b + 1],
                )
            )
    for c in outs:
        c.start()

    attn_load.wait()

    def qv_sums(c):
        wide_sum = dot(ones(), wide[:, c])[0:1, :]
        sums[len(SUMS) : len(SUMS) + 1, c] = wide_sum

    columns(3 * D, 256, qv_sums)
    for name, part in ((Q_BIAS_NAME, 0), (V_BIAS_NAME, 2)):
        at = SUMS.index(name)
        sums[at : at + 1, 0:D] = sums[len(SUMS) : len(SUMS) + 1, part * D : (part + 1) * D]
    own[4][...] = jnp.zeros(own[4].shape, own[4].dtype)
    padded = round_up(len(VECTOR_LIST), 16)
    for v, (name, j) in enumerate(VECTOR_LIST):
        at = SUMS.index(name)
        stage[v : v + 1, :] = sums[at : at + 1, j * LANES : (j + 1) * LANES]
    stage[len(VECTOR_LIST) : padded, :] = jnp.zeros((padded - len(VECTOR_LIST), LANES), jnp.float32)
    own[4][0, 0:padded, :] = low(stage[0:padded, :])
    adding.swap(4, 0, parts[4].depth, 0).start()
    swaps.append((4, 1, parts[4].depth))
    adding.offer(4, lambda: adding.swap(4, 0, parts[4].depth, 0).wait_recv(), start_vectors)
    adding.pump()
    pieces(W_QKV_NAME, narrow, lambda: wide[:, 0 : 3 * D], 128, 3)
    finish(stage, stage_margin(parts), out)
    adding.drain()
    for p, steps, block in swaps:
        loop(steps, lambda i: adding.swap(p, i * block, block, i).wait_send())
    for c in outs:
        c.wait()


def even_backward(place, tokens, cotangent, lengths, mats, saved, table, entries):
    rows = part_rows(entries)
    sz = Sizes(tokens, lengths)
    parts = shares(place)
    dma = pltpu.SemaphoreType.DMA
    plan = slot_plan(place, rows)
    rects = [(part, k) for part in parts for k in part.parts]
    any_spec = pl.BlockSpec(memory_space=pl.ANY)
    vmem = pl.BlockSpec(memory_space=pltpu.VMEM)
    smem = pl.BlockSpec(memory_space=pltpu.SMEM)
    bf, f32 = jnp.bfloat16, jnp.float32
    shapes = saved_shapes(sz)
    scratch = lambda name: pltpu.VMEM(*shapes[name])
    out, input_grad = pl.pallas_call(
        functools.partial(even_kernel, place, entries, sz),
        out_shape=[
            jax.ShapeDtypeStruct((rows, LANES), f32),
            jax.ShapeDtypeStruct(tokens.shape, f32),
        ],
        in_specs=[any_spec, any_spec, smem, vmem] + [any_spec] * 12,
        out_specs=[vmem, any_spec],
        scratch_shapes=[pltpu.VMEM((2, part.depth, part.half), bf) for part in parts]
        + [pltpu.VMEM((part.depth, part.half), bf) for part in parts]
        + [
            pltpu.VMEM((most_blocks(part, entries), 2, part.high, part.half), bf)
            for part in parts[:4]
        ]
        + [
            pltpu.VMEM((plan[k][1], part.parts[k][1], part.parts[k][3]), bf) for part, k in rects
        ]
        + [dma((plan[k][1],)) for _, k in rects]
        + [dma((5, place.classes, place.chips)), dma((5, 12)), dma((5, 12)), dma((4, 2))]
        + [dma((most_blocks(part, entries), 2)) for part in parts[:4]]
        + [
            pltpu.VMEM((-(-len(VECTOR_LIST) // 16), 16, LANES), bf),
            dma((32,)),
            dma((-(-len(VECTOR_LIST) // 16),)),
            dma((4,)),
            pltpu.VMEM((2 * stage_margin(parts) + rows + 32, LANES), f32),
            pltpu.VMEM(TABLE, f32),
            pltpu.VMEM((FF, D), bf),
            pltpu.VMEM((D, FF), bf),
            scratch(ACT_NAME),
            scratch(SLOPE_NAME),
            scratch(QKV_NAME),
            scratch(PROBS_NAME),
            scratch(MIX_NAME),
            scratch(MID_NAME),
            scratch(MLP_IN_NAME),
            pltpu.VMEM((sz.total, D), bf),
            pltpu.VMEM((sz.total, D), bf),
            pltpu.VMEM((sz.total, D), f32),
            pltpu.VMEM((max(8, sz.full - sz.rows), D), f32),
            pltpu.VMEM((2, 8, D), f32),
            pltpu.SemaphoreType.DMA((24 + 2 * sz.buffers,)),
            pltpu.SemaphoreType.DMA((2 * sz.buffers,)),
        ],
        compiler_params=pltpu.CompilerParams(
            collective_id=1, has_side_effects=True, vmem_limit_bytes=67 * 10**6
        ),
        name=BACKWARD_NAME,
    )(tokens, cotangent, lengths, table, *[mats[m] for m in MATRICES], *[saved[s] for s in SAVED])
    return input_grad, out.reshape(-1)[:entries]


def solution(mesh):
    place = Place(mesh)

    def shards(tokens, cotangent, params, lengths):
        mats, saved, table, out = forward(place, tokens, params, lengths)
        input_grad, grad = (even_backward if fits(place) else backward)(
            place, tokens, cotangent, lengths, mats, saved, table, params.shape[0]
        )
        return out, input_grad, grad

    rows, flat = P(AXES, None), P(AXES)
    return jax.shard_map(
        shards,
        mesh=mesh,
        in_specs=(rows, rows, flat, rows),
        out_specs=(rows, rows, flat),
        check_vma=False,
    )
```

```python
import functools
import math

import jax
import jax.numpy as jnp
from jax import lax
from jax.experimental import pallas as pl
from jax.experimental.pallas import tpu as pltpu
from jax.sharding import PartitionSpec as P

ATTN_IN_NAME = "attn_in"
QKV_NAME = "qkv"
PROBS_NAME = "probs"
MIX_NAME = "mix"
MID_NAME = "mid"
MLP_IN_NAME = "mlp_in"
ACT_NAME = "act"
SLOPE_NAME = "slope"
LN1_GAIN_NAME = "ln1_gain"
LN1_BIAS_NAME = "ln1_bias"
W_QKV_NAME = "w_qkv"
Q_BIAS_NAME = "q_bias"
V_BIAS_NAME = "v_bias"
W_PROJ_NAME = "w_proj"
PROJ_BIAS_NAME = "proj_bias"
LN2_GAIN_NAME = "ln2_gain"
LN2_BIAS_NAME = "ln2_bias"
W_FC1_NAME = "w_fc1"
FC1_BIAS_NAME = "fc1_bias"
W_FC2_NAME = "w_fc2"
FC2_BIAS_NAME = "fc2_bias"
G_NAME = "g"
X_NAME = "x"
BACKWARD_NAME = "backward"
AXES = ("dp", "fsdp")
LANES = 128
CORE = 3
MESH = pl.DeviceIdType.MESH


def quot(a, b):
    if isinstance(a, int) and isinstance(b, int):
        return a // b
    return a if isinstance(b, int) and b == 1 else lax.div(a, jnp.int32(b))


def rest(a, b):
    if isinstance(a, int) and isinstance(b, int):
        return a % b
    return lax.rem(a, jnp.int32(b))


def pick(cond, a, b):
    return lax.select(cond, lax.add(jnp.int32(0), a), lax.add(jnp.int32(0), b))


class Place:
    def __init__(self, mesh):
        devs = mesh.devices
        spot = lambda d: (*d.coords, d.core_on_chip)
        self.shape = devs.shape
        self.digits = []
        for axis in range(2):
            line = [spot(devs[i, 0] if axis == 0 else devs[0, i]) for i in range(devs.shape[axis])]
            found, stride = [], 1
            while stride < len(line):
                delta = [b - a for a, b in zip(line[0], line[stride])]
                phys = [p for p in range(4) if delta[p]][0]
                step, size = delta[phys], 1
                while (
                    size * stride < len(line)
                    and line[size * stride][phys] - line[0][phys] == size * step
                    and all(line[size * stride][q] == line[0][q] for q in range(4) if q != phys)
                ):
                    size += 1
                found.append((phys, step, size, stride))
                stride *= size
            self.digits.append(found)
        self.size = [1, 1, 1, 1]
        for found in self.digits:
            for phys, _, size, _ in found:
                self.size[phys] *= size
        self.devices = devs.size
        self.chips = math.prod(self.size[:3])
        long = max(range(3), key=lambda p: self.size[p])
        a, b = [p for p in range(3) if p != long]
        self.orders = ((long, a, b), (long, b, a))
        self.shares = (1, 1)
        if self.chips <= 16:
            self.orders += ((a, long, b), (b, long, a))
            self.shares += (2, 2)
        self.classes = len(self.orders)

    def coords(self):
        index = [lax.axis_index(name) for name in AXES]
        out = [0, 0, 0, 0]
        for axis in range(2):
            for phys, step, size, stride in self.digits[axis]:
                out[phys] = out[phys] + rest(quot(index[axis], stride), size) * step
        return out

    def device(self, coords):
        out = []
        for axis in range(2):
            total = 0
            for phys, step, size, stride in self.digits[axis]:
                total = total + rest(quot(coords[phys], step), size) * stride
            out.append(total)
        return tuple(out)

    def flat(self, coords):
        dp, fsdp = self.device(coords)
        return dp * self.shape[1] + fsdp

    def chip(self, coords):
        return (coords[0] * self.size[1] + coords[1]) * self.size[2] + coords[2]

    def class_rows(self, rows):
        units = rows // 16
        counts = [units * share // sum(self.shares) for share in self.shares]
        counts[-1] += units - sum(counts)
        out, start = [], 0
        for count in counts:
            out.append((start * 16, count * 16))
            start += count
        return out


def flipped(mine, rel, size):
    total, bit = 0, 1
    while bit < size:
        total = total + bit * rest(rest(quot(mine, bit), 2) + rest(quot(rel, bit), 2), 2)
        bit *= 2
    return total


def both(*conds):
    known = [c for c in conds if isinstance(c, bool)]
    if not all(known):
        return False
    rest = [c for c in conds if not isinstance(c, bool)]
    return functools.reduce(jnp.logical_and, rest) if rest else True


def when(cond, fn):
    if isinstance(cond, bool):
        if cond:
            fn()
    else:
        pl.when(cond)(fn)


def moved(coords, dim, by):
    out = list(coords)
    out[dim] = out[dim] + by
    return out


def partner(coords):
    out = list(coords)
    out[CORE] = 1 - out[CORE]
    return out


def neighbours(place, me):
    out = [(True, partner(me))]
    for dim in range(3):
        if place.size[dim] == 1:
            continue
        if place.size[dim] == 2:
            other = list(me)
            other[dim] = 1 - other[dim]
            out.append((True, other))
        else:
            out.append((me[dim] < place.size[dim] - 1, moved(me, dim, 1)))
            out.append((me[dim] > 0, moved(me, dim, -1)))
    return out


def greet(place, me):
    barrier = pltpu.get_barrier_semaphore()
    nbrs = neighbours(place, me)
    for cond, who in nbrs:
        when(
            cond,
            lambda who=who: pl.semaphore_signal(
                barrier, inc=1, device_id=place.device(who), device_id_type=pl.DeviceIdType.MESH
            ),
        )
    peers = sum(1 if cond is True else jnp.where(cond, 1, 0) for cond, _ in nbrs)
    pl.semaphore_wait(barrier, peers)


def onward(place, order, me, rel, src):
    out = []
    for pos in range(3):
        dim = order[pos]
        size = place.size[dim]
        if size == 1:
            continue
        later = [rel[d] == 0 for d in order[pos + 1 :]]
        if size == 2:
            other = list(me)
            other[dim] = 1 - other[dim]
            out.append((both(*later, rel[dim] == 0), pos, 0, other))
        else:
            for way, by in ((0, 1), (1, -1)):
                if by == 1:
                    here = both(me[dim] >= src[dim], me[dim] < size - 1)
                else:
                    here = both(me[dim] <= src[dim], me[dim] > 0)
                cond = both(*later, here)
                out.append((cond, pos, way, moved(me, dim, by)))
    return out


PASSES = (
    0, 16, 32, 48, 1, 17, 40, 33, 52, 49, 41, 56, 3, 8, 2, 20, 35, 34, 10, 53, 18, 28,
    11, 5, 51, 36, 12, 19, 45, 57, 50, 9, 7, 21, 55, 54, 60, 25, 44, 6, 22, 29, 24, 42,
    58, 27, 37, 26, 59, 43, 15, 23, 4, 39, 61, 14, 30, 13, 62, 38, 63, 31, 47, 46,
)


def walk_parts(place, body, reverse=False, after=None):
    if place.size[:3] == [2, 2, 4]:
        for i, code in enumerate(PASSES[::-1] if reverse else PASSES):
            body(code // 16, ((code // 8) % 2, (code // 4) % 2, code % 4))
            if after is not None:
                after(i)
        return

    def each(rel):
        for k in range(place.classes):
            body(k, rel)

    walk(place, each, reverse)
    if after is not None:
        after(None)


def walk(place, body, reverse=False):
    sizes = place.size[:3]
    if place.chips <= 16:
        rels = [
            (x, y, z) for x in range(sizes[0]) for y in range(sizes[1]) for z in range(sizes[2])
        ]
        rels.sort(key=lambda r: (sum(r), r), reverse=reverse)
        for rel in rels:
            body(rel)
        return

    def step(i, carry):
        i = place.chips - 1 - i if reverse else i
        body((i % sizes[0], (i // sizes[0]) % sizes[1], i // (sizes[0] * sizes[1])))
        return carry

    lax.fori_loop(0, place.chips, step, 0)


def source_of(place, me, rel):
    return [flipped(me[d], rel[d], place.size[d]) for d in range(3)] + [me[CORE]]


def gather_all(place, me, held, send, recv, cross, after=None):
    rows = held.shape[1]
    parts = place.class_rows(rows)

    def copy(k, src, slot, sem, who):
        start, count = parts[k]
        ref = held.at[place.flat(src), pl.ds(start, count), :]
        return pltpu.make_async_remote_copy(
            src_ref=ref,
            dst_ref=ref,
            send_sem=send.at[k, place.chip(src), slot],
            recv_sem=sem.at[k, place.chip(src)],
            device_id=place.device(who),
            device_id_type=pl.DeviceIdType.MESH,
        )

    def sends(k, rel, src, act):
        for cond, pos, way, who in onward(place, place.orders[k], me, rel, src):
            when(cond, lambda: act(copy(k, src, pos * 2 + way, recv, who)))
        act(copy(k, src, 6, cross, partner(me)))

    def go(k, rel):
        src = source_of(place, me, rel)
        home = both(*[r == 0 for r in rel])
        if home is not True:
            away = True if home is False else jnp.logical_not(home)
            when(away, lambda: copy(k, src, 0, recv, me).wait_recv())
        sends(k, rel, src, lambda c: c.start())

    walk_parts(place, go, after=after)

    def drain(rel):
        src = source_of(place, me, rel)
        theirs = partner(src)
        for k in range(place.classes):
            sends(k, rel, src, lambda c: c.wait_send())
            copy(k, theirs, 0, cross, me).wait_recv()

    walk(place, drain)


def gather_sems(place):
    return [
        pltpu.SemaphoreType.DMA((place.classes, place.chips, 7)),
        pltpu.SemaphoreType.DMA((place.classes, place.chips)),
        pltpu.SemaphoreType.DMA((place.classes, place.chips)),
    ]


def slot_plan(place, rows):
    plan = []
    for order in place.orders:
        starts, total = [], 0
        for pos in range(3):
            before = math.prod(place.size[d] for d in order[:pos])
            size = place.size[order[pos]]
            starts.append(total)
            total += before * (1 if size == 2 else size + 1 if size > 1 else 0)
        plan.append((starts, total))
    return plan


def slot_of(place, plan, k, pos, way, at, dest):
    order = place.orders[k]
    index = 0
    for d in order[:pos]:
        index = index * place.size[d] + dest[d]
    dim = order[pos]
    size = place.size[dim]
    if size > 2:
        spot = dest[dim]
        if way == 1:
            spot = spot + pick(at[dim] == dest[dim], size - dest[dim], 0)
        index = index * (size + 1) + spot
    return plan[k][0][pos] + index


def add_rows(dst, a, b, count, step=16):
    def body(i, carry):
        r = pl.ds(pl.multiple_of(i * step, step), step)
        dst(r, a(r).astype(jnp.float32) + b(r).astype(jnp.float32))
        return carry

    lax.fori_loop(0, count // step, body, 0)


def scatter_all(place, me, own, cross, slots, total, sems):
    cross_send, cross_recv, send, recv = sems
    rows = own.shape[1]
    parts = place.class_rows(rows)
    plan = slot_plan(place, rows)

    def swap(dest):
        return pltpu.make_async_remote_copy(
            src_ref=own.at[place.flat(partner(dest))],
            dst_ref=cross.at[place.chip(dest)],
            send_sem=cross_send.at[place.chip(dest)],
            recv_sem=cross_recv.at[place.chip(dest)],
            device_id=place.device(partner(me)),
            device_id_type=pl.DeviceIdType.MESH,
        )

    def pass_on(k, pos, way, dest, to):
        start, count = parts[k]
        slot = slot_of(place, plan, k, pos, way, to, dest)
        return pltpu.make_async_remote_copy(
            src_ref=own.at[place.flat(dest), pl.ds(start, count), :],
            dst_ref=slots[k].at[slot],
            send_sem=send.at[k, place.chip(dest)],
            recv_sem=recv[k].at[slot],
            device_id=place.device(to),
            device_id_type=pl.DeviceIdType.MESH,
        )

    def parents(k, rel, dest):
        order = place.orders[k]
        out = []
        for pos in range(3):
            dim = order[pos]
            size = place.size[dim]
            if size == 1:
                continue
            later = both(*[rel[d] == 0 for d in order[pos + 1 :]])
            if size == 2:
                other = list(me)
                other[dim] = 1 - other[dim]
                away = rel[dim] == 1
                out.append((both(later, away), pos, 0, other))
            else:
                out.append((both(later, me[dim] > dest[dim]), pos, 0, moved(me, dim, -1)))
                out.append((both(later, me[dim] < dest[dim]), pos, 1, moved(me, dim, 1)))
        return out

    walk(place, lambda rel: swap(source_of(place, me, rel)).start(), reverse=True)

    def go(rel):
        dest = source_of(place, me, rel)
        home = both(*[r == 0 for r in rel])
        flat, chip = place.flat(dest), place.chip(dest)
        swap(dest).wait_recv()

        def mix(final):
            for k in range(place.classes):
                start, count = parts[k]

                def rows_of(r):
                    return pl.ds(r.start + start, r.size)

                if final:

                    def put(r, v):
                        total[rows_of(r), :] = v

                    def held(r):
                        return total[rows_of(r), :]

                else:

                    def put(r, v):
                        own[flat, rows_of(r), :] = v.astype(own.dtype)

                    def held(r):
                        return own[flat, rows_of(r), :]

                add_rows(
                    put,
                    lambda r: own[flat, rows_of(r), :],
                    lambda r: cross[chip, rows_of(r), :],
                    count,
                )
                for cond, pos, way, who in onward(place, place.orders[k], me, rel, dest):

                    def take():
                        slot = slot_of(place, plan, k, pos, way, me, dest)
                        pass_on(k, pos, way, dest, me).wait_recv()
                        add_rows(put, held, lambda r: slots[k][slot, r, :], count)

                    when(cond, take)
                if not final:
                    for cond, pos, way, who in parents(k, rel, dest):
                        when(cond, lambda: pass_on(k, pos, way, dest, who).start())

        if isinstance(home, bool):
            mix(home)
        else:
            pl.when(home)(lambda: mix(True))
            pl.when(jnp.logical_not(home))(lambda: mix(False))

    walk(place, go, reverse=True)

    def drain(rel):
        dest = source_of(place, me, rel)
        swap(dest).wait_send()
        for k in range(place.classes):
            for cond, pos, way, who in parents(k, rel, dest):
                when(cond, lambda: pass_on(k, pos, way, dest, who).wait_send())

    walk(place, drain)


def scatter_scratch(place, rows):
    parts = place.class_rows(rows)
    plan = slot_plan(place, rows)
    dma = pltpu.SemaphoreType.DMA
    return (
        [pltpu.VMEM((place.chips, rows, LANES), jnp.bfloat16)],
        [pltpu.VMEM((plan[k][1], parts[k][1], LANES), jnp.bfloat16) for k in range(place.classes)],
        [dma((place.chips,)), dma((place.chips,)), dma((place.classes, place.chips))],
        [dma((plan[k][1],)) for k in range(place.classes)],
    )


D = 768
HEAD_DIM = 64
FF = 3072
EPSILON = 1e-06
NEG_FILL = -1e30
ROOT_HALF = 0.7071067811865476
INV_ROOT_TWO_PI = 0.3989422804014327

PIECES = (
    (LN1_GAIN_NAME, (D,)),
    (LN1_BIAS_NAME, (D,)),
    (W_QKV_NAME, (D, 3 * D)),
    (Q_BIAS_NAME, (D,)),
    (V_BIAS_NAME, (D,)),
    (W_PROJ_NAME, (D, D)),
    (PROJ_BIAS_NAME, (D,)),
    (LN2_GAIN_NAME, (D,)),
    (LN2_BIAS_NAME, (D,)),
    (W_FC1_NAME, (D, FF)),
    (FC1_BIAS_NAME, (FF,)),
    (W_FC2_NAME, (FF, D)),
    (FC2_BIAS_NAME, (D,)),
)
MATRICES = tuple(name for name, shape in PIECES if len(shape) == 2)
VECTORS = tuple(name for name, shape in PIECES if len(shape) == 1)
SHAPES = dict(PIECES)


def row_bases():
    bases, row = {}, 0
    for name, shape in PIECES:
        bases[name] = row
        row += math.prod(shape) // LANES
    return bases, row


BASES, TOTAL_ROWS = row_bases()
IMAGE_MAX = 98
QKV_BIAS = len(VECTORS)
TABLE = (16, FF)


def part_rows(entries):
    return -(-((LANES - 1 + entries - 1) // LANES + 1) // 16) * 16


def tile(i):
    return pl.ds(pl.multiple_of(i * 16, 16), 16)


def loop(count, body, unroll=1):
    def step(i, carry):
        for u in range(unroll):
            body(i * unroll + u)
        return carry

    whole = count // unroll
    if whole:
        lax.fori_loop(0, whole, step, 0)
    for i in range(whole * unroll, count):
        body(i)


def aligned(raw, held, stage, which, entries):
    rows = held.shape[1]
    shift = (entries * which) % LANES
    stage[0:8, :] = jnp.zeros((8, LANES), jnp.float32)

    def turn(i):
        stage[pl.ds(pl.multiple_of(i * 16 + 8, 8), 16), :] = pltpu.roll(
            raw[tile(i), :].astype(jnp.float32), shift, 1
        )

    loop(rows // 16, turn, 8)

    def merge(i):
        lane = lax.broadcasted_iota(jnp.int32, (16, LANES), 1)
        now = stage[pl.ds(i * 16 + 8, 16), :]
        before = stage[pl.ds(i * 16 + 7, 16), :]
        held[which, tile(i), :] = jnp.where(lane < shift, before, now).astype(held.dtype)

    loop(rows // 16, merge, 8)


def round_up(value, unit):
    return -(-value // unit) * unit


class Span:
    def __init__(self, low, high, name, first, depth, vectors):
        self.low, self.high = low, high
        self.name, self.first, self.depth = name, first, depth
        self.vectors = vectors


def spans(cuts):
    out, row, early = [], 0, []
    for name, shape in PIECES:
        count = math.prod(shape) // LANES
        if len(shape) == 1:
            if out:
                out[-1].vectors.append(name)
                out[-1].high = row + count
            else:
                early.append(name)
        else:
            depth = shape[0] // cuts[name]
            blocks = shape[1] // LANES
            for c in range(cuts[name]):
                start = row + c * depth * blocks
                span = Span(start, start + depth * blocks, name, c * depth, depth, [])
                if not out:
                    span.low, span.vectors = 0, early
                out.append(span)
        row += count
    return out


GATHER_SPANS = spans({name: 1 for name in MATRICES})
SCATTER_SPANS = spans({W_QKV_NAME: 2, W_PROJ_NAME: 1, W_FC1_NAME: 2, W_FC2_NAME: 2})


def stage_rows(spans_, rows):
    return round_up(max(s.high - s.low for s in spans_), 16) + 2 * rows + 32


def owners(span, entries):
    return (span.low * LANES) // entries, (span.high * LANES - 1) // entries


def spread(held, stage, span, entries):
    rows = held.shape[1]
    low, high = owners(span, entries)

    def one(i):
        d = low + i
        base = (entries * d) // LANES - span.low + rows
        cut = (entries * d) % LANES
        first = stage[pl.ds(base, 1), :]

        def body(t):
            stage[pl.ds(base + t * 16, 16), :] = held[d, tile(t), :].astype(jnp.float32)

        loop(rows // 16, body, 8)
        row = stage[pl.ds(base, 1), :]
        stage[pl.ds(base, 1), :] = jnp.where(cut != 0, row + first, row)

    loop(high - low + 1, one)


def form(stage, span, margin, out):
    blocks = SHAPES[span.name][1] // LANES
    base = margin + BASES[span.name] + span.first * blocks - span.low

    def body(i):
        for j in range(blocks):
            out[tile(i + span.first // 16), j * LANES : (j + 1) * LANES] = stage[
                pl.ds(base + i * 16 * blocks + j, 16, stride=blocks), :
            ].astype(out.dtype)

    loop(span.depth // 16, body, max(1, 24 // blocks))


def vector_rows(stage, span, margin, table):
    for name in span.vectors:
        at = margin + BASES[name] - span.low
        row = VECTORS.index(name)
        for j in range(SHAPES[name][0] // LANES):
            table[row : row + 1, j * LANES : (j + 1) * LANES] = stage[at + j : at + j + 1, :]


def vector(table, name):
    row = VECTORS.index(name)
    return table[row : row + 1, 0 : SHAPES[name][0]]


def lay(stage, span, margin, first, value):
    blocks = SHAPES[span.name][1] // LANES
    base = margin + BASES[span.name] - span.low + first * blocks
    for i in range(value.shape[0] // 16):
        for j in range(blocks):
            stage[pl.ds(base + i * 16 * blocks + j, 16, stride=blocks), :] = value[
                i * 16 : (i + 1) * 16, j * LANES : (j + 1) * LANES
            ]


def lay_vectors(stage, span, margin, table):
    for name in span.vectors:
        at = margin + BASES[name] - span.low
        row = VECTORS.index(name)
        for j in range(SHAPES[name][0] // LANES):
            stage[at + j : at + j + 1, :] = table[row : row + 1, j * LANES : (j + 1) * LANES]


def cut(stage, span, own, entries):
    rows = own.shape[1]
    low, high = owners(span, entries)

    def whole(d):
        base = (entries * d) // LANES - span.low + rows

        def body(t):
            own[d, tile(t), :] = stage[pl.ds(base + t * 16, 16), :].astype(own.dtype)

        loop(rows // 16, body, 8)

    def edge(d):
        base = (entries * d) // LANES - span.low + rows

        def body(t):
            now = stage[pl.ds(base + t * 16, 16), :]
            row = base + t * 16 - rows + lax.broadcasted_iota(jnp.int32, (16, LANES), 0)
            inside = jnp.logical_and(row >= 0, row < span.high - span.low)
            before = own[d, tile(t), :].astype(jnp.float32)
            own[d, tile(t), :] = jnp.where(inside, now, before).astype(own.dtype)

        loop(rows // 16, body, 8)

    edge(low)
    if high - low > 1:
        loop(high - low - 1, lambda i: whole(low + 1 + i))
    if high > low:
        edge(high)


def mean_of(v):
    return jnp.sum(v, axis=-1, keepdims=True) * (1.0 / v.shape[-1])


def normalize(v):
    centred = v - mean_of(v)
    inv_std = lax.rsqrt(mean_of(centred * centred) + EPSILON)
    return centred * inv_std, inv_std


def norm_back(grad_out, normed, inv_std, gain):
    grad_norm = grad_out * gain
    return inv_std * (grad_norm - mean_of(grad_norm) - normed * mean_of(grad_norm * normed))


def dot(a, b, left=1, right=0):
    return lax.dot_general(
        a, b, (((left,), (right,)), ((), ())), preferred_element_type=jnp.float32
    )


def columns(width, block, body):
    loop(width // block, lambda i: body(pl.ds(pl.multiple_of(i * block, block), block)))


def segments(lengths, b, images, shape, dim):
    position = lax.broadcasted_iota(jnp.int32, shape, dim)
    total, seg = 0, jnp.zeros(shape, jnp.int32)
    for i in range(images):
        total = total + lengths[b, i]
        seg = seg + jnp.where(position >= total, 1, 0)
    return seg


def valid_rows(lengths, b, images, count):
    return jnp.where(segments(lengths, b, images, (count, 1), 0) < images, 1.0, 0.0)


class Sizes:
    def __init__(self, tokens, lengths):
        self.buffers, self.images = lengths.shape
        self.full = tokens.shape[0] // self.buffers
        self.rows = min(self.full, round_up(self.images * IMAGE_MAX, 16))
        self.total = self.rows * self.buffers
        self.pairs = D // LANES

    def at(self, b):
        return slice(b * self.rows, (b + 1) * self.rows)

    def given(self, b):
        return slice(b * self.full, b * self.full + self.rows)


def low(v):
    return v.astype(jnp.bfloat16)


def half_lanes(rows):
    lane = lax.broadcasted_iota(jnp.int32, (rows, LANES), 1)
    first = low(jnp.where(lane < HEAD_DIM, 1.0, 0.0))
    return first, low(jnp.where(lane < HEAD_DIM, 0.0, 1.0))


SCALE = 1.0 / math.sqrt(HEAD_DIM)
SAVED = (ATTN_IN_NAME, QKV_NAME, PROBS_NAME, MIX_NAME, MID_NAME, MLP_IN_NAME, ACT_NAME, SLOPE_NAME)


def saved_shapes(sz):
    t = sz.total
    bf = jnp.bfloat16
    return {
        ATTN_IN_NAME: ((t, D), bf),
        QKV_NAME: ((t, 3 * D), bf),
        PROBS_NAME: ((sz.buffers * sz.pairs * 2, sz.rows, sz.rows), bf),
        MIX_NAME: ((t, D), bf),
        MID_NAME: ((t, D), jnp.float32),
        MLP_IN_NAME: ((t, D), bf),
        ACT_NAME: ((t, FF), bf),
        SLOPE_NAME: ((t, FF), bf),
    }


def forward_kernel(place, entries, sz, raw, tokens, lengths, *refs):
    mats, refs = dict(zip(MATRICES, refs[:4])), refs[4:]
    out_saved, refs = dict(zip(SAVED, refs[:8])), refs[8:]
    table, block_out, refs = refs[0], refs[1], refs[2:]
    held, stage, refs = refs[0], refs[1], refs[2:]
    w, refs = dict(zip(MATRICES, refs[:4])), refs[4:]
    a, refs = dict(zip(SAVED, refs[:8])), refs[8:]
    normed = refs[0]
    send, recv, cross, done_w, done_a = refs[1:]
    me = place.coords()
    margin = held.shape[1]

    aligned(raw, held, stage, place.flat(me), entries)
    greet(place, me)

    def norm_first(i):
        for b in range(sz.buffers):
            x = tokens[pl.ds(pl.multiple_of(b * sz.full + i * 16, 16), 16), :].astype(jnp.float32)
            normed[pl.ds(pl.multiple_of(b * sz.rows + i * 16, 16), 16), :] = normalize(x)[0]

    def after(i):
        if i is None or i == 8:
            loop(sz.rows // 16, norm_first)

    gather_all(place, me, held, send, recv, cross, after)

    def keep(name):
        pltpu.make_async_copy(a[name], out_saved[name], done_a.at[SAVED.index(name)]).start()

    for span in GATHER_SPANS:
        name = span.name
        spread(held, stage, span, entries)
        form(stage, span, margin, w[name])
        vector_rows(stage, span, margin, table)
        m = MATRICES.index(name)
        pltpu.make_async_copy(w[name], mats[name], done_w.at[m]).start()
    table[QKV_BIAS : QKV_BIAS + 1, 0:D] = vector(table, Q_BIAS_NAME)
    table[QKV_BIAS : QKV_BIAS + 1, D : 2 * D] = jnp.zeros((1, D), jnp.float32)
    table[QKV_BIAS : QKV_BIAS + 1, 2 * D : 3 * D] = vector(table, V_BIAS_NAME)

    def scale_first(i):
        a[ATTN_IN_NAME][tile(i), :] = low(
            normed[tile(i), :] * vector(table, LN1_GAIN_NAME) + vector(table, LN1_BIAS_NAME)
        )

    loop(sz.total // 16, scale_first)
    keep(ATTN_IN_NAME)

    def to_qkv(c):
        a[QKV_NAME][:, c] = low(
            dot(a[ATTN_IN_NAME][...], w[W_QKV_NAME][:, c]) + table[QKV_BIAS : QKV_BIAS + 1, c]
        )

    columns(3 * D, 256, to_qkv)
    keep(QKV_NAME)

    qkv, probs, mix = a[QKV_NAME], a[PROBS_NAME], a[MIX_NAME]
    for b in range(sz.buffers):
        rows = sz.at(b)
        seg_r = segments(lengths, b, sz.images, (sz.rows, 1), 0)
        seg_c = segments(lengths, b, sz.images, (1, sz.rows), 1)

        def attend(p):
            halves = half_lanes(sz.rows)
            at = lambda part: pl.ds(pl.multiple_of(part * D + p * LANES, LANES), LANES)
            q, k, v = (qkv[rows, at(part)] for part in range(3))
            mixed = None
            for h in range(2):
                s = dot(q * (halves[h] * SCALE).astype(q.dtype), k, 1, 1)
                s = jnp.where(seg_r == seg_c, s, NEG_FILL)
                e = jnp.exp(s - jnp.max(s, axis=-1, keepdims=True))
                pr = low(e * (1.0 / jnp.sum(e, axis=-1, keepdims=True)))
                probs[(b * sz.pairs + p) * 2 + h] = pr
                part = dot(pr, v * halves[h])
                mixed = part if mixed is None else mixed + part
            mix[rows, at(0)] = low(mixed)

        loop(sz.pairs, attend)
    keep(PROBS_NAME)
    keep(MIX_NAME)

    def to_mid(c):
        made = dot(mix[...], w[W_PROJ_NAME][:, c]) + table[
            VECTORS.index(PROJ_BIAS_NAME) : VECTORS.index(PROJ_BIAS_NAME) + 1, c
        ]
        for b in range(sz.buffers):
            a[MID_NAME][sz.at(b), c] = (
                tokens[sz.given(b), c].astype(jnp.float32) + made[sz.at(b), :]
            )

    columns(D, 256, to_mid)
    keep(MID_NAME)

    def norm_second(i):
        a[MLP_IN_NAME][tile(i), :] = low(
            normalize(a[MID_NAME][tile(i), :])[0] * vector(table, LN2_GAIN_NAME)
            + vector(table, LN2_BIAS_NAME)
        )

    loop(sz.total // 16, norm_second)
    keep(MLP_IN_NAME)

    def to_act(c):
        at = VECTORS.index(FC1_BIAS_NAME)
        pre = dot(a[MLP_IN_NAME][...], w[W_FC1_NAME][:, c]) + table[at : at + 1, c]
        phi = 0.5 * (1.0 + lax.erf(pre * ROOT_HALF))
        a[ACT_NAME][:, c] = low(pre * phi)
        a[SLOPE_NAME][:, c] = low(phi + pre * jnp.exp(-0.5 * pre * pre) * INV_ROOT_TWO_PI)

    columns(FF, 256, to_act)
    keep(ACT_NAME)
    keep(SLOPE_NAME)

    def to_out(c):
        at = VECTORS.index(FC2_BIAS_NAME)
        made = dot(a[ACT_NAME][...], w[W_FC2_NAME][:, c]) + table[at : at + 1, c]
        for b in range(sz.buffers):
            valid = valid_rows(lengths, b, sz.images, sz.rows)
            block_out[sz.given(b), c] = low(valid * (a[MID_NAME][sz.at(b), c] + made[sz.at(b), :]))
            if sz.full > sz.rows:
                block_out[b * sz.full + sz.rows : (b + 1) * sz.full, c] = jnp.zeros(
                    (sz.full - sz.rows, made.shape[1]), jnp.bfloat16
                )

    columns(D, 256, to_out)
    for m, name in enumerate(MATRICES):
        pltpu.make_async_copy(w[name], mats[name], done_w.at[m]).wait()
    for i, name in enumerate(SAVED):
        pltpu.make_async_copy(a[name], out_saved[name], done_a.at[i]).wait()


def forward(place, tokens, params, lengths):
    entries = params.shape[0]
    rows = part_rows(entries)
    sz = Sizes(tokens, lengths)
    raw = jnp.pad(params, (0, rows * LANES - entries)).reshape(rows, LANES)
    any_spec = pl.BlockSpec(memory_space=pl.ANY)
    vmem = pl.BlockSpec(memory_space=pltpu.VMEM)
    smem = pl.BlockSpec(memory_space=pltpu.SMEM)
    saved = saved_shapes(sz)
    bf = jnp.bfloat16
    outs = pl.pallas_call(
        functools.partial(forward_kernel, place, entries, sz),
        out_shape=[jax.ShapeDtypeStruct(SHAPES[n], bf) for n in MATRICES]
        + [jax.ShapeDtypeStruct(*saved[n]) for n in SAVED]
        + [jax.ShapeDtypeStruct(TABLE, jnp.float32), jax.ShapeDtypeStruct(tokens.shape, bf)],
        in_specs=[vmem, vmem, smem],
        out_specs=[any_spec] * 12 + [vmem, vmem],
        scratch_shapes=[
            pltpu.VMEM((place.devices, rows, LANES), bf),
            pltpu.VMEM((stage_rows(GATHER_SPANS, rows), LANES), jnp.float32),
        ]
        + [pltpu.VMEM(SHAPES[n], bf) for n in MATRICES]
        + [pltpu.VMEM(*saved[n]) for n in SAVED]
        + [pltpu.VMEM((sz.total, D), jnp.float32)]
        + gather_sems(place)
        + [pltpu.SemaphoreType.DMA((4,)), pltpu.SemaphoreType.DMA((8,))],
        compiler_params=pltpu.CompilerParams(
            collective_id=0, has_side_effects=True, vmem_limit_bytes=67 * 10**6
        ),
        name="forward",
    )(raw, tokens, lengths)
    return dict(zip(MATRICES, outs[:4])), dict(zip(SAVED, outs[4:12])), outs[12], outs[13]


SUMS = tuple(VECTORS)


def backward_kernel(place, entries, sz, tokens, cotangent, lengths, table, *refs):
    mats, refs = dict(zip(MATRICES, refs[:4])), refs[4:]
    given, refs = dict(zip(SAVED, refs[:8])), refs[8:]
    out, input_grad, refs = refs[0], refs[1], refs[2:]
    own, cross, refs = refs[0], refs[1], refs[2:]
    n = place.classes
    slots, refs = refs[:n], refs[n:]
    cross_send, cross_recv, send = refs[:3]
    recv, refs = refs[3 : 3 + n], refs[3 + n :]
    stage, total, sums, refs = refs[0], refs[1], refs[2], refs[3:]
    big_a, big_b, refs = refs[0], refs[1], refs[2:]
    wide, slope, qkv, probs, mix, mid, narrow, x, g, temp, blank, load, done = refs
    me = place.coords()
    margin = own.shape[1]
    count = sz.total
    order = (G_NAME, ACT_NAME, W_FC2_NAME, SLOPE_NAME, MLP_IN_NAME, W_FC1_NAME, MID_NAME, MIX_NAME, X_NAME, QKV_NAME, PROBS_NAME)

    def fetches(name):
        sem = load.at[order.index(name)]
        if name in (G_NAME, X_NAME):
            src, dst = (cotangent, g) if name == G_NAME else (tokens, x)
            return [
                pltpu.make_async_copy(
                    src.at[sz.given(b)],
                    dst.at[sz.at(b)],
                    load.at[order.index(name) if b == 0 else len(order) + 10 + 2 * b + (name == G_NAME)],
                )
                for b in range(sz.buffers)
            ]
        return [pltpu.make_async_copy(*places[name], sem)]

    places = {
        ACT_NAME: (given[ACT_NAME], wide),
        SLOPE_NAME: (given[SLOPE_NAME], slope),
        MLP_IN_NAME: (given[MLP_IN_NAME], narrow),
        MID_NAME: (given[MID_NAME], mid),
        MIX_NAME: (given[MIX_NAME], mix),
        QKV_NAME: (given[QKV_NAME], qkv),
        PROBS_NAME: (given[PROBS_NAME], probs),
        W_FC2_NAME: (mats[W_FC2_NAME], big_a),
        W_FC1_NAME: (mats[W_FC1_NAME], big_b),
    }

    def begin(name):
        for c in fetches(name):
            c.start()

    def ready(name):
        for c in fetches(name):
            c.wait()

    for name in order:
        begin(name)
    greet(place, me)

    def sum_to(name, c, value):
        at = SUMS.index(name)
        sums[at : at + 1, c] = value

    def ones():
        return jnp.ones((8, count), jnp.bfloat16)

    def column_sums(name, ref, width):
        def body(c):
            sum_to(name, c, dot(ones(), ref[:, c])[0:1, :])

        columns(width, 256, body)

    def pieces(name, left, right, block):
        for span in [s for s in SCATTER_SPANS if s.name == name]:

            def body(i):
                first = pl.multiple_of(span.first + i * block, block)
                lay(stage, span, margin, first, dot(left[:, pl.ds(first, block)], right(), 0, 0))

            loop(span.depth // block, body)
            yield span

    def finish(span):
        lay_vectors(stage, span, margin, sums)
        cut(stage, span, own, entries)

    ready(G_NAME)
    for b in range(sz.buffers):
        rows = sz.at(b)
        valid = valid_rows(lengths, b, sz.images, sz.rows)
        g[rows, :] = low(g[rows, :].astype(jnp.float32) * valid)
    ready(ACT_NAME)
    column_sums(FC2_BIAS_NAME, g, D)
    for span in pieces(W_FC2_NAME, wide, lambda: g[...], 256):
        finish(span)

    ready(W_FC2_NAME)
    ready(SLOPE_NAME)

    def to_pre(i):
        c = pl.ds(pl.multiple_of(i * 256, 256), 256)
        made = dot(g[...], big_a[c, :], 1, 1)
        wide[:, c] = low(made * slope[:, c].astype(jnp.float32))

    loop(FF // 256, to_pre)
    late = [
        pltpu.make_async_copy(
            mats[W_QKV_NAME].at[:, i * D : (i + 1) * D],
            big_a.at[i * D : (i + 1) * D],
            load.at[len(order) + 8 + i],
        )
        for i in range(3)
    ]
    late.append(
        pltpu.make_async_copy(mats[W_PROJ_NAME], big_a.at[3 * D : 4 * D], load.at[len(order) + 11])
    )
    for c in reversed(late):
        c.start()
    ready(MLP_IN_NAME)
    column_sums(FC1_BIAS_NAME, wide, FF)
    for span in pieces(W_FC1_NAME, narrow, lambda: wide[...], 128):
        finish(span)

    attn_load = pltpu.make_async_copy(given[ATTN_IN_NAME], narrow, load.at[len(order) + 7])
    attn_load.start()
    ready(W_FC1_NAME)

    def to_mlp(i):
        c = pl.ds(pl.multiple_of(i * 256, 256), 256)
        temp[:, c] = dot(wide[...], big_b[c, :], 1, 1)

    loop(D // 256, to_mlp)
    ready(MID_NAME)

    def column_add(name, value, first):
        at = SUMS.index(name)
        part = jnp.sum(value, axis=0, keepdims=True)
        before = sums[at : at + 1, 0:D]
        sums[at : at + 1, 0:D] = part if first else before + part

    def clear(name):
        at = SUMS.index(name)
        sums[at : at + 1, 0:D] = jnp.zeros((1, D), jnp.float32)

    clear(LN2_GAIN_NAME)
    clear(LN2_BIAS_NAME)

    def back_second(i):
        normed, inv = normalize(mid[tile(i), :])
        d = temp[tile(i), :]
        column_add(LN2_GAIN_NAME, d * normed, False)
        column_add(LN2_BIAS_NAME, d, False)
        v = g[tile(i), :].astype(jnp.float32) + norm_back(d, normed, inv, vector(table, LN2_GAIN_NAME))
        mid[tile(i), :] = v
        g[tile(i), :] = low(v)

    loop(count // 16, back_second)
    ready(MIX_NAME)
    column_sums(PROJ_BIAS_NAME, g, D)
    for span in pieces(W_PROJ_NAME, mix, lambda: g[...], 256):
        finish(span)
    late[3].wait()

    def to_mix(i):
        c = pl.ds(pl.multiple_of(i * 256, 256), 256)
        rows = pl.ds(pl.multiple_of(3 * D + i * 256, 256), 256)
        slope[:, c] = low(dot(g[...], big_a[rows, :], 1, 1))

    loop(D // 256, to_mix)
    ready(QKV_NAME)
    ready(PROBS_NAME)
    for b in range(sz.buffers):
        rows = sz.at(b)

        def attend(p):
            halves = half_lanes(sz.rows)
            at = lambda part: pl.ds(pl.multiple_of(part * D + p * LANES, LANES), LANES)
            q, k, v = (qkv[rows, at(part)] for part in range(3))
            dm = slope[rows, at(0)]
            dq = dk = dv = 0.0
            for h in range(2):
                pr = probs[(b * sz.pairs + p) * 2 + h]
                dmh = dm * halves[h]
                dp = dot(dmh, v, 1, 1)
                prf = pr.astype(jnp.float32)
                ds = low(prf * (dp - jnp.sum(prf * dp, axis=-1, keepdims=True)))
                dv = dv + dot(pr, dmh, 0, 0)
                dq = dq + dot(ds, k * halves[h])
                dk = dk + dot(ds, q * halves[h], 0, 0)
            wide[rows, at(0)] = low(dq * SCALE)
            wide[rows, at(1)] = low(dk * SCALE)
            wide[rows, at(2)] = low(dv)

        loop(sz.pairs, attend)
    for c in late[:3]:
        c.wait()

    def to_attn(i):
        c = pl.ds(pl.multiple_of(i * 256, 256), 256)
        made = None
        for part in range(3):
            rows = pl.ds(pl.multiple_of(part * D + i * 256, 256), 256)
            term = dot(wide[:, part * D : (part + 1) * D], big_a[rows, :], 1, 1)
            made = term if made is None else made + term
        temp[:, c] = made

    loop(D // 256, to_attn)
    ready(X_NAME)
    clear(LN1_GAIN_NAME)
    clear(LN1_BIAS_NAME)

    def back_first(i):
        normed, inv = normalize(x[tile(i), :].astype(jnp.float32))
        d = temp[tile(i), :]
        column_add(LN1_GAIN_NAME, d * normed, False)
        column_add(LN1_BIAS_NAME, d, False)
        mid[tile(i), :] = mid[tile(i), :] + norm_back(d, normed, inv, vector(table, LN1_GAIN_NAME))

    loop(count // 16, back_first)
    outs = []
    for b in range(sz.buffers):
        outs.append(
            pltpu.make_async_copy(mid.at[sz.at(b)], input_grad.at[sz.given(b)], done.at[2 * b])
        )
        if sz.full > sz.rows:
            blank[...] = jnp.zeros(blank.shape, blank.dtype)
            outs.append(
                pltpu.make_async_copy(
                    blank,
                    input_grad.at[b * sz.full + sz.rows : (b + 1) * sz.full],
                    done.at[2 * b + 1],
                )
            )
    for c in outs:
        c.start()

    attn_load.wait()

    def qv_sums(c):
        wide_sum = dot(ones(), wide[:, c])[0:1, :]
        sums[len(SUMS) : len(SUMS) + 1, c] = wide_sum

    columns(3 * D, 256, qv_sums)
    for name, part in ((Q_BIAS_NAME, 0), (V_BIAS_NAME, 2)):
        at = SUMS.index(name)
        sums[at : at + 1, 0:D] = sums[len(SUMS) : len(SUMS) + 1, part * D : (part + 1) * D]
    for span in pieces(W_QKV_NAME, narrow, lambda: wide[:, 0 : 3 * D], 128):
        finish(span)

    scatter_all(place, me, own, cross, slots, total, (cross_send, cross_recv, send, recv))
    shift = (entries * place.flat(me)) % LANES
    back = (LANES - shift) % LANES
    rows = own.shape[1]

    def turn(i):
        total[tile(i), :] = pltpu.roll(total[tile(i), :], back, 1)

    loop(rows // 16, turn, 8)

    def merge(i):
        lane = lax.broadcasted_iota(jnp.int32, (16, LANES), 1)
        now = total[pl.ds(i * 16, 16), :]
        after = total[pl.ds(i * 16 + 1, 16), :]
        out[tile(i), :] = jnp.where(lane < LANES - shift, now, after)

    loop(rows // 16, merge, 8)
    for c in outs:
        c.wait()


def backward(place, tokens, cotangent, lengths, mats, saved, table, entries):
    rows = part_rows(entries)
    sz = Sizes(tokens, lengths)
    cross, slots, sems, recv = scatter_scratch(place, rows)
    any_spec = pl.BlockSpec(memory_space=pl.ANY)
    vmem = pl.BlockSpec(memory_space=pltpu.VMEM)
    smem = pl.BlockSpec(memory_space=pltpu.SMEM)
    bf, f32 = jnp.bfloat16, jnp.float32
    shapes = saved_shapes(sz)
    scratch = lambda name: pltpu.VMEM(*shapes[name])
    out, input_grad = pl.pallas_call(
        functools.partial(backward_kernel, place, entries, sz),
        out_shape=[
            jax.ShapeDtypeStruct((rows, LANES), f32),
            jax.ShapeDtypeStruct(tokens.shape, f32),
        ],
        in_specs=[any_spec, any_spec, smem, vmem] + [any_spec] * 12,
        out_specs=[vmem, any_spec],
        scratch_shapes=[pltpu.VMEM((place.devices, rows, LANES), bf)]
        + cross
        + slots
        + sems
        + recv
        + [
            pltpu.VMEM((stage_rows(SCATTER_SPANS, rows), LANES), f32),
            pltpu.VMEM((rows + 16, LANES), f32),
            pltpu.VMEM(TABLE, f32),
            pltpu.VMEM((FF, D), bf),
            pltpu.VMEM((D, FF), bf),
            scratch(ACT_NAME),
            scratch(SLOPE_NAME),
            scratch(QKV_NAME),
            scratch(PROBS_NAME),
            scratch(MIX_NAME),
            scratch(MID_NAME),
            scratch(MLP_IN_NAME),
            pltpu.VMEM((sz.total, D), bf),
            pltpu.VMEM((sz.total, D), bf),
            pltpu.VMEM((sz.total, D), f32),
            pltpu.VMEM((max(8, sz.full - sz.rows), D), f32),
            pltpu.SemaphoreType.DMA((24 + 2 * sz.buffers,)),
            pltpu.SemaphoreType.DMA((2 * sz.buffers,)),
        ],
        compiler_params=pltpu.CompilerParams(
            collective_id=1, has_side_effects=True, vmem_limit_bytes=67 * 10**6
        ),
        name=BACKWARD_NAME,
    )(tokens, cotangent, lengths, table, *[mats[m] for m in MATRICES], *[saved[s] for s in SAVED])
    return input_grad, out.reshape(-1)[:entries]


class Share:
    def __init__(self, place, name, depth, width, low):
        self.name, self.depth, self.half = name, depth, width // 2
        self.high = depth // place.chips
        self.low = low
        self.rows = self.high * (width // LANES)
        third = self.high // 3
        if name is None:
            self.parts = {2: (0, self.high, 0, self.half)}
        elif third % 32:
            first = -(-self.half // LANES // 2) * LANES
            self.parts = {
                2: (0, third, 0, self.half),
                3: (third, third, 0, self.half),
                0: (2 * third, third, 0, first),
                1: (2 * third, third, first, self.half - first),
            }
        else:
            self.parts = {
                2: (0, third, 0, self.half),
                3: (third, third, 0, self.half),
                0: (2 * third, third // 2, 0, self.half),
                1: (2 * third + third // 2, third // 2, 0, self.half),
            }


def shares(place):
    out = [Share(place, n, *SHAPES[n], BASES[n]) for n in MATRICES]
    return out + [Share(place, None, 16 * place.chips, 2 * LANES, None)]


VECTOR_LIST = [(n, j) for n in VECTORS for j in range(SHAPES[n][0] // LANES)]


def fits(place):
    return place.size == [2, 2, 4, 2]


def block_of(place, coords):
    return (coords[1] * 2 + coords[0]) * 4 + coords[2]


def chip_of(block):
    return [rest(quot(block, 4), 2), quot(block, 8), rest(block, 4)]


class Summing:
    def __init__(self, place, me, parts, own, cross, slots, send, recv, cross_send, cross_recv):
        self.place, self.me, self.parts = place, me, parts
        self.own, self.cross, self.slots = own, cross, slots
        self.send, self.recv = send, recv
        self.cross_send, self.cross_recv = cross_send, cross_recv
        self.plan = slot_plan(place, 16 * sum(place.shares))
        self.slot, self.sent = 0, []
        self.waits, self.then = {}, {}

    def rect(self, p, k, dest):
        top, high, left, wide = self.parts[p].parts[k]
        row = block_of(self.place, dest) * self.parts[p].high + top
        return pl.multiple_of(row, 16), high, left, wide

    def swap(self, p, first, count, chunk):
        rows = pl.ds(pl.multiple_of(first, 16), count)
        return pltpu.make_async_remote_copy(
            src_ref=self.own[p].at[1 - self.me[CORE], rows, :],
            dst_ref=self.cross[p].at[rows, :],
            send_sem=self.cross_send.at[p, chunk],
            recv_sem=self.cross_recv.at[p, chunk],
            device_id=self.place.device(partner(self.me)),
            device_id_type=MESH,
        )

    def hand(self, p, k, pos, way, dest, to):
        row, high, left, wide = self.rect(p, k, dest)
        slot = slot_of(self.place, self.plan, k, pos, way, to, dest)
        return pltpu.make_async_remote_copy(
            src_ref=self.own[p].at[self.me[CORE], pl.ds(row, high), pl.ds(left, wide)],
            dst_ref=self.slots[p][k].at[slot],
            send_sem=self.send.at[p, k, self.place.chip(dest)],
            recv_sem=self.recv[p][k].at[slot],
            device_id=self.place.device(to),
            device_id_type=MESH,
        )

    def parents(self, k, rel, dest):
        order = self.place.orders[k]
        for pos in range(2, -1, -1):
            dim = order[pos]
            if rel[dim] == 0:
                continue
            if self.place.size[dim] == 2:
                other = list(self.me)
                other[dim] = 1 - other[dim]
                return [(True, pos, 0, other)]
            here, there = self.me[dim], dest[dim]
            return [
                (here > there, pos, 0, moved(self.me, dim, -1)),
                (here < there, pos, 1, moved(self.me, dim, 1)),
            ]
        return []

    def aim(self, x, y, turn):
        z = self.me[2]
        inner = pick(z >= 2, 3 - z, z)
        end, middle = TURNS[0][turn], TURNS[1][turn]
        at = pick(inner == 0, end, middle)
        dest = [
            1 - self.me[0] if x else self.me[0],
            1 - self.me[1] if y else self.me[1],
            pick(z >= 2, 3 - at, at),
        ]
        cond = inner == 0 if turn == 0 else inner == 1 if turn == 3 else True
        if turn == 4:
            dest[2] = z
        return cond, dest + [self.me[CORE]]

    def task(self, p, k, rel, dest):
        row, high, left, wide = self.rect(p, k, dest)
        core = self.me[CORE]
        cols = slice(left, left + wide)

        def add(terms):
            for i in range(high // 16):
                rows = pl.ds(pl.multiple_of(row + i * 16, 16), 16)
                value = self.own[p][core, rows, cols].astype(jnp.float32)
                for term in terms:
                    value = value + term(i, rows).astype(jnp.float32)
                self.own[p][core, rows, cols] = low(value)

        def kid(pos, way):
            slot = slot_of(self.place, self.plan, k, pos, way, self.me, dest)
            return lambda i, rows: self.slots[p][k][slot, i * 16 : (i + 1) * 16, :]

        kids = onward(self.place, self.place.orders[k], self.me, rel, dest)
        sure = [(pos, way) for cond, pos, way, _ in kids if cond is True]
        for pos, way in sure:
            self.hand(p, k, pos, way, dest, self.me).wait_recv()
        add([lambda i, rows: self.cross[p][rows, cols]] + [kid(*s) for s in sure])
        for cond, pos, way, _ in kids:
            if cond is True or cond is False:
                continue

            def take(pos=pos, way=way):
                self.hand(p, k, pos, way, dest, self.me).wait_recv()
                add([kid(pos, way)])

            pl.when(cond)(take)
        for cond, pos, way, to in self.parents(k, rel, dest):
            when(cond, lambda: self.hand(p, k, pos, way, dest, to).start())

    def offer(self, p, waits, then):
        self.waits[p], self.then[p] = waits, then

    def step(self, p, k, x, y, turn):
        if p in self.waits:
            self.waits.pop(p)()
        cond, dest = self.aim(x, y, turn)
        rel = (x, y, 0 if turn == 4 else 1)
        when(cond, lambda: self.task(p, k, rel, dest))
        self.sent.append((p, k, x, y, turn))
        if x == y == 0 and turn == 4:
            self.then[p](k)

    def pump(self):
        self.slot += 1
        last = self.slot == len(SCHEDULE) - 1
        early, self.sent = (self.sent, []) if last else ([], self.sent)
        for code in SCHEDULE[self.slot]:
            p, k = len(MATRICES) - 1 - code // 80, (code // 20) % 4
            x, y, turn = (code // 10) % 2, (code // 5) % 2, code % 5
            self.step(p, k, x, y, turn)
            if p == 0 and k == 2:
                self.step(len(MATRICES), k, x, y, turn)
            for one in early[:4]:
                self.ended(*one)
            early = early[4:]
        self.sent = early + self.sent

    def ended(self, p, k, x, y, turn):
        known, dest = self.aim(x, y, turn)

        def wait():
            rel = (x, y, 0 if turn == 4 else 1)
            for cond, pos, way, to in self.parents(k, rel, dest):
                when(cond, lambda: self.hand(p, k, pos, way, dest, to).wait_send())

        if (x, y, turn) != (0, 0, 4):
            when(known, wait)

    def drain(self):
        for one in self.sent:
            self.ended(*one)


def most_blocks(part, entries):
    return ((entries + 2 * LANES) // LANES - 1) // part.rows + 2


def meeting(part, entries, block):
    start = (part.low + block * part.rows) * LANES
    return quot(start, entries), quot(start + part.rows * LANES - 1, entries)


def first_block(part, entries, flat):
    ahead = entries * flat - part.low * LANES
    return quot(pick(ahead > 0, ahead, 0), part.rows * LANES)


def deliver(place, me, parts, own, land, land_send, land_recv, vec_land, vec_send, vec_recv, local, entries):
    flat, core = place.flat(me), me[CORE]
    mine = block_of(place, me)
    devices = place.devices

    def device(d):
        return (quot(d, place.shape[1]), rest(d, place.shape[1]))

    def piece(p, k):
        top, high, left, wide = parts[p].parts[k]
        return pl.ds(top, high), pl.ds(left, wide)

    def source(p, block, k):
        top, high, left, wide = parts[p].parts[k]
        row = pl.multiple_of(block * parts[p].high + top, 16)
        return own[p].at[core, pl.ds(row, high), pl.ds(left, wide)]

    def block_copy(p, block, to, which, k):
        part = parts[p]
        slot = block - first_block(part, entries, to)
        return pltpu.make_async_remote_copy(
            src_ref=source(p, block, k),
            dst_ref=land[p].at[slot, core, *piece(p, k)],
            send_sem=land_send.at[p, which, k],
            recv_sem=land_recv[p].at[slot, core, k],
            device_id=device(to),
            device_id_type=MESH,
        )

    def block_local(p, block, k):
        part = parts[p]
        slot = block - first_block(part, entries, flat)
        return pltpu.make_async_copy(
            source(p, block, k),
            land[p].at[slot, core, *piece(p, k)],
            local.at[p, k],
        )

    def sends(p):
        one, two = meeting(parts[p], entries, mine)
        return [
            (one != flat, one, 0),
            (jnp.logical_and(two != one, two != flat), two, 1),
        ], pick(one == flat, 1, pick(two == flat, 1, 0)) > 0

    def vector_pairs():
        out = []
        for v, (name, j) in enumerate(VECTOR_LIST):
            row = BASES[name] + j
            for d in range((row * LANES) // entries, ((row + 1) * LANES - 1) // entries + 1):
                if (v // 16, d) not in out:
                    out.append((v // 16, d))
        return out

    def vector_copy(n, block, d):
        return pltpu.make_async_remote_copy(
            src_ref=own[4].at[0, block * 16 : (block + 1) * 16, :],
            dst_ref=vec_land.at[block],
            send_sem=vec_send.at[n],
            recv_sem=vec_recv.at[block],
            device_id=device(d),
            device_id_type=MESH,
        )

    def start(p, k):
        remote, here = sends(p)
        for cond, to, which in remote:
            pl.when(cond)(lambda: block_copy(p, mine, to, which, k).start())
        pl.when(here)(lambda: block_local(p, mine, k).start())

    def start_vectors():
        for n, (block, d) in enumerate(vector_pairs()):
            home = place.flat(chip_of(block) + [0])
            if home == d:

                @pl.when(flat == d)
                def _():
                    vec_land[block] = own[4][0, block * 16 : (block + 1) * 16, :]

            else:
                pl.when(flat == home)(lambda: vector_copy(n, block, d).start())

    def expected(p):
        part = parts[p]
        low_block = first_block(part, entries, flat)
        top = part.low + part.rows * place.chips
        begins = part.low * LANES < entries * (flat + 1)
        ends = top * LANES > entries * flat
        for i in range(min(most_blocks(part, entries), place.chips)):
            block = low_block + i
            inside = (part.low + block * part.rows) * LANES < entries * (flat + 1)
            yield both_all(begins, ends, inside, block < place.chips), block, i

    def both_all(*conds):
        return functools.reduce(jnp.logical_and, conds)

    def finish(stage, margin, out):
        base = quot(entries * flat, LANES)
        for p in (3, 2, 1, 0):
            part = parts[p]
            blocks = 2 * part.half // LANES
            remote, here = sends(p)
            for k in part.parts:
                pl.when(here)(lambda: block_local(p, mine, k).wait())
            for cond, block, i in expected(p):

                def take():
                    for half in range(2):
                        sender = place.flat(chip_of_traced(block) + [half])

                        @pl.when(sender != flat)
                        def _():
                            for k in part.parts:
                                spot = land[p].at[i, half, *piece(p, k)]
                                pltpu.make_async_remote_copy(
                                    src_ref=spot,
                                    dst_ref=spot,
                                    send_sem=land_send.at[p, 0, k],
                                    recv_sem=land_recv[p].at[i, half, k],
                                    device_id=device(sender),
                                    device_id_type=MESH,
                                ).wait_recv()

                    at = part.low + block * part.rows - base + margin
                    for r in range(part.high // 16):
                        for half in range(2):
                            for j in range(blocks // 2):
                                stage[
                                    pl.ds(
                                        at + r * 16 * blocks + half * (blocks // 2) + j,
                                        16,
                                        stride=blocks,
                                    ),
                                    :,
                                ] = land[p][
                                    i, half, r * 16 : (r + 1) * 16, j * LANES : (j + 1) * LANES
                                ].astype(jnp.float32)

                pl.when(cond)(take)
        for n, (block, d) in enumerate(vector_pairs()):
            home = place.flat(chip_of(block) + [0])

            @pl.when(flat == d)
            def _():
                if home != d:
                    vector_copy(n, block, d).wait_recv()
                for v in range(block * 16, min((block + 1) * 16, len(VECTOR_LIST))):
                    name, j = VECTOR_LIST[v]
                    row = BASES[name] + j
                    if (row * LANES) // entries <= d <= ((row + 1) * LANES - 1) // entries:
                        spot = row - (entries * d) // LANES + margin
                        stage[spot : spot + 1, :] = vec_land[block][
                            v % 16 : v % 16 + 1, :
                        ].astype(jnp.float32)

        shift = rest(entries * flat, LANES)
        back = rest(LANES - shift, LANES)
        rows = out.shape[0]

        def turn(i):
            at = pl.ds(pl.multiple_of(margin + i * 16, 16), 16)
            stage[at, :] = pltpu.roll(stage[at, :], back, 1)

        loop(rows // 16 + 1, turn, 8)

        def merge(i):
            lane = lax.broadcasted_iota(jnp.int32, (16, LANES), 1)
            now = stage[pl.ds(margin + i * 16, 16), :]
            after = stage[pl.ds(margin + i * 16 + 1, 16), :]
            out[tile(i), :] = jnp.where(lane < LANES - shift, now, after)

        loop(rows // 16, merge, 8)
        for p in range(4):
            for cond, to, which in sends(p)[0]:
                for k in parts[p].parts:
                    pl.when(cond)(lambda: block_copy(p, mine, to, which, k).wait_send())
        for n, (block, d) in enumerate(vector_pairs()):
            home = place.flat(chip_of(block) + [0])
            if home != d:
                pl.when(flat == home)(lambda: vector_copy(n, block, d).wait_send())

    return start, start_vectors, finish


def chip_of_traced(block):
    return [rest(quot(block, 4), 2), quot(block, 8), rest(block, 4)]


SCHEDULE = (
        (),
        (),
        (),
        (76, 48, 71),
        (45,),
        (75, 70),
        (55,),
        (56, 65),
        (115, 87, 136, 85),
        (46, 95, 135, 150, 126, 125, 33),
        (60, 72, 155, 86, 151, 116, 50),
        (5, 127, 40, 35, 78, 130, 97),
        (154, 51, 61, 99, 120, 128),
        (145, 32, 105, 158, 215),
        (159, 90, 49, 98, 15, 66, 112, 88),
        (210, 114, 110, 140, 59, 58, 217, 77, 156),
        (138, 195, 25, 235, 17),
        (111, 16, 73, 131, 121, 62, 96, 19, 230),
        (137, 47, 119, 216, 178, 6, 146),
        (57, 41, 7, 238, 157, 207, 237, 68, 206, 152, 205, 79),
        (141, 219, 233, 118, 122, 218, 139, 193, 225, 67, 37, 236),
        (133, 39, 30, 220, 10, 209, 9),
        (132, 147, 113, 91, 8, 231, 52, 74, 42, 80, 36),
        (53, 200, 117, 199, 92, 134, 69, 221),
        (106, 142, 173, 0, 232, 38, 108, 100, 153),
        (208, 109, 129, 12, 20, 226, 175, 93, 201, 185, 63, 211, 18, 190),
        (11, 222, 107, 223, 176, 81, 196, 26, 31, 43, 179, 168, 101, 197, 278, 191, 28, 166, 227,
     310, 277, 256, 212, 13, 255, 228, 198, 257, 82, 295, 258, 273, 275, 234, 271, 296, 1, 123, 313,
     315, 21, 270, 285, 102, 187, 103, 170, 165, 29, 318, 64, 276, 14, 300, 245, 188, 286, 316, 317,
     203, 239, 2, 169, 250, 311, 298, 252, 279, 23, 290, 192, 305, 3, 180, 83, 265, 186, 177, 202,
     171, 27, 251, 160, 89, 280, 291, 248, 148, 297, 306, 194, 260, 172, 167, 319, 259, 94, 247,
     229, 181, 281, 240, 34, 253, 288, 246, 312, 266, 307, 213, 254, 149, 22, 268, 299, 224, 143,
     274, 161, 272, 182, 301, 241, 124, 214, 292, 293, 287, 174, 261, 308, 54, 162, 267, 183, 289,
     189, 249, 24, 163, 283, 269, 302, 84, 303, 242, 104, 314, 144, 282, 243, 204, 309, 294, 262,
     263, 4, 44, 184, 164, 244, 304, 284, 264),
)
TURNS = ((3, 2, 1, 3, 0), (3, 3, 2, 0, 1))


def stage_margin(parts):
    return max(part.rows for part in parts[:4]) + 16


def even_kernel(place, entries, sz, tokens, cotangent, lengths, table, *refs):
    mats, refs = dict(zip(MATRICES, refs[:4])), refs[4:]
    given, refs = dict(zip(SAVED, refs[:8])), refs[8:]
    out, input_grad, refs = refs[0], refs[1], refs[2:]
    parts = shares(place)
    own, cross, land, refs = refs[:5], refs[5:10], refs[10:14], refs[14:]
    slots, recv = [], []
    for part in parts:
        slots.append(dict(zip(part.parts, refs)))
        refs = refs[len(part.parts) :]
    for part in parts:
        recv.append(dict(zip(part.parts, refs)))
        refs = refs[len(part.parts) :]
    send, cross_send, cross_recv, land_send, refs = *refs[:4], refs[4:]
    land_recv, refs = refs[:4], refs[4:]
    vec_land, vec_send, vec_recv, local, refs = *refs[:4], refs[4:]
    stage, sums, refs = refs[0], refs[1], refs[2:]
    big_a, big_b, refs = refs[0], refs[1], refs[2:]
    wide, slope, qkv, probs, mix, mid, narrow, x, g, temp, blank, partial, load, done = refs
    me = place.coords()
    flat = place.flat(me)
    count = sz.total
    order = (G_NAME, ACT_NAME, W_FC2_NAME, SLOPE_NAME, MLP_IN_NAME, W_FC1_NAME, MID_NAME, MIX_NAME, X_NAME, QKV_NAME, PROBS_NAME)

    def fetches(name):
        sem = load.at[order.index(name)]
        if name in (G_NAME, X_NAME):
            src, dst = (cotangent, g) if name == G_NAME else (tokens, x)
            return [
                pltpu.make_async_copy(
                    src.at[sz.given(b)],
                    dst.at[sz.at(b)],
                    load.at[order.index(name) if b == 0 else len(order) + 10 + 2 * b + (name == G_NAME)],
                )
                for b in range(sz.buffers)
            ]
        return [pltpu.make_async_copy(*places[name], sem)]

    places = {
        ACT_NAME: (given[ACT_NAME], wide),
        SLOPE_NAME: (given[SLOPE_NAME], slope),
        MLP_IN_NAME: (given[MLP_IN_NAME], narrow),
        MID_NAME: (given[MID_NAME], mid),
        MIX_NAME: (given[MIX_NAME], mix),
        QKV_NAME: (given[QKV_NAME], qkv),
        PROBS_NAME: (given[PROBS_NAME], probs),
        W_FC2_NAME: (mats[W_FC2_NAME], big_a),
        W_FC1_NAME: (mats[W_FC1_NAME], big_b),
    }

    def begin(name):
        for c in fetches(name):
            c.start()

    def ready(name):
        for c in fetches(name):
            c.wait()

    for name in order:
        begin(name)
    barrier = pltpu.get_barrier_semaphore()

    def hello(d):
        @pl.when(d != flat)
        def _():
            pl.semaphore_signal(
                barrier,
                inc=1,
                device_id=(quot(d, place.shape[1]), rest(d, place.shape[1])),
                device_id_type=MESH,
            )

    loop(place.devices, hello)
    adding = Summing(
        place, me, parts, own, cross, slots, send, recv, cross_send, cross_recv
    )
    start, start_vectors, finish = deliver(
        place, me, parts, own, land, land_send, land_recv, vec_land, vec_send, vec_recv, local, entries
    )

    def stepped(steps, body, groups):
        each = steps // groups
        for n in range(groups):
            loop(each, lambda i: body(n * each + i))
            adding.pump()

    def sum_to(name, c, value):
        at = SUMS.index(name)
        sums[at : at + 1, c] = value

    def ones():
        return jnp.ones((8, count), jnp.bfloat16)

    def column_sums(name, ref, width):
        def body(c):
            sum_to(name, c, dot(ones(), ref[:, c])[0:1, :])

        columns(width, 256, body)

    def pieces(name, left, right, block, groups):
        p = MATRICES.index(name)
        half = parts[p].half
        steps = parts[p].depth // block

        def body(i):
            first = pl.multiple_of(i * block, block)
            value = low(dot(left[:, pl.ds(first, block)], right(), 0, 0))
            own[p][0, pl.ds(first, block), :] = value[:, :half]
            own[p][1, pl.ds(first, block), :] = value[:, half:]
            adding.swap(p, first, block, i).start()

        waits = lambda: loop(steps, lambda i: adding.swap(p, i * block, block, i).wait_recv())
        adding.offer(p, waits, lambda k: start(p, k))
        stepped(steps, body, groups)
        swaps.append((p, steps, block))

    swaps = []

    ready(G_NAME)
    for b in range(sz.buffers):
        rows = sz.at(b)
        valid = valid_rows(lengths, b, sz.images, sz.rows)
        g[rows, :] = low(g[rows, :].astype(jnp.float32) * valid)
    ready(ACT_NAME)
    column_sums(FC2_BIAS_NAME, g, D)
    pl.semaphore_wait(barrier, place.devices - 1)
    pieces(W_FC2_NAME, wide, lambda: g[...], 256, 1)

    ready(W_FC2_NAME)
    ready(SLOPE_NAME)

    def to_pre(i):
        c = pl.ds(pl.multiple_of(i * 256, 256), 256)
        made = dot(g[...], big_a[c, :], 1, 1)
        wide[:, c] = low(made * slope[:, c].astype(jnp.float32))

    stepped(FF // 256, to_pre, 3)
    late = [
        pltpu.make_async_copy(
            mats[W_QKV_NAME].at[:, i * D : (i + 1) * D],
            big_a.at[i * D : (i + 1) * D],
            load.at[len(order) + 8 + i],
        )
        for i in range(3)
    ]
    late.append(
        pltpu.make_async_copy(mats[W_PROJ_NAME], big_a.at[3 * D : 4 * D], load.at[len(order) + 11])
    )
    for c in reversed(late):
        c.start()
    ready(MLP_IN_NAME)
    column_sums(FC1_BIAS_NAME, wide, FF)
    pieces(W_FC1_NAME, narrow, lambda: wide[...], 128, 3)

    attn_load = pltpu.make_async_copy(given[ATTN_IN_NAME], narrow, load.at[len(order) + 7])
    attn_load.start()
    ready(W_FC1_NAME)

    def to_mlp(i):
        c = pl.ds(pl.multiple_of(i * 256, 256), 256)
        temp[:, c] = dot(wide[...], big_b[c, :], 1, 1)

    stepped(D // 256, to_mlp, 3)
    ready(MID_NAME)

    def folded(v):
        return v[0:8, :] + v[8:16, :]

    def norm_sums(body, gain, bias):
        partial[...] = jnp.zeros(partial.shape, jnp.float32)

        def step(i):
            for which, value in enumerate(body(i)):
                partial[which] += folded(value)

        loop(count // 16, step, 2)
        for which, name in enumerate((gain, bias)):
            at = SUMS.index(name)
            sums[at : at + 1, 0:D] = jnp.sum(partial[which], axis=0, keepdims=True)


    def back_second(i):
        normed, inv = normalize(mid[tile(i), :])
        d = temp[tile(i), :]
        v = g[tile(i), :].astype(jnp.float32) + norm_back(d, normed, inv, vector(table, LN2_GAIN_NAME))
        mid[tile(i), :] = v
        g[tile(i), :] = low(v)
        return d * normed, d

    norm_sums(back_second, LN2_GAIN_NAME, LN2_BIAS_NAME)
    ready(MIX_NAME)
    column_sums(PROJ_BIAS_NAME, g, D)
    adding.pump()
    pieces(W_PROJ_NAME, mix, lambda: g[...], 256, 1)
    late[3].wait()

    def to_mix(i):
        c = pl.ds(pl.multiple_of(i * 256, 256), 256)
        rows = pl.ds(pl.multiple_of(3 * D + i * 256, 256), 256)
        slope[:, c] = low(dot(g[...], big_a[rows, :], 1, 1))

    stepped(D // 256, to_mix, 1)
    ready(QKV_NAME)
    ready(PROBS_NAME)
    for b in range(sz.buffers):
        rows = sz.at(b)

        def attend(p):
            halves = half_lanes(sz.rows)
            at = lambda part: pl.ds(pl.multiple_of(part * D + p * LANES, LANES), LANES)
            q, k, v = (qkv[rows, at(part)] for part in range(3))
            dm = slope[rows, at(0)]
            dq = dk = dv = 0.0
            for h in range(2):
                pr = probs[(b * sz.pairs + p) * 2 + h]
                dmh = dm * halves[h]
                dp = dot(dmh, v, 1, 1)
                prf = pr.astype(jnp.float32)
                ds = low(prf * (dp - jnp.sum(prf * dp, axis=-1, keepdims=True)))
                dv = dv + dot(pr, dmh, 0, 0)
                dq = dq + dot(ds, k * halves[h])
                dk = dk + dot(ds, q * halves[h], 0, 0)
            wide[rows, at(0)] = low(dq * SCALE)
            wide[rows, at(1)] = low(dk * SCALE)
            wide[rows, at(2)] = low(dv)

        stepped(sz.pairs, attend, 3)
    for c in late[:3]:
        c.wait()

    def to_attn(i):
        c = pl.ds(pl.multiple_of(i * 256, 256), 256)
        made = None
        for part in range(3):
            rows = pl.ds(pl.multiple_of(part * D + i * 256, 256), 256)
            term = dot(wide[:, part * D : (part + 1) * D], big_a[rows, :], 1, 1)
            made = term if made is None else made + term
        temp[:, c] = made

    stepped(D // 256, to_attn, 3)
    ready(X_NAME)

    def back_first(i):
        normed, inv = normalize(x[tile(i), :].astype(jnp.float32))
        d = temp[tile(i), :]
        mid[tile(i), :] = mid[tile(i), :] + norm_back(d, normed, inv, vector(table, LN1_GAIN_NAME))
        return d * normed, d

    norm_sums(back_first, LN1_GAIN_NAME, LN1_BIAS_NAME)
    outs = []
    for b in range(sz.buffers):
        outs.append(
            pltpu.make_async_copy(mid.at[sz.at(b)], input_grad.at[sz.given(b)], done.at[2 * b])
        )
        if sz.full > sz.rows:
            blank[...] = jnp.zeros(blank.shape, blank.dtype)
            outs.append(
                pltpu.make_async_copy(
                    blank,
                    input_grad.at[b * sz.full + sz.rows : (b + 1) * sz.full],
                    done.at[2 * b + 1],
                )
            )
    for c in outs:
        c.start()

    attn_load.wait()

    def qv_sums(c):
        wide_sum = dot(ones(), wide[:, c])[0:1, :]
        sums[len(SUMS) : len(SUMS) + 1, c] = wide_sum

    columns(3 * D, 256, qv_sums)
    for name, part in ((Q_BIAS_NAME, 0), (V_BIAS_NAME, 2)):
        at = SUMS.index(name)
        sums[at : at + 1, 0:D] = sums[len(SUMS) : len(SUMS) + 1, part * D : (part + 1) * D]
    own[4][...] = jnp.zeros(own[4].shape, own[4].dtype)
    padded = round_up(len(VECTOR_LIST), 16)
    for v, (name, j) in enumerate(VECTOR_LIST):
        at = SUMS.index(name)
        stage[v : v + 1, :] = sums[at : at + 1, j * LANES : (j + 1) * LANES]
    stage[len(VECTOR_LIST) : padded, :] = jnp.zeros((padded - len(VECTOR_LIST), LANES), jnp.float32)
    own[4][0, 0:padded, :] = low(stage[0:padded, :])
    adding.swap(4, 0, parts[4].depth, 0).start()
    swaps.append((4, 1, parts[4].depth))
    adding.offer(4, lambda: adding.swap(4, 0, parts[4].depth, 0).wait_recv(), lambda k: start_vectors())
    adding.pump()
    pieces(W_QKV_NAME, narrow, lambda: wide[:, 0 : 3 * D], 128, 3)
    finish(stage, stage_margin(parts), out)
    adding.drain()
    for p, steps, block in swaps:
        loop(steps, lambda i: adding.swap(p, i * block, block, i).wait_send())
    for c in outs:
        c.wait()


def even_backward(place, tokens, cotangent, lengths, mats, saved, table, entries):
    rows = part_rows(entries)
    sz = Sizes(tokens, lengths)
    parts = shares(place)
    dma = pltpu.SemaphoreType.DMA
    plan = slot_plan(place, rows)
    rects = [(part, k) for part in parts for k in part.parts]
    any_spec = pl.BlockSpec(memory_space=pl.ANY)
    vmem = pl.BlockSpec(memory_space=pltpu.VMEM)
    smem = pl.BlockSpec(memory_space=pltpu.SMEM)
    bf, f32 = jnp.bfloat16, jnp.float32
    shapes = saved_shapes(sz)
    scratch = lambda name: pltpu.VMEM(*shapes[name])
    out, input_grad = pl.pallas_call(
        functools.partial(even_kernel, place, entries, sz),
        out_shape=[
            jax.ShapeDtypeStruct((rows, LANES), f32),
            jax.ShapeDtypeStruct(tokens.shape, f32),
        ],
        in_specs=[any_spec, any_spec, smem, vmem] + [any_spec] * 12,
        out_specs=[vmem, any_spec],
        scratch_shapes=[pltpu.VMEM((2, part.depth, part.half), bf) for part in parts]
        + [pltpu.VMEM((part.depth, part.half), bf) for part in parts]
        + [
            pltpu.VMEM((most_blocks(part, entries), 2, part.high, part.half), bf)
            for part in parts[:4]
        ]
        + [
            pltpu.VMEM((plan[k][1], part.parts[k][1], part.parts[k][3]), bf) for part, k in rects
        ]
        + [dma((plan[k][1],)) for _, k in rects]
        + [dma((5, place.classes, place.chips)), dma((5, 12)), dma((5, 12)), dma((4, 2, place.classes))]
        + [dma((most_blocks(part, entries), 2, place.classes)) for part in parts[:4]]
        + [
            pltpu.VMEM((-(-len(VECTOR_LIST) // 16), 16, LANES), bf),
            dma((32,)),
            dma((-(-len(VECTOR_LIST) // 16),)),
            dma((4, place.classes)),
            pltpu.VMEM((2 * stage_margin(parts) + rows + 32, LANES), f32),
            pltpu.VMEM(TABLE, f32),
            pltpu.VMEM((FF, D), bf),
            pltpu.VMEM((D, FF), bf),
            scratch(ACT_NAME),
            scratch(SLOPE_NAME),
            scratch(QKV_NAME),
            scratch(PROBS_NAME),
            scratch(MIX_NAME),
            scratch(MID_NAME),
            scratch(MLP_IN_NAME),
            pltpu.VMEM((sz.total, D), bf),
            pltpu.VMEM((sz.total, D), bf),
            pltpu.VMEM((sz.total, D), f32),
            pltpu.VMEM((max(8, sz.full - sz.rows), D), f32),
            pltpu.VMEM((2, 8, D), f32),
            pltpu.SemaphoreType.DMA((24 + 2 * sz.buffers,)),
            pltpu.SemaphoreType.DMA((2 * sz.buffers,)),
        ],
        compiler_params=pltpu.CompilerParams(
            collective_id=1, has_side_effects=True, vmem_limit_bytes=67 * 10**6
        ),
        name=BACKWARD_NAME,
    )(tokens, cotangent, lengths, table, *[mats[m] for m in MATRICES], *[saved[s] for s in SAVED])
    return input_grad, out.reshape(-1)[:entries]


def solution(mesh):
    place = Place(mesh)

    def shards(tokens, cotangent, params, lengths):
        mats, saved, table, out = forward(place, tokens, params, lengths)
        input_grad, grad = (even_backward if fits(place) else backward)(
            place, tokens, cotangent, lengths, mats, saved, table, params.shape[0]
        )
        return out, input_grad, grad

    rows, flat = P(AXES, None), P(AXES)
    return jax.shard_map(
        shards,
        mesh=mesh,
        in_specs=(rows, rows, flat, rows),
        out_specs=(rows, rows, flat),
        check_vma=False,
    )
```

```python
import functools
import math

import jax
import jax.numpy as jnp
from jax import lax
from jax.experimental import pallas as pl
from jax.experimental.pallas import tpu as pltpu
from jax.sharding import PartitionSpec as P

ATTN_IN_NAME = "attn_in"
QKV_NAME = "qkv"
PROBS_NAME = "probs"
MIX_NAME = "mix"
MID_NAME = "mid"
MLP_IN_NAME = "mlp_in"
ACT_NAME = "act"
SLOPE_NAME = "slope"
LN1_GAIN_NAME = "ln1_gain"
LN1_BIAS_NAME = "ln1_bias"
W_QKV_NAME = "w_qkv"
Q_BIAS_NAME = "q_bias"
V_BIAS_NAME = "v_bias"
W_PROJ_NAME = "w_proj"
PROJ_BIAS_NAME = "proj_bias"
LN2_GAIN_NAME = "ln2_gain"
LN2_BIAS_NAME = "ln2_bias"
W_FC1_NAME = "w_fc1"
FC1_BIAS_NAME = "fc1_bias"
W_FC2_NAME = "w_fc2"
FC2_BIAS_NAME = "fc2_bias"
G_NAME = "g"
X_NAME = "x"
BACKWARD_NAME = "backward"
AXES = ("dp", "fsdp")
LANES = 128
CORE = 3
MESH = pl.DeviceIdType.MESH


def quot(a, b):
    if isinstance(a, int) and isinstance(b, int):
        return a // b
    return a if isinstance(b, int) and b == 1 else lax.div(a, jnp.int32(b))


def rest(a, b):
    if isinstance(a, int) and isinstance(b, int):
        return a % b
    return lax.rem(a, jnp.int32(b))


def pick(cond, a, b):
    return lax.select(cond, lax.add(jnp.int32(0), a), lax.add(jnp.int32(0), b))


class Place:
    def __init__(self, mesh):
        devs = mesh.devices
        spot = lambda d: (*d.coords, d.core_on_chip)
        self.shape = devs.shape
        self.digits = []
        for axis in range(2):
            line = [spot(devs[i, 0] if axis == 0 else devs[0, i]) for i in range(devs.shape[axis])]
            found, stride = [], 1
            while stride < len(line):
                delta = [b - a for a, b in zip(line[0], line[stride])]
                phys = [p for p in range(4) if delta[p]][0]
                step, size = delta[phys], 1
                while (
                    size * stride < len(line)
                    and line[size * stride][phys] - line[0][phys] == size * step
                    and all(line[size * stride][q] == line[0][q] for q in range(4) if q != phys)
                ):
                    size += 1
                found.append((phys, step, size, stride))
                stride *= size
            self.digits.append(found)
        self.size = [1, 1, 1, 1]
        for found in self.digits:
            for phys, _, size, _ in found:
                self.size[phys] *= size
        self.devices = devs.size
        self.chips = math.prod(self.size[:3])
        long = max(range(3), key=lambda p: self.size[p])
        a, b = [p for p in range(3) if p != long]
        self.orders = ((long, a, b), (long, b, a))
        self.shares = (1, 1)
        if self.chips <= 16:
            self.orders += ((a, long, b), (b, long, a))
            self.shares += (2, 2)
        self.classes = len(self.orders)

    def coords(self):
        index = [lax.axis_index(name) for name in AXES]
        out = [0, 0, 0, 0]
        for axis in range(2):
            for phys, step, size, stride in self.digits[axis]:
                out[phys] = out[phys] + rest(quot(index[axis], stride), size) * step
        return out

    def device(self, coords):
        out = []
        for axis in range(2):
            total = 0
            for phys, step, size, stride in self.digits[axis]:
                total = total + rest(quot(coords[phys], step), size) * stride
            out.append(total)
        return tuple(out)

    def flat(self, coords):
        dp, fsdp = self.device(coords)
        return dp * self.shape[1] + fsdp

    def chip(self, coords):
        return (coords[0] * self.size[1] + coords[1]) * self.size[2] + coords[2]

    def class_rows(self, rows):
        units = rows // 16
        counts = [units * share // sum(self.shares) for share in self.shares]
        counts[-1] += units - sum(counts)
        out, start = [], 0
        for count in counts:
            out.append((start * 16, count * 16))
            start += count
        return out


def flipped(mine, rel, size):
    total, bit = 0, 1
    while bit < size:
        total = total + bit * rest(rest(quot(mine, bit), 2) + rest(quot(rel, bit), 2), 2)
        bit *= 2
    return total


def both(*conds):
    known = [c for c in conds if isinstance(c, bool)]
    if not all(known):
        return False
    rest = [c for c in conds if not isinstance(c, bool)]
    return functools.reduce(jnp.logical_and, rest) if rest else True


def when(cond, fn):
    if isinstance(cond, bool):
        if cond:
            fn()
    else:
        pl.when(cond)(fn)


def moved(coords, dim, by):
    out = list(coords)
    out[dim] = out[dim] + by
    return out


def partner(coords):
    out = list(coords)
    out[CORE] = 1 - out[CORE]
    return out


def neighbours(place, me):
    out = [(True, partner(me))]
    for dim in range(3):
        if place.size[dim] == 1:
            continue
        if place.size[dim] == 2:
            other = list(me)
            other[dim] = 1 - other[dim]
            out.append((True, other))
        else:
            out.append((me[dim] < place.size[dim] - 1, moved(me, dim, 1)))
            out.append((me[dim] > 0, moved(me, dim, -1)))
    return out


def greet(place, me):
    barrier = pltpu.get_barrier_semaphore()
    nbrs = neighbours(place, me)
    for cond, who in nbrs:
        when(
            cond,
            lambda who=who: pl.semaphore_signal(
                barrier, inc=1, device_id=place.device(who), device_id_type=pl.DeviceIdType.MESH
            ),
        )
    peers = sum(1 if cond is True else jnp.where(cond, 1, 0) for cond, _ in nbrs)
    pl.semaphore_wait(barrier, peers)


def onward(place, order, me, rel, src):
    out = []
    for pos in range(3):
        dim = order[pos]
        size = place.size[dim]
        if size == 1:
            continue
        later = [rel[d] == 0 for d in order[pos + 1 :]]
        if size == 2:
            other = list(me)
            other[dim] = 1 - other[dim]
            out.append((both(*later, rel[dim] == 0), pos, 0, other))
        else:
            for way, by in ((0, 1), (1, -1)):
                if by == 1:
                    here = both(me[dim] >= src[dim], me[dim] < size - 1)
                else:
                    here = both(me[dim] <= src[dim], me[dim] > 0)
                cond = both(*later, here)
                out.append((cond, pos, way, moved(me, dim, by)))
    return out


PASSES = (
    0, 16, 32, 48, 1, 17, 40, 33, 52, 49, 41, 56, 3, 8, 2, 20, 35, 34, 10, 53, 18, 28,
    11, 5, 51, 36, 12, 19, 45, 57, 50, 9, 7, 21, 55, 54, 60, 25, 44, 6, 22, 29, 24, 42,
    58, 27, 37, 26, 59, 43, 15, 23, 4, 39, 61, 14, 30, 13, 62, 38, 63, 31, 47, 46,
)


def walk_parts(place, body, reverse=False, after=None):
    if place.size[:3] == [2, 2, 4]:
        for i, code in enumerate(PASSES[::-1] if reverse else PASSES):
            body(code // 16, ((code // 8) % 2, (code // 4) % 2, code % 4))
            if after is not None:
                after(i)
        return

    def each(rel):
        for k in range(place.classes):
            body(k, rel)

    walk(place, each, reverse)
    if after is not None:
        after(None)


def walk(place, body, reverse=False):
    sizes = place.size[:3]
    if place.chips <= 16:
        rels = [
            (x, y, z) for x in range(sizes[0]) for y in range(sizes[1]) for z in range(sizes[2])
        ]
        rels.sort(key=lambda r: (sum(r), r), reverse=reverse)
        for rel in rels:
            body(rel)
        return

    def step(i, carry):
        i = place.chips - 1 - i if reverse else i
        body((i % sizes[0], (i // sizes[0]) % sizes[1], i // (sizes[0] * sizes[1])))
        return carry

    lax.fori_loop(0, place.chips, step, 0)


def source_of(place, me, rel):
    return [flipped(me[d], rel[d], place.size[d]) for d in range(3)] + [me[CORE]]


def gather_all(place, me, held, send, recv, cross, after=None):
    rows = held.shape[1]
    parts = place.class_rows(rows)

    def copy(k, src, slot, sem, who):
        start, count = parts[k]
        ref = held.at[place.flat(src), pl.ds(start, count), :]
        return pltpu.make_async_remote_copy(
            src_ref=ref,
            dst_ref=ref,
            send_sem=send.at[k, place.chip(src), slot],
            recv_sem=sem.at[k, place.chip(src)],
            device_id=place.device(who),
            device_id_type=pl.DeviceIdType.MESH,
        )

    def sends(k, rel, src, act):
        for cond, pos, way, who in onward(place, place.orders[k], me, rel, src):
            when(cond, lambda: act(copy(k, src, pos * 2 + way, recv, who)))
        act(copy(k, src, 6, cross, partner(me)))

    def go(k, rel):
        src = source_of(place, me, rel)
        home = both(*[r == 0 for r in rel])
        if home is not True:
            away = True if home is False else jnp.logical_not(home)
            when(away, lambda: copy(k, src, 0, recv, me).wait_recv())
        sends(k, rel, src, lambda c: c.start())

    walk_parts(place, go, after=after)

    def drain(rel):
        src = source_of(place, me, rel)
        theirs = partner(src)
        for k in range(place.classes):
            sends(k, rel, src, lambda c: c.wait_send())
            copy(k, theirs, 0, cross, me).wait_recv()

    walk(place, drain)


def gather_sems(place):
    return [
        pltpu.SemaphoreType.DMA((place.classes, place.chips, 7)),
        pltpu.SemaphoreType.DMA((place.classes, place.chips)),
        pltpu.SemaphoreType.DMA((place.classes, place.chips)),
    ]


def slot_plan(place, rows):
    plan = []
    for order in place.orders:
        starts, total = [], 0
        for pos in range(3):
            before = math.prod(place.size[d] for d in order[:pos])
            size = place.size[order[pos]]
            starts.append(total)
            total += before * (1 if size == 2 else size + 1 if size > 1 else 0)
        plan.append((starts, total))
    return plan


def slot_of(place, plan, k, pos, way, at, dest):
    order = place.orders[k]
    index = 0
    for d in order[:pos]:
        index = index * place.size[d] + dest[d]
    dim = order[pos]
    size = place.size[dim]
    if size > 2:
        spot = dest[dim]
        if way == 1:
            spot = spot + pick(at[dim] == dest[dim], size - dest[dim], 0)
        index = index * (size + 1) + spot
    return plan[k][0][pos] + index


def add_rows(dst, a, b, count, step=16):
    def body(i, carry):
        r = pl.ds(pl.multiple_of(i * step, step), step)
        dst(r, a(r).astype(jnp.float32) + b(r).astype(jnp.float32))
        return carry

    lax.fori_loop(0, count // step, body, 0)


def scatter_all(place, me, own, cross, slots, total, sems):
    cross_send, cross_recv, send, recv = sems
    rows = own.shape[1]
    parts = place.class_rows(rows)
    plan = slot_plan(place, rows)

    def swap(dest):
        return pltpu.make_async_remote_copy(
            src_ref=own.at[place.flat(partner(dest))],
            dst_ref=cross.at[place.chip(dest)],
            send_sem=cross_send.at[place.chip(dest)],
            recv_sem=cross_recv.at[place.chip(dest)],
            device_id=place.device(partner(me)),
            device_id_type=pl.DeviceIdType.MESH,
        )

    def pass_on(k, pos, way, dest, to):
        start, count = parts[k]
        slot = slot_of(place, plan, k, pos, way, to, dest)
        return pltpu.make_async_remote_copy(
            src_ref=own.at[place.flat(dest), pl.ds(start, count), :],
            dst_ref=slots[k].at[slot],
            send_sem=send.at[k, place.chip(dest)],
            recv_sem=recv[k].at[slot],
            device_id=place.device(to),
            device_id_type=pl.DeviceIdType.MESH,
        )

    def parents(k, rel, dest):
        order = place.orders[k]
        out = []
        for pos in range(3):
            dim = order[pos]
            size = place.size[dim]
            if size == 1:
                continue
            later = both(*[rel[d] == 0 for d in order[pos + 1 :]])
            if size == 2:
                other = list(me)
                other[dim] = 1 - other[dim]
                away = rel[dim] == 1
                out.append((both(later, away), pos, 0, other))
            else:
                out.append((both(later, me[dim] > dest[dim]), pos, 0, moved(me, dim, -1)))
                out.append((both(later, me[dim] < dest[dim]), pos, 1, moved(me, dim, 1)))
        return out

    walk(place, lambda rel: swap(source_of(place, me, rel)).start(), reverse=True)

    def go(rel):
        dest = source_of(place, me, rel)
        home = both(*[r == 0 for r in rel])
        flat, chip = place.flat(dest), place.chip(dest)
        swap(dest).wait_recv()

        def mix(final):
            for k in range(place.classes):
                start, count = parts[k]

                def rows_of(r):
                    return pl.ds(r.start + start, r.size)

                if final:

                    def put(r, v):
                        total[rows_of(r), :] = v

                    def held(r):
                        return total[rows_of(r), :]

                else:

                    def put(r, v):
                        own[flat, rows_of(r), :] = v.astype(own.dtype)

                    def held(r):
                        return own[flat, rows_of(r), :]

                add_rows(
                    put,
                    lambda r: own[flat, rows_of(r), :],
                    lambda r: cross[chip, rows_of(r), :],
                    count,
                )
                for cond, pos, way, who in onward(place, place.orders[k], me, rel, dest):

                    def take():
                        slot = slot_of(place, plan, k, pos, way, me, dest)
                        pass_on(k, pos, way, dest, me).wait_recv()
                        add_rows(put, held, lambda r: slots[k][slot, r, :], count)

                    when(cond, take)
                if not final:
                    for cond, pos, way, who in parents(k, rel, dest):
                        when(cond, lambda: pass_on(k, pos, way, dest, who).start())

        if isinstance(home, bool):
            mix(home)
        else:
            pl.when(home)(lambda: mix(True))
            pl.when(jnp.logical_not(home))(lambda: mix(False))

    walk(place, go, reverse=True)

    def drain(rel):
        dest = source_of(place, me, rel)
        swap(dest).wait_send()
        for k in range(place.classes):
            for cond, pos, way, who in parents(k, rel, dest):
                when(cond, lambda: pass_on(k, pos, way, dest, who).wait_send())

    walk(place, drain)


def scatter_scratch(place, rows):
    parts = place.class_rows(rows)
    plan = slot_plan(place, rows)
    dma = pltpu.SemaphoreType.DMA
    return (
        [pltpu.VMEM((place.chips, rows, LANES), jnp.bfloat16)],
        [pltpu.VMEM((plan[k][1], parts[k][1], LANES), jnp.bfloat16) for k in range(place.classes)],
        [dma((place.chips,)), dma((place.chips,)), dma((place.classes, place.chips))],
        [dma((plan[k][1],)) for k in range(place.classes)],
    )


D = 768
HEAD_DIM = 64
FF = 3072
EPSILON = 1e-06
NEG_FILL = -1e30
ROOT_HALF = 0.7071067811865476
INV_ROOT_TWO_PI = 0.3989422804014327

PIECES = (
    (LN1_GAIN_NAME, (D,)),
    (LN1_BIAS_NAME, (D,)),
    (W_QKV_NAME, (D, 3 * D)),
    (Q_BIAS_NAME, (D,)),
    (V_BIAS_NAME, (D,)),
    (W_PROJ_NAME, (D, D)),
    (PROJ_BIAS_NAME, (D,)),
    (LN2_GAIN_NAME, (D,)),
    (LN2_BIAS_NAME, (D,)),
    (W_FC1_NAME, (D, FF)),
    (FC1_BIAS_NAME, (FF,)),
    (W_FC2_NAME, (FF, D)),
    (FC2_BIAS_NAME, (D,)),
)
MATRICES = tuple(name for name, shape in PIECES if len(shape) == 2)
VECTORS = tuple(name for name, shape in PIECES if len(shape) == 1)
SHAPES = dict(PIECES)


def row_bases():
    bases, row = {}, 0
    for name, shape in PIECES:
        bases[name] = row
        row += math.prod(shape) // LANES
    return bases, row


BASES, TOTAL_ROWS = row_bases()
IMAGE_MAX = 98
QKV_BIAS = len(VECTORS)
TABLE = (16, FF)


def part_rows(entries):
    return -(-((LANES - 1 + entries - 1) // LANES + 1) // 16) * 16


def tile(i):
    return pl.ds(pl.multiple_of(i * 16, 16), 16)


def loop(count, body, unroll=1):
    def step(i, carry):
        for u in range(unroll):
            body(i * unroll + u)
        return carry

    whole = count // unroll
    if whole:
        lax.fori_loop(0, whole, step, 0)
    for i in range(whole * unroll, count):
        body(i)


def aligned(raw, held, stage, which, entries):
    rows = held.shape[1]
    shift = (entries * which) % LANES
    stage[0:8, :] = jnp.zeros((8, LANES), jnp.float32)

    def turn(i):
        stage[pl.ds(pl.multiple_of(i * 16 + 8, 8), 16), :] = pltpu.roll(
            raw[tile(i), :].astype(jnp.float32), shift, 1
        )

    loop(rows // 16, turn, 8)

    def merge(i):
        lane = lax.broadcasted_iota(jnp.int32, (16, LANES), 1)
        now = stage[pl.ds(i * 16 + 8, 16), :]
        before = stage[pl.ds(i * 16 + 7, 16), :]
        held[which, tile(i), :] = jnp.where(lane < shift, before, now).astype(held.dtype)

    loop(rows // 16, merge, 8)


def round_up(value, unit):
    return -(-value // unit) * unit


class Span:
    def __init__(self, low, high, name, first, depth, vectors):
        self.low, self.high = low, high
        self.name, self.first, self.depth = name, first, depth
        self.vectors = vectors


def spans(cuts):
    out, row, early = [], 0, []
    for name, shape in PIECES:
        count = math.prod(shape) // LANES
        if len(shape) == 1:
            if out:
                out[-1].vectors.append(name)
                out[-1].high = row + count
            else:
                early.append(name)
        else:
            depth = shape[0] // cuts[name]
            blocks = shape[1] // LANES
            for c in range(cuts[name]):
                start = row + c * depth * blocks
                span = Span(start, start + depth * blocks, name, c * depth, depth, [])
                if not out:
                    span.low, span.vectors = 0, early
                out.append(span)
        row += count
    return out


GATHER_SPANS = spans({name: 1 for name in MATRICES})
SCATTER_SPANS = spans({W_QKV_NAME: 2, W_PROJ_NAME: 1, W_FC1_NAME: 2, W_FC2_NAME: 2})


def stage_rows(spans_, rows):
    return round_up(max(s.high - s.low for s in spans_), 16) + 2 * rows + 32


def owners(span, entries):
    return (span.low * LANES) // entries, (span.high * LANES - 1) // entries


def spread(held, stage, span, entries):
    rows = held.shape[1]
    low, high = owners(span, entries)

    def one(i):
        d = low + i
        base = (entries * d) // LANES - span.low + rows
        cut = (entries * d) % LANES
        first = stage[pl.ds(base, 1), :]

        def body(t):
            stage[pl.ds(base + t * 16, 16), :] = held[d, tile(t), :].astype(jnp.float32)

        loop(rows // 16, body, 8)
        row = stage[pl.ds(base, 1), :]
        stage[pl.ds(base, 1), :] = jnp.where(cut != 0, row + first, row)

    loop(high - low + 1, one)


def form(stage, span, margin, out):
    blocks = SHAPES[span.name][1] // LANES
    base = margin + BASES[span.name] + span.first * blocks - span.low

    def body(i):
        for j in range(blocks):
            out[tile(i + span.first // 16), j * LANES : (j + 1) * LANES] = stage[
                pl.ds(base + i * 16 * blocks + j, 16, stride=blocks), :
            ].astype(out.dtype)

    loop(span.depth // 16, body, max(1, 24 // blocks))


def vector_rows(stage, span, margin, table):
    for name in span.vectors:
        at = margin + BASES[name] - span.low
        row = VECTORS.index(name)
        for j in range(SHAPES[name][0] // LANES):
            table[row : row + 1, j * LANES : (j + 1) * LANES] = stage[at + j : at + j + 1, :]


def vector(table, name):
    row = VECTORS.index(name)
    return table[row : row + 1, 0 : SHAPES[name][0]]


def lay(stage, span, margin, first, value):
    blocks = SHAPES[span.name][1] // LANES
    base = margin + BASES[span.name] - span.low + first * blocks
    for i in range(value.shape[0] // 16):
        for j in range(blocks):
            stage[pl.ds(base + i * 16 * blocks + j, 16, stride=blocks), :] = value[
                i * 16 : (i + 1) * 16, j * LANES : (j + 1) * LANES
            ]


def lay_vectors(stage, span, margin, table):
    for name in span.vectors:
        at = margin + BASES[name] - span.low
        row = VECTORS.index(name)
        for j in range(SHAPES[name][0] // LANES):
            stage[at + j : at + j + 1, :] = table[row : row + 1, j * LANES : (j + 1) * LANES]


def cut(stage, span, own, entries):
    rows = own.shape[1]
    low, high = owners(span, entries)

    def whole(d):
        base = (entries * d) // LANES - span.low + rows

        def body(t):
            own[d, tile(t), :] = stage[pl.ds(base + t * 16, 16), :].astype(own.dtype)

        loop(rows // 16, body, 8)

    def edge(d):
        base = (entries * d) // LANES - span.low + rows

        def body(t):
            now = stage[pl.ds(base + t * 16, 16), :]
            row = base + t * 16 - rows + lax.broadcasted_iota(jnp.int32, (16, LANES), 0)
            inside = jnp.logical_and(row >= 0, row < span.high - span.low)
            before = own[d, tile(t), :].astype(jnp.float32)
            own[d, tile(t), :] = jnp.where(inside, now, before).astype(own.dtype)

        loop(rows // 16, body, 8)

    edge(low)
    if high - low > 1:
        loop(high - low - 1, lambda i: whole(low + 1 + i))
    if high > low:
        edge(high)


def mean_of(v):
    return jnp.sum(v, axis=-1, keepdims=True) * (1.0 / v.shape[-1])


def normalize(v):
    centred = v - mean_of(v)
    inv_std = lax.rsqrt(mean_of(centred * centred) + EPSILON)
    return centred * inv_std, inv_std


def norm_back(grad_out, normed, inv_std, gain):
    grad_norm = grad_out * gain
    return inv_std * (grad_norm - mean_of(grad_norm) - normed * mean_of(grad_norm * normed))


def dot(a, b, left=1, right=0):
    return lax.dot_general(
        a, b, (((left,), (right,)), ((), ())), preferred_element_type=jnp.float32
    )


def columns(width, block, body):
    loop(width // block, lambda i: body(pl.ds(pl.multiple_of(i * block, block), block)))


def segments(lengths, b, images, shape, dim):
    position = lax.broadcasted_iota(jnp.int32, shape, dim)
    total, seg = 0, jnp.zeros(shape, jnp.int32)
    for i in range(images):
        total = total + lengths[b, i]
        seg = seg + jnp.where(position >= total, 1, 0)
    return seg


def valid_rows(lengths, b, images, count):
    return jnp.where(segments(lengths, b, images, (count, 1), 0) < images, 1.0, 0.0)


class Sizes:
    def __init__(self, tokens, lengths):
        self.buffers, self.images = lengths.shape
        self.full = tokens.shape[0] // self.buffers
        self.rows = min(self.full, round_up(self.images * IMAGE_MAX, 16))
        self.total = self.rows * self.buffers
        self.pairs = D // LANES

    def at(self, b):
        return slice(b * self.rows, (b + 1) * self.rows)

    def given(self, b):
        return slice(b * self.full, b * self.full + self.rows)


def low(v):
    return v.astype(jnp.bfloat16)


def half_lanes(rows):
    lane = lax.broadcasted_iota(jnp.int32, (rows, LANES), 1)
    first = low(jnp.where(lane < HEAD_DIM, 1.0, 0.0))
    return first, low(jnp.where(lane < HEAD_DIM, 0.0, 1.0))


SCALE = 1.0 / math.sqrt(HEAD_DIM)
SAVED = (ATTN_IN_NAME, QKV_NAME, PROBS_NAME, MIX_NAME, MID_NAME, MLP_IN_NAME, ACT_NAME, SLOPE_NAME)


def saved_shapes(sz):
    t = sz.total
    bf = jnp.bfloat16
    return {
        ATTN_IN_NAME: ((t, D), bf),
        QKV_NAME: ((t, 3 * D), bf),
        PROBS_NAME: ((sz.buffers * sz.pairs * 2, sz.rows, sz.rows), bf),
        MIX_NAME: ((t, D), bf),
        MID_NAME: ((t, D), jnp.float32),
        MLP_IN_NAME: ((t, D), bf),
        ACT_NAME: ((t, FF), bf),
        SLOPE_NAME: ((t, FF), bf),
    }


def forward_kernel(place, entries, sz, raw, tokens, lengths, *refs):
    mats, refs = dict(zip(MATRICES, refs[:4])), refs[4:]
    out_saved, refs = dict(zip(SAVED, refs[:8])), refs[8:]
    table, block_out, refs = refs[0], refs[1], refs[2:]
    held, stage, refs = refs[0], refs[1], refs[2:]
    w, refs = dict(zip(MATRICES, refs[:4])), refs[4:]
    a, refs = dict(zip(SAVED, refs[:8])), refs[8:]
    normed = refs[0]
    send, recv, cross, done_w, done_a = refs[1:]
    me = place.coords()
    margin = held.shape[1]

    aligned(raw, held, stage, place.flat(me), entries)
    greet(place, me)

    def norm_first(i):
        for b in range(sz.buffers):
            x = tokens[pl.ds(pl.multiple_of(b * sz.full + i * 16, 16), 16), :].astype(jnp.float32)
            normed[pl.ds(pl.multiple_of(b * sz.rows + i * 16, 16), 16), :] = normalize(x)[0]

    def after(i):
        if i is None or i == 8:
            loop(sz.rows // 16, norm_first)

    gather_all(place, me, held, send, recv, cross, after)

    def keep(name):
        pltpu.make_async_copy(a[name], out_saved[name], done_a.at[SAVED.index(name)]).start()

    for span in GATHER_SPANS:
        name = span.name
        spread(held, stage, span, entries)
        form(stage, span, margin, w[name])
        vector_rows(stage, span, margin, table)
        m = MATRICES.index(name)
        pltpu.make_async_copy(w[name], mats[name], done_w.at[m]).start()
    table[QKV_BIAS : QKV_BIAS + 1, 0:D] = vector(table, Q_BIAS_NAME)
    table[QKV_BIAS : QKV_BIAS + 1, D : 2 * D] = jnp.zeros((1, D), jnp.float32)
    table[QKV_BIAS : QKV_BIAS + 1, 2 * D : 3 * D] = vector(table, V_BIAS_NAME)

    def scale_first(i):
        a[ATTN_IN_NAME][tile(i), :] = low(
            normed[tile(i), :] * vector(table, LN1_GAIN_NAME) + vector(table, LN1_BIAS_NAME)
        )

    loop(sz.total // 16, scale_first)
    keep(ATTN_IN_NAME)

    def to_qkv(c):
        a[QKV_NAME][:, c] = low(
            dot(a[ATTN_IN_NAME][...], w[W_QKV_NAME][:, c]) + table[QKV_BIAS : QKV_BIAS + 1, c]
        )

    columns(3 * D, 256, to_qkv)
    keep(QKV_NAME)

    qkv, probs, mix = a[QKV_NAME], a[PROBS_NAME], a[MIX_NAME]
    for b in range(sz.buffers):
        rows = sz.at(b)
        seg_r = segments(lengths, b, sz.images, (sz.rows, 1), 0)
        seg_c = segments(lengths, b, sz.images, (1, sz.rows), 1)

        def attend(p):
            halves = half_lanes(sz.rows)
            at = lambda part: pl.ds(pl.multiple_of(part * D + p * LANES, LANES), LANES)
            q, k, v = (qkv[rows, at(part)] for part in range(3))
            mixed = None
            for h in range(2):
                s = dot(q * (halves[h] * SCALE).astype(q.dtype), k, 1, 1)
                s = jnp.where(seg_r == seg_c, s, NEG_FILL)
                e = jnp.exp(s - jnp.max(s, axis=-1, keepdims=True))
                pr = low(e * (1.0 / jnp.sum(e, axis=-1, keepdims=True)))
                probs[(b * sz.pairs + p) * 2 + h] = pr
                part = dot(pr, v * halves[h])
                mixed = part if mixed is None else mixed + part
            mix[rows, at(0)] = low(mixed)

        loop(sz.pairs, attend)
    keep(PROBS_NAME)
    keep(MIX_NAME)

    def to_mid(c):
        made = dot(mix[...], w[W_PROJ_NAME][:, c]) + table[
            VECTORS.index(PROJ_BIAS_NAME) : VECTORS.index(PROJ_BIAS_NAME) + 1, c
        ]
        for b in range(sz.buffers):
            a[MID_NAME][sz.at(b), c] = (
                tokens[sz.given(b), c].astype(jnp.float32) + made[sz.at(b), :]
            )

    columns(D, 256, to_mid)
    keep(MID_NAME)

    def norm_second(i):
        a[MLP_IN_NAME][tile(i), :] = low(
            normalize(a[MID_NAME][tile(i), :])[0] * vector(table, LN2_GAIN_NAME)
            + vector(table, LN2_BIAS_NAME)
        )

    loop(sz.total // 16, norm_second)
    keep(MLP_IN_NAME)

    def to_act(c):
        at = VECTORS.index(FC1_BIAS_NAME)
        pre = dot(a[MLP_IN_NAME][...], w[W_FC1_NAME][:, c]) + table[at : at + 1, c]
        phi = 0.5 * (1.0 + lax.erf(pre * ROOT_HALF))
        a[ACT_NAME][:, c] = low(pre * phi)
        a[SLOPE_NAME][:, c] = low(phi + pre * jnp.exp(-0.5 * pre * pre) * INV_ROOT_TWO_PI)

    columns(FF, 256, to_act)
    keep(ACT_NAME)
    keep(SLOPE_NAME)

    def to_out(c):
        at = VECTORS.index(FC2_BIAS_NAME)
        made = dot(a[ACT_NAME][...], w[W_FC2_NAME][:, c]) + table[at : at + 1, c]
        for b in range(sz.buffers):
            valid = valid_rows(lengths, b, sz.images, sz.rows)
            block_out[sz.given(b), c] = low(valid * (a[MID_NAME][sz.at(b), c] + made[sz.at(b), :]))
            if sz.full > sz.rows:
                block_out[b * sz.full + sz.rows : (b + 1) * sz.full, c] = jnp.zeros(
                    (sz.full - sz.rows, made.shape[1]), jnp.bfloat16
                )

    columns(D, 256, to_out)
    for m, name in enumerate(MATRICES):
        pltpu.make_async_copy(w[name], mats[name], done_w.at[m]).wait()
    for i, name in enumerate(SAVED):
        pltpu.make_async_copy(a[name], out_saved[name], done_a.at[i]).wait()


def forward(place, tokens, params, lengths):
    entries = params.shape[0]
    rows = part_rows(entries)
    sz = Sizes(tokens, lengths)
    raw = jnp.pad(params, (0, rows * LANES - entries)).reshape(rows, LANES)
    any_spec = pl.BlockSpec(memory_space=pl.ANY)
    vmem = pl.BlockSpec(memory_space=pltpu.VMEM)
    smem = pl.BlockSpec(memory_space=pltpu.SMEM)
    saved = saved_shapes(sz)
    bf = jnp.bfloat16
    outs = pl.pallas_call(
        functools.partial(forward_kernel, place, entries, sz),
        out_shape=[jax.ShapeDtypeStruct(SHAPES[n], bf) for n in MATRICES]
        + [jax.ShapeDtypeStruct(*saved[n]) for n in SAVED]
        + [jax.ShapeDtypeStruct(TABLE, jnp.float32), jax.ShapeDtypeStruct(tokens.shape, bf)],
        in_specs=[vmem, vmem, smem],
        out_specs=[any_spec] * 12 + [vmem, vmem],
        scratch_shapes=[
            pltpu.VMEM((place.devices, rows, LANES), bf),
            pltpu.VMEM((stage_rows(GATHER_SPANS, rows), LANES), jnp.float32),
        ]
        + [pltpu.VMEM(SHAPES[n], bf) for n in MATRICES]
        + [pltpu.VMEM(*saved[n]) for n in SAVED]
        + [pltpu.VMEM((sz.total, D), jnp.float32)]
        + gather_sems(place)
        + [pltpu.SemaphoreType.DMA((4,)), pltpu.SemaphoreType.DMA((8,))],
        compiler_params=pltpu.CompilerParams(
            collective_id=0, has_side_effects=True, vmem_limit_bytes=67 * 10**6
        ),
        name="forward",
    )(raw, tokens, lengths)
    return dict(zip(MATRICES, outs[:4])), dict(zip(SAVED, outs[4:12])), outs[12], outs[13]


SUMS = tuple(VECTORS)


def backward_kernel(place, entries, sz, tokens, cotangent, lengths, table, *refs):
    mats, refs = dict(zip(MATRICES, refs[:4])), refs[4:]
    given, refs = dict(zip(SAVED, refs[:8])), refs[8:]
    out, input_grad, refs = refs[0], refs[1], refs[2:]
    own, cross, refs = refs[0], refs[1], refs[2:]
    n = place.classes
    slots, refs = refs[:n], refs[n:]
    cross_send, cross_recv, send = refs[:3]
    recv, refs = refs[3 : 3 + n], refs[3 + n :]
    stage, total, sums, refs = refs[0], refs[1], refs[2], refs[3:]
    big_a, big_b, refs = refs[0], refs[1], refs[2:]
    wide, slope, qkv, probs, mix, mid, narrow, x, g, temp, blank, load, done = refs
    me = place.coords()
    margin = own.shape[1]
    count = sz.total
    order = (G_NAME, ACT_NAME, W_FC2_NAME, SLOPE_NAME, MLP_IN_NAME, W_FC1_NAME, MID_NAME, MIX_NAME, X_NAME, QKV_NAME, PROBS_NAME)

    def fetches(name):
        sem = load.at[order.index(name)]
        if name in (G_NAME, X_NAME):
            src, dst = (cotangent, g) if name == G_NAME else (tokens, x)
            return [
                pltpu.make_async_copy(
                    src.at[sz.given(b)],
                    dst.at[sz.at(b)],
                    load.at[order.index(name) if b == 0 else len(order) + 10 + 2 * b + (name == G_NAME)],
                )
                for b in range(sz.buffers)
            ]
        return [pltpu.make_async_copy(*places[name], sem)]

    places = {
        ACT_NAME: (given[ACT_NAME], wide),
        SLOPE_NAME: (given[SLOPE_NAME], slope),
        MLP_IN_NAME: (given[MLP_IN_NAME], narrow),
        MID_NAME: (given[MID_NAME], mid),
        MIX_NAME: (given[MIX_NAME], mix),
        QKV_NAME: (given[QKV_NAME], qkv),
        PROBS_NAME: (given[PROBS_NAME], probs),
        W_FC2_NAME: (mats[W_FC2_NAME], big_a),
        W_FC1_NAME: (mats[W_FC1_NAME], big_b),
    }

    def begin(name):
        for c in fetches(name):
            c.start()

    def ready(name):
        for c in fetches(name):
            c.wait()

    for name in order:
        begin(name)
    greet(place, me)

    def sum_to(name, c, value):
        at = SUMS.index(name)
        sums[at : at + 1, c] = value

    def ones():
        return jnp.ones((8, count), jnp.bfloat16)

    def column_sums(name, ref, width):
        def body(c):
            sum_to(name, c, dot(ones(), ref[:, c])[0:1, :])

        columns(width, 256, body)

    def pieces(name, left, right, block):
        for span in [s for s in SCATTER_SPANS if s.name == name]:

            def body(i):
                first = pl.multiple_of(span.first + i * block, block)
                lay(stage, span, margin, first, dot(left[:, pl.ds(first, block)], right(), 0, 0))

            loop(span.depth // block, body)
            yield span

    def finish(span):
        lay_vectors(stage, span, margin, sums)
        cut(stage, span, own, entries)

    ready(G_NAME)
    for b in range(sz.buffers):
        rows = sz.at(b)
        valid = valid_rows(lengths, b, sz.images, sz.rows)
        g[rows, :] = low(g[rows, :].astype(jnp.float32) * valid)
    ready(ACT_NAME)
    column_sums(FC2_BIAS_NAME, g, D)
    for span in pieces(W_FC2_NAME, wide, lambda: g[...], 256):
        finish(span)

    ready(W_FC2_NAME)
    ready(SLOPE_NAME)

    def to_pre(i):
        c = pl.ds(pl.multiple_of(i * 256, 256), 256)
        made = dot(g[...], big_a[c, :], 1, 1)
        wide[:, c] = low(made * slope[:, c].astype(jnp.float32))

    loop(FF // 256, to_pre)
    late = [
        pltpu.make_async_copy(
            mats[W_QKV_NAME].at[:, i * D : (i + 1) * D],
            big_a.at[i * D : (i + 1) * D],
            load.at[len(order) + 8 + i],
        )
        for i in range(3)
    ]
    late.append(
        pltpu.make_async_copy(mats[W_PROJ_NAME], big_a.at[3 * D : 4 * D], load.at[len(order) + 11])
    )
    for c in reversed(late):
        c.start()
    ready(MLP_IN_NAME)
    column_sums(FC1_BIAS_NAME, wide, FF)
    for span in pieces(W_FC1_NAME, narrow, lambda: wide[...], 128):
        finish(span)

    attn_load = pltpu.make_async_copy(given[ATTN_IN_NAME], narrow, load.at[len(order) + 7])
    attn_load.start()
    ready(W_FC1_NAME)

    def to_mlp(i):
        c = pl.ds(pl.multiple_of(i * 256, 256), 256)
        temp[:, c] = dot(wide[...], big_b[c, :], 1, 1)

    loop(D // 256, to_mlp)
    ready(MID_NAME)

    def column_add(name, value, first):
        at = SUMS.index(name)
        part = jnp.sum(value, axis=0, keepdims=True)
        before = sums[at : at + 1, 0:D]
        sums[at : at + 1, 0:D] = part if first else before + part

    def clear(name):
        at = SUMS.index(name)
        sums[at : at + 1, 0:D] = jnp.zeros((1, D), jnp.float32)

    clear(LN2_GAIN_NAME)
    clear(LN2_BIAS_NAME)

    def back_second(i):
        normed, inv = normalize(mid[tile(i), :])
        d = temp[tile(i), :]
        column_add(LN2_GAIN_NAME, d * normed, False)
        column_add(LN2_BIAS_NAME, d, False)
        v = g[tile(i), :].astype(jnp.float32) + norm_back(d, normed, inv, vector(table, LN2_GAIN_NAME))
        mid[tile(i), :] = v
        g[tile(i), :] = low(v)

    loop(count // 16, back_second)
    ready(MIX_NAME)
    column_sums(PROJ_BIAS_NAME, g, D)
    for span in pieces(W_PROJ_NAME, mix, lambda: g[...], 256):
        finish(span)
    late[3].wait()

    def to_mix(i):
        c = pl.ds(pl.multiple_of(i * 256, 256), 256)
        rows = pl.ds(pl.multiple_of(3 * D + i * 256, 256), 256)
        slope[:, c] = low(dot(g[...], big_a[rows, :], 1, 1))

    loop(D // 256, to_mix)
    ready(QKV_NAME)
    ready(PROBS_NAME)
    for b in range(sz.buffers):
        rows = sz.at(b)

        def attend(p):
            halves = half_lanes(sz.rows)
            at = lambda part: pl.ds(pl.multiple_of(part * D + p * LANES, LANES), LANES)
            q, k, v = (qkv[rows, at(part)] for part in range(3))
            dm = slope[rows, at(0)]
            dq = dk = dv = 0.0
            for h in range(2):
                pr = probs[(b * sz.pairs + p) * 2 + h]
                dmh = dm * halves[h]
                dp = dot(dmh, v, 1, 1)
                prf = pr.astype(jnp.float32)
                ds = low(prf * (dp - jnp.sum(prf * dp, axis=-1, keepdims=True)))
                dv = dv + dot(pr, dmh, 0, 0)
                dq = dq + dot(ds, k * halves[h])
                dk = dk + dot(ds, q * halves[h], 0, 0)
            wide[rows, at(0)] = low(dq * SCALE)
            wide[rows, at(1)] = low(dk * SCALE)
            wide[rows, at(2)] = low(dv)

        loop(sz.pairs, attend)
    for c in late[:3]:
        c.wait()

    def to_attn(i):
        c = pl.ds(pl.multiple_of(i * 256, 256), 256)
        made = None
        for part in range(3):
            rows = pl.ds(pl.multiple_of(part * D + i * 256, 256), 256)
            term = dot(wide[:, part * D : (part + 1) * D], big_a[rows, :], 1, 1)
            made = term if made is None else made + term
        temp[:, c] = made

    loop(D // 256, to_attn)
    ready(X_NAME)
    clear(LN1_GAIN_NAME)
    clear(LN1_BIAS_NAME)

    def back_first(i):
        normed, inv = normalize(x[tile(i), :].astype(jnp.float32))
        d = temp[tile(i), :]
        column_add(LN1_GAIN_NAME, d * normed, False)
        column_add(LN1_BIAS_NAME, d, False)
        mid[tile(i), :] = mid[tile(i), :] + norm_back(d, normed, inv, vector(table, LN1_GAIN_NAME))

    loop(count // 16, back_first)
    outs = []
    for b in range(sz.buffers):
        outs.append(
            pltpu.make_async_copy(mid.at[sz.at(b)], input_grad.at[sz.given(b)], done.at[2 * b])
        )
        if sz.full > sz.rows:
            blank[...] = jnp.zeros(blank.shape, blank.dtype)
            outs.append(
                pltpu.make_async_copy(
                    blank,
                    input_grad.at[b * sz.full + sz.rows : (b + 1) * sz.full],
                    done.at[2 * b + 1],
                )
            )
    for c in outs:
        c.start()

    attn_load.wait()

    def qv_sums(c):
        wide_sum = dot(ones(), wide[:, c])[0:1, :]
        sums[len(SUMS) : len(SUMS) + 1, c] = wide_sum

    columns(3 * D, 256, qv_sums)
    for name, part in ((Q_BIAS_NAME, 0), (V_BIAS_NAME, 2)):
        at = SUMS.index(name)
        sums[at : at + 1, 0:D] = sums[len(SUMS) : len(SUMS) + 1, part * D : (part + 1) * D]
    for span in pieces(W_QKV_NAME, narrow, lambda: wide[:, 0 : 3 * D], 128):
        finish(span)

    scatter_all(place, me, own, cross, slots, total, (cross_send, cross_recv, send, recv))
    shift = (entries * place.flat(me)) % LANES
    back = (LANES - shift) % LANES
    rows = own.shape[1]

    def turn(i):
        total[tile(i), :] = pltpu.roll(total[tile(i), :], back, 1)

    loop(rows // 16, turn, 8)

    def merge(i):
        lane = lax.broadcasted_iota(jnp.int32, (16, LANES), 1)
        now = total[pl.ds(i * 16, 16), :]
        after = total[pl.ds(i * 16 + 1, 16), :]
        out[tile(i), :] = jnp.where(lane < LANES - shift, now, after)

    loop(rows // 16, merge, 8)
    for c in outs:
        c.wait()


def backward(place, tokens, cotangent, lengths, mats, saved, table, entries):
    rows = part_rows(entries)
    sz = Sizes(tokens, lengths)
    cross, slots, sems, recv = scatter_scratch(place, rows)
    any_spec = pl.BlockSpec(memory_space=pl.ANY)
    vmem = pl.BlockSpec(memory_space=pltpu.VMEM)
    smem = pl.BlockSpec(memory_space=pltpu.SMEM)
    bf, f32 = jnp.bfloat16, jnp.float32
    shapes = saved_shapes(sz)
    scratch = lambda name: pltpu.VMEM(*shapes[name])
    out, input_grad = pl.pallas_call(
        functools.partial(backward_kernel, place, entries, sz),
        out_shape=[
            jax.ShapeDtypeStruct((rows, LANES), f32),
            jax.ShapeDtypeStruct(tokens.shape, f32),
        ],
        in_specs=[any_spec, any_spec, smem, vmem] + [any_spec] * 12,
        out_specs=[vmem, any_spec],
        scratch_shapes=[pltpu.VMEM((place.devices, rows, LANES), bf)]
        + cross
        + slots
        + sems
        + recv
        + [
            pltpu.VMEM((stage_rows(SCATTER_SPANS, rows), LANES), f32),
            pltpu.VMEM((rows + 16, LANES), f32),
            pltpu.VMEM(TABLE, f32),
            pltpu.VMEM((FF, D), bf),
            pltpu.VMEM((D, FF), bf),
            scratch(ACT_NAME),
            scratch(SLOPE_NAME),
            scratch(QKV_NAME),
            scratch(PROBS_NAME),
            scratch(MIX_NAME),
            scratch(MID_NAME),
            scratch(MLP_IN_NAME),
            pltpu.VMEM((sz.total, D), bf),
            pltpu.VMEM((sz.total, D), bf),
            pltpu.VMEM((sz.total, D), f32),
            pltpu.VMEM((max(8, sz.full - sz.rows), D), f32),
            pltpu.SemaphoreType.DMA((24 + 2 * sz.buffers,)),
            pltpu.SemaphoreType.DMA((2 * sz.buffers,)),
        ],
        compiler_params=pltpu.CompilerParams(
            collective_id=1, has_side_effects=True, vmem_limit_bytes=67 * 10**6
        ),
        name=BACKWARD_NAME,
    )(tokens, cotangent, lengths, table, *[mats[m] for m in MATRICES], *[saved[s] for s in SAVED])
    return input_grad, out.reshape(-1)[:entries]


class Share:
    def __init__(self, place, name, depth, width, low):
        self.name, self.depth, self.half = name, depth, width // 2
        self.high = depth // place.chips
        self.low = low
        self.rows = self.high * (width // LANES)
        third = self.high // 3
        if name is None:
            self.parts = {2: (0, self.high, 0, self.half)}
        elif third % 32:
            first = -(-self.half // LANES // 2) * LANES
            self.parts = {
                2: (0, third, 0, self.half),
                3: (third, third, 0, self.half),
                0: (2 * third, third, 0, first),
                1: (2 * third, third, first, self.half - first),
            }
        else:
            self.parts = {
                2: (0, third, 0, self.half),
                3: (third, third, 0, self.half),
                0: (2 * third, third // 2, 0, self.half),
                1: (2 * third + third // 2, third // 2, 0, self.half),
            }


def shares(place):
    out = [Share(place, n, *SHAPES[n], BASES[n]) for n in MATRICES]
    return out + [Share(place, None, 16 * place.chips, 2 * LANES, None)]


VECTOR_LIST = [(n, j) for n in VECTORS for j in range(SHAPES[n][0] // LANES)]


def fits(place):
    return place.size == [2, 2, 4, 2]


def block_of(place, coords):
    return (coords[1] * 2 + coords[0]) * 4 + coords[2]


def chip_of(block):
    return [rest(quot(block, 4), 2), quot(block, 8), rest(block, 4)]


class Summing:
    def __init__(self, place, me, parts, own, cross, slots, send, recv, cross_send, cross_recv):
        self.place, self.me, self.parts = place, me, parts
        self.own, self.cross, self.slots = own, cross, slots
        self.send, self.recv = send, recv
        self.cross_send, self.cross_recv = cross_send, cross_recv
        self.plan = slot_plan(place, 16 * sum(place.shares))
        self.slot, self.sent = 0, []
        self.waits, self.then, self.left = {}, {}, {}

    def rect(self, p, k, dest):
        top, high, left, wide = self.parts[p].parts[k]
        row = block_of(self.place, dest) * self.parts[p].high + top
        return pl.multiple_of(row, 16), high, left, wide

    def swap(self, p, first, count, chunk):
        rows = pl.ds(pl.multiple_of(first, 16), count)
        return pltpu.make_async_remote_copy(
            src_ref=self.own[p].at[1 - self.me[CORE], rows, :],
            dst_ref=self.cross[p].at[rows, :],
            send_sem=self.cross_send.at[p, chunk],
            recv_sem=self.cross_recv.at[p, chunk],
            device_id=self.place.device(partner(self.me)),
            device_id_type=MESH,
        )

    def hand(self, p, k, pos, way, dest, to):
        row, high, left, wide = self.rect(p, k, dest)
        slot = slot_of(self.place, self.plan, k, pos, way, to, dest)
        return pltpu.make_async_remote_copy(
            src_ref=self.own[p].at[self.me[CORE], pl.ds(row, high), pl.ds(left, wide)],
            dst_ref=self.slots[p][k].at[slot],
            send_sem=self.send.at[p, k, self.place.chip(dest)],
            recv_sem=self.recv[p][k].at[slot],
            device_id=self.place.device(to),
            device_id_type=MESH,
        )

    def parents(self, k, rel, dest):
        order = self.place.orders[k]
        for pos in range(2, -1, -1):
            dim = order[pos]
            if rel[dim] == 0:
                continue
            if self.place.size[dim] == 2:
                other = list(self.me)
                other[dim] = 1 - other[dim]
                return [(True, pos, 0, other)]
            here, there = self.me[dim], dest[dim]
            return [
                (here > there, pos, 0, moved(self.me, dim, -1)),
                (here < there, pos, 1, moved(self.me, dim, 1)),
            ]
        return []

    def aim(self, x, y, turn):
        z = self.me[2]
        inner = pick(z >= 2, 3 - z, z)
        end, middle = TURNS[0][turn], TURNS[1][turn]
        at = pick(inner == 0, end, middle)
        dest = [
            1 - self.me[0] if x else self.me[0],
            1 - self.me[1] if y else self.me[1],
            pick(z >= 2, 3 - at, at),
        ]
        cond = inner == 0 if turn == 0 else inner == 1 if turn == 3 else True
        if turn == 4:
            dest[2] = z
        return cond, dest + [self.me[CORE]]

    def task(self, p, k, rel, dest):
        row, high, left, wide = self.rect(p, k, dest)
        core = self.me[CORE]
        cols = slice(left, left + wide)

        def add(terms):
            for i in range(high // 16):
                rows = pl.ds(pl.multiple_of(row + i * 16, 16), 16)
                value = self.own[p][core, rows, cols].astype(jnp.float32)
                for term in terms:
                    value = value + term(i, rows).astype(jnp.float32)
                self.own[p][core, rows, cols] = low(value)

        def kid(pos, way):
            slot = slot_of(self.place, self.plan, k, pos, way, self.me, dest)
            return lambda i, rows: self.slots[p][k][slot, i * 16 : (i + 1) * 16, :]

        kids = onward(self.place, self.place.orders[k], self.me, rel, dest)
        sure = [(pos, way) for cond, pos, way, _ in kids if cond is True]
        for pos, way in sure:
            self.hand(p, k, pos, way, dest, self.me).wait_recv()
        add([lambda i, rows: self.cross[p][rows, cols]] + [kid(*s) for s in sure])
        for cond, pos, way, _ in kids:
            if cond is True or cond is False:
                continue

            def take(pos=pos, way=way):
                self.hand(p, k, pos, way, dest, self.me).wait_recv()
                add([kid(pos, way)])

            pl.when(cond)(take)
        for cond, pos, way, to in self.parents(k, rel, dest):
            when(cond, lambda: self.hand(p, k, pos, way, dest, to).start())

    def offer(self, p, waits, then):
        self.waits[p], self.then[p] = waits, then
        self.left[p] = len(self.parts[p].parts)

    def step(self, p, k, x, y, turn):
        if p in self.waits:
            self.waits.pop(p)()
        cond, dest = self.aim(x, y, turn)
        rel = (x, y, 0 if turn == 4 else 1)
        when(cond, lambda: self.task(p, k, rel, dest))
        self.sent.append((p, k, x, y, turn))
        if x == y == 0 and turn == 4:
            self.left[p] -= 1
            if not self.left[p]:
                self.then[p]()

    def pump(self):
        self.slot += 1
        last = self.slot == len(SCHEDULE) - 1
        early, self.sent = (self.sent, []) if last else ([], self.sent)
        for code in SCHEDULE[self.slot]:
            p, k = len(MATRICES) - 1 - code // 80, (code // 20) % 4
            x, y, turn = (code // 10) % 2, (code // 5) % 2, code % 5
            self.step(p, k, x, y, turn)
            if p == 0 and k == 2:
                self.step(len(MATRICES), k, x, y, turn)
            for one in early[:4]:
                self.ended(*one)
            early = early[4:]
        self.sent = early + self.sent

    def ended(self, p, k, x, y, turn):
        known, dest = self.aim(x, y, turn)

        def wait():
            rel = (x, y, 0 if turn == 4 else 1)
            for cond, pos, way, to in self.parents(k, rel, dest):
                when(cond, lambda: self.hand(p, k, pos, way, dest, to).wait_send())

        if (x, y, turn) != (0, 0, 4):
            when(known, wait)

    def drain(self):
        for one in self.sent:
            self.ended(*one)


def most_blocks(part, entries):
    return ((entries + 2 * LANES) // LANES - 1) // part.rows + 2


def meeting(part, entries, block):
    start = (part.low + block * part.rows) * LANES
    return quot(start, entries), quot(start + part.rows * LANES - 1, entries)


def first_block(part, entries, flat):
    ahead = entries * flat - part.low * LANES
    return quot(pick(ahead > 0, ahead, 0), part.rows * LANES)


def deliver(place, me, parts, own, land, land_send, land_recv, vec_land, vec_send, vec_recv, local, entries):
    flat, core = place.flat(me), me[CORE]
    mine = block_of(place, me)
    devices = place.devices

    def device(d):
        return (quot(d, place.shape[1]), rest(d, place.shape[1]))

    def block_copy(p, block, to, which):
        part = parts[p]
        slot = block - first_block(part, entries, to)
        return pltpu.make_async_remote_copy(
            src_ref=own[p].at[core, pl.ds(pl.multiple_of(block * part.high, 16), part.high), :],
            dst_ref=land[p].at[slot, core],
            send_sem=land_send.at[p, which],
            recv_sem=land_recv[p].at[slot, core],
            device_id=device(to),
            device_id_type=MESH,
        )

    def block_local(p, block):
        part = parts[p]
        slot = block - first_block(part, entries, flat)
        return pltpu.make_async_copy(
            own[p].at[core, pl.ds(pl.multiple_of(block * part.high, 16), part.high), :],
            land[p].at[slot, core],
            local.at[p],
        )

    def sends(p):
        one, two = meeting(parts[p], entries, mine)
        return [
            (one != flat, one, 0),
            (jnp.logical_and(two != one, two != flat), two, 1),
        ], pick(one == flat, 1, pick(two == flat, 1, 0)) > 0

    def vector_pairs():
        out = []
        for v, (name, j) in enumerate(VECTOR_LIST):
            row = BASES[name] + j
            for d in range((row * LANES) // entries, ((row + 1) * LANES - 1) // entries + 1):
                if (v // 16, d) not in out:
                    out.append((v // 16, d))
        return out

    def vector_copy(n, block, d):
        return pltpu.make_async_remote_copy(
            src_ref=own[4].at[0, block * 16 : (block + 1) * 16, :],
            dst_ref=vec_land.at[block],
            send_sem=vec_send.at[n],
            recv_sem=vec_recv.at[block],
            device_id=device(d),
            device_id_type=MESH,
        )

    def start(p):
        remote, here = sends(p)
        for cond, to, which in remote:
            pl.when(cond)(lambda: block_copy(p, mine, to, which).start())
        pl.when(here)(lambda: block_local(p, mine).start())

    def start_vectors():
        for n, (block, d) in enumerate(vector_pairs()):
            home = place.flat(chip_of(block) + [0])
            if home == d:

                @pl.when(flat == d)
                def _():
                    vec_land[block] = own[4][0, block * 16 : (block + 1) * 16, :]

            else:
                pl.when(flat == home)(lambda: vector_copy(n, block, d).start())

    def expected(p):
        part = parts[p]
        low_block = first_block(part, entries, flat)
        top = part.low + part.rows * place.chips
        begins = part.low * LANES < entries * (flat + 1)
        ends = top * LANES > entries * flat
        for i in range(min(most_blocks(part, entries), place.chips)):
            block = low_block + i
            inside = (part.low + block * part.rows) * LANES < entries * (flat + 1)
            yield both_all(begins, ends, inside, block < place.chips), block, i

    def both_all(*conds):
        return functools.reduce(jnp.logical_and, conds)

    def finish(stage, margin, out):
        base = quot(entries * flat, LANES)
        for p in (3, 2, 1, 0):
            part = parts[p]
            blocks = 2 * part.half // LANES
            remote, here = sends(p)
            pl.when(here)(lambda: block_local(p, mine).wait())
            for cond, block, i in expected(p):

                def take():
                    for half in range(2):
                        source = place.flat(chip_of_traced(block) + [half])

                        @pl.when(source != flat)
                        def _():
                            pltpu.make_async_remote_copy(
                                src_ref=land[p].at[i, half],
                                dst_ref=land[p].at[i, half],
                                send_sem=land_send.at[p, 0],
                                recv_sem=land_recv[p].at[i, half],
                                device_id=device(source),
                                device_id_type=MESH,
                            ).wait_recv()

                    at = part.low + block * part.rows - base + margin
                    for r in range(part.high // 16):
                        for half in range(2):
                            for j in range(blocks // 2):
                                stage[
                                    pl.ds(
                                        at + r * 16 * blocks + half * (blocks // 2) + j,
                                        16,
                                        stride=blocks,
                                    ),
                                    :,
                                ] = land[p][
                                    i, half, r * 16 : (r + 1) * 16, j * LANES : (j + 1) * LANES
                                ].astype(jnp.float32)

                pl.when(cond)(take)
        for n, (block, d) in enumerate(vector_pairs()):
            home = place.flat(chip_of(block) + [0])

            @pl.when(flat == d)
            def _():
                if home != d:
                    vector_copy(n, block, d).wait_recv()
                for v in range(block * 16, min((block + 1) * 16, len(VECTOR_LIST))):
                    name, j = VECTOR_LIST[v]
                    row = BASES[name] + j
                    if (row * LANES) // entries <= d <= ((row + 1) * LANES - 1) // entries:
                        spot = row - (entries * d) // LANES + margin
                        stage[spot : spot + 1, :] = vec_land[block][
                            v % 16 : v % 16 + 1, :
                        ].astype(jnp.float32)

        shift = rest(entries * flat, LANES)
        back = rest(LANES - shift, LANES)
        rows = out.shape[0]

        def turn(i):
            at = pl.ds(pl.multiple_of(margin + i * 16, 16), 16)
            stage[at, :] = pltpu.roll(stage[at, :], back, 1)

        loop(rows // 16 + 1, turn, 8)

        def merge(i):
            lane = lax.broadcasted_iota(jnp.int32, (16, LANES), 1)
            now = stage[pl.ds(margin + i * 16, 16), :]
            after = stage[pl.ds(margin + i * 16 + 1, 16), :]
            out[tile(i), :] = jnp.where(lane < LANES - shift, now, after)

        loop(rows // 16, merge, 8)
        for p in range(4):
            for cond, to, which in sends(p)[0]:
                pl.when(cond)(lambda: block_copy(p, mine, to, which).wait_send())
        for n, (block, d) in enumerate(vector_pairs()):
            home = place.flat(chip_of(block) + [0])
            if home != d:
                pl.when(flat == home)(lambda: vector_copy(n, block, d).wait_send())

    return start, start_vectors, finish


def chip_of_traced(block):
    return [rest(quot(block, 4), 2), quot(block, 8), rest(block, 4)]


SCHEDULE = (
    (),
    (),
    (55, 78, 70),
    (),
    (50, 72, 60),
    (71, 56, 76),
    (77, 45, 58),
    (35, 5, 48, 7),
    (75, 155, 47, 46, 18),
    (158, 51, 40, 125, 137, 127, 6),
    (117, 150, 96, 65, 17, 135, 126, 74),
    (30, 19, 87, 15),
    (66, 95, 36, 111, 99),
    (61, 98, 110, 130, 89, 41),
    (114, 120, 68, 38, 116, 97, 32, 195, 233, 236, 115, 39, 140, 205, 145),
    (215, 238, 25, 151, 216),
    (138, 156, 62, 57, 33, 90, 8, 31, 37, 136, 85, 93, 105, 206, 235),
    (129, 67, 210, 153, 121, 196, 88),
    (146, 152, 200, 185, 157, 29, 113),
    (217, 191, 91, 207, 179, 141),
    (20, 52, 122, 73, 100, 197, 118, 59, 168, 92),
    (53, 79, 9, 211, 154, 106, 139, 131),
    (13, 94, 147, 230, 16, 128, 42, 80, 28, 49, 10, 26, 201, 86),
    (132, 178, 190, 159, 133, 208, 212, 225, 142),
    (69, 218, 231, 11, 108, 220, 232, 112, 0, 119, 107),
    (54, 81, 237, 63, 202, 175, 226, 186, 101),
    (1, 166, 199, 12, 193, 176, 198, 228, 165, 239, 221, 177, 298, 248, 278, 187, 123, 180, 21,
     170, 313, 64, 173, 310, 255, 227, 295, 245, 143, 285, 82, 315, 102, 174, 256, 172, 258,
     257, 2, 171, 275, 296, 276, 288, 316, 188, 181, 270, 160, 219, 203, 250, 192, 300, 305,
     290, 148, 318, 83, 109, 277, 161, 222, 311, 265, 134, 189, 43, 317, 167, 253, 149, 271,
     306, 266, 297, 163, 103, 246, 223, 280, 247, 268, 84, 213, 251, 291, 240, 169, 44, 312,
     286, 3, 259, 14, 260, 252, 272, 27, 209, 229, 301, 267, 194, 144, 104, 273, 124, 307, 182,
     23, 299, 292, 279, 241, 287, 308, 293, 162, 183, 34, 214, 261, 281, 249, 319, 234, 22, 243,
     302, 289, 274, 4, 164, 269, 303, 314, 204, 254, 283, 262, 294, 242, 184, 309, 282, 224,
     263, 24, 244, 304, 264, 284),
)
TURNS = ((3, 2, 1, 3, 0), (3, 3, 2, 0, 1))


def stage_margin(parts):
    return max(part.rows for part in parts[:4]) + 16


def even_kernel(place, entries, sz, tokens, cotangent, lengths, table, *refs):
    mats, refs = dict(zip(MATRICES, refs[:4])), refs[4:]
    given, refs = dict(zip(SAVED, refs[:8])), refs[8:]
    out, input_grad, refs = refs[0], refs[1], refs[2:]
    parts = shares(place)
    own, cross, land, refs = refs[:5], refs[5:10], refs[10:14], refs[14:]
    slots, recv = [], []
    for part in parts:
        slots.append(dict(zip(part.parts, refs)))
        refs = refs[len(part.parts) :]
    for part in parts:
        recv.append(dict(zip(part.parts, refs)))
        refs = refs[len(part.parts) :]
    send, cross_send, cross_recv, land_send, refs = *refs[:4], refs[4:]
    land_recv, refs = refs[:4], refs[4:]
    vec_land, vec_send, vec_recv, local, refs = *refs[:4], refs[4:]
    stage, sums, refs = refs[0], refs[1], refs[2:]
    big_a, big_b, refs = refs[0], refs[1], refs[2:]
    wide, slope, qkv, probs, mix, mid, narrow, x, g, temp, blank, partial, load, done = refs
    me = place.coords()
    flat = place.flat(me)
    count = sz.total
    order = (G_NAME, ACT_NAME, W_FC2_NAME, SLOPE_NAME, MLP_IN_NAME, W_FC1_NAME, MID_NAME, MIX_NAME, X_NAME, QKV_NAME, PROBS_NAME)

    def fetches(name):
        sem = load.at[order.index(name)]
        if name in (G_NAME, X_NAME):
            src, dst = (cotangent, g) if name == G_NAME else (tokens, x)
            return [
                pltpu.make_async_copy(
                    src.at[sz.given(b)],
                    dst.at[sz.at(b)],
                    load.at[order.index(name) if b == 0 else len(order) + 10 + 2 * b + (name == G_NAME)],
                )
                for b in range(sz.buffers)
            ]
        return [pltpu.make_async_copy(*places[name], sem)]

    places = {
        ACT_NAME: (given[ACT_NAME], wide),
        SLOPE_NAME: (given[SLOPE_NAME], slope),
        MLP_IN_NAME: (given[MLP_IN_NAME], narrow),
        MID_NAME: (given[MID_NAME], mid),
        MIX_NAME: (given[MIX_NAME], mix),
        QKV_NAME: (given[QKV_NAME], qkv),
        PROBS_NAME: (given[PROBS_NAME], probs),
        W_FC2_NAME: (mats[W_FC2_NAME], big_a),
        W_FC1_NAME: (mats[W_FC1_NAME], big_b),
    }

    def begin(name):
        for c in fetches(name):
            c.start()

    def ready(name):
        for c in fetches(name):
            c.wait()

    for name in order:
        begin(name)
    barrier = pltpu.get_barrier_semaphore()

    def hello(d):
        @pl.when(d != flat)
        def _():
            pl.semaphore_signal(
                barrier,
                inc=1,
                device_id=(quot(d, place.shape[1]), rest(d, place.shape[1])),
                device_id_type=MESH,
            )

    loop(place.devices, hello)
    adding = Summing(
        place, me, parts, own, cross, slots, send, recv, cross_send, cross_recv
    )
    start, start_vectors, finish = deliver(
        place, me, parts, own, land, land_send, land_recv, vec_land, vec_send, vec_recv, local, entries
    )

    def stepped(steps, body, groups):
        each = steps // groups
        for n in range(groups):
            loop(each, lambda i: body(n * each + i))
            adding.pump()

    def sum_to(name, c, value):
        at = SUMS.index(name)
        sums[at : at + 1, c] = value

    def ones():
        return jnp.ones((8, count), jnp.bfloat16)

    def column_sums(name, ref, width):
        def body(c):
            sum_to(name, c, dot(ones(), ref[:, c])[0:1, :])

        columns(width, 256, body)

    def pieces(name, left, right, block, groups):
        p = MATRICES.index(name)
        half = parts[p].half
        steps = parts[p].depth // block

        def body(i):
            first = pl.multiple_of(i * block, block)
            value = low(dot(left[:, pl.ds(first, block)], right(), 0, 0))
            own[p][0, pl.ds(first, block), :] = value[:, :half]
            own[p][1, pl.ds(first, block), :] = value[:, half:]
            adding.swap(p, first, block, i).start()

        waits = lambda: loop(steps, lambda i: adding.swap(p, i * block, block, i).wait_recv())
        adding.offer(p, waits, lambda: start(p))
        stepped(steps, body, groups)
        swaps.append((p, steps, block))

    swaps = []

    ready(G_NAME)
    for b in range(sz.buffers):
        rows = sz.at(b)
        valid = valid_rows(lengths, b, sz.images, sz.rows)
        g[rows, :] = low(g[rows, :].astype(jnp.float32) * valid)
    ready(ACT_NAME)
    column_sums(FC2_BIAS_NAME, g, D)
    pl.semaphore_wait(barrier, place.devices - 1)
    pieces(W_FC2_NAME, wide, lambda: g[...], 256, 1)

    ready(W_FC2_NAME)
    ready(SLOPE_NAME)

    def to_pre(i):
        c = pl.ds(pl.multiple_of(i * 256, 256), 256)
        made = dot(g[...], big_a[c, :], 1, 1)
        wide[:, c] = low(made * slope[:, c].astype(jnp.float32))

    stepped(FF // 256, to_pre, 3)
    late = [
        pltpu.make_async_copy(
            mats[W_QKV_NAME].at[:, i * D : (i + 1) * D],
            big_a.at[i * D : (i + 1) * D],
            load.at[len(order) + 8 + i],
        )
        for i in range(3)
    ]
    late.append(
        pltpu.make_async_copy(mats[W_PROJ_NAME], big_a.at[3 * D : 4 * D], load.at[len(order) + 11])
    )
    for c in reversed(late):
        c.start()
    ready(MLP_IN_NAME)
    column_sums(FC1_BIAS_NAME, wide, FF)
    pieces(W_FC1_NAME, narrow, lambda: wide[...], 128, 3)

    attn_load = pltpu.make_async_copy(given[ATTN_IN_NAME], narrow, load.at[len(order) + 7])
    attn_load.start()
    ready(W_FC1_NAME)

    def to_mlp(i):
        c = pl.ds(pl.multiple_of(i * 256, 256), 256)
        temp[:, c] = dot(wide[...], big_b[c, :], 1, 1)

    stepped(D // 256, to_mlp, 3)
    ready(MID_NAME)

    def folded(v):
        return v[0:8, :] + v[8:16, :]

    def norm_sums(body, gain, bias):
        partial[...] = jnp.zeros(partial.shape, jnp.float32)

        def step(i):
            for which, value in enumerate(body(i)):
                partial[which] += folded(value)

        loop(count // 16, step, 2)
        for which, name in enumerate((gain, bias)):
            at = SUMS.index(name)
            sums[at : at + 1, 0:D] = jnp.sum(partial[which], axis=0, keepdims=True)


    def back_second(i):
        normed, inv = normalize(mid[tile(i), :])
        d = temp[tile(i), :]
        v = g[tile(i), :].astype(jnp.float32) + norm_back(d, normed, inv, vector(table, LN2_GAIN_NAME))
        mid[tile(i), :] = v
        g[tile(i), :] = low(v)
        return d * normed, d

    norm_sums(back_second, LN2_GAIN_NAME, LN2_BIAS_NAME)
    ready(MIX_NAME)
    column_sums(PROJ_BIAS_NAME, g, D)
    adding.pump()
    pieces(W_PROJ_NAME, mix, lambda: g[...], 256, 1)
    late[3].wait()

    def to_mix(i):
        c = pl.ds(pl.multiple_of(i * 256, 256), 256)
        rows = pl.ds(pl.multiple_of(3 * D + i * 256, 256), 256)
        slope[:, c] = low(dot(g[...], big_a[rows, :], 1, 1))

    stepped(D // 256, to_mix, 1)
    ready(QKV_NAME)
    ready(PROBS_NAME)
    for b in range(sz.buffers):
        rows = sz.at(b)

        def attend(p):
            halves = half_lanes(sz.rows)
            at = lambda part: pl.ds(pl.multiple_of(part * D + p * LANES, LANES), LANES)
            q, k, v = (qkv[rows, at(part)] for part in range(3))
            dm = slope[rows, at(0)]
            dq = dk = dv = 0.0
            for h in range(2):
                pr = probs[(b * sz.pairs + p) * 2 + h]
                dmh = dm * halves[h]
                dp = dot(dmh, v, 1, 1)
                prf = pr.astype(jnp.float32)
                ds = low(prf * (dp - jnp.sum(prf * dp, axis=-1, keepdims=True)))
                dv = dv + dot(pr, dmh, 0, 0)
                dq = dq + dot(ds, k * halves[h])
                dk = dk + dot(ds, q * halves[h], 0, 0)
            wide[rows, at(0)] = low(dq * SCALE)
            wide[rows, at(1)] = low(dk * SCALE)
            wide[rows, at(2)] = low(dv)

        stepped(sz.pairs, attend, 3)
    for c in late[:3]:
        c.wait()

    def to_attn(i):
        c = pl.ds(pl.multiple_of(i * 256, 256), 256)
        made = None
        for part in range(3):
            rows = pl.ds(pl.multiple_of(part * D + i * 256, 256), 256)
            term = dot(wide[:, part * D : (part + 1) * D], big_a[rows, :], 1, 1)
            made = term if made is None else made + term
        temp[:, c] = made

    stepped(D // 256, to_attn, 3)
    ready(X_NAME)

    def back_first(i):
        normed, inv = normalize(x[tile(i), :].astype(jnp.float32))
        d = temp[tile(i), :]
        mid[tile(i), :] = mid[tile(i), :] + norm_back(d, normed, inv, vector(table, LN1_GAIN_NAME))
        return d * normed, d

    norm_sums(back_first, LN1_GAIN_NAME, LN1_BIAS_NAME)
    outs = []
    for b in range(sz.buffers):
        outs.append(
            pltpu.make_async_copy(mid.at[sz.at(b)], input_grad.at[sz.given(b)], done.at[2 * b])
        )
        if sz.full > sz.rows:
            blank[...] = jnp.zeros(blank.shape, blank.dtype)
            outs.append(
                pltpu.make_async_copy(
                    blank,
                    input_grad.at[b * sz.full + sz.rows : (b + 1) * sz.full],
                    done.at[2 * b + 1],
                )
            )
    for c in outs:
        c.start()

    attn_load.wait()

    def qv_sums(c):
        wide_sum = dot(ones(), wide[:, c])[0:1, :]
        sums[len(SUMS) : len(SUMS) + 1, c] = wide_sum

    columns(3 * D, 256, qv_sums)
    for name, part in ((Q_BIAS_NAME, 0), (V_BIAS_NAME, 2)):
        at = SUMS.index(name)
        sums[at : at + 1, 0:D] = sums[len(SUMS) : len(SUMS) + 1, part * D : (part + 1) * D]
    own[4][...] = jnp.zeros(own[4].shape, own[4].dtype)
    padded = round_up(len(VECTOR_LIST), 16)
    for v, (name, j) in enumerate(VECTOR_LIST):
        at = SUMS.index(name)
        stage[v : v + 1, :] = sums[at : at + 1, j * LANES : (j + 1) * LANES]
    stage[len(VECTOR_LIST) : padded, :] = jnp.zeros((padded - len(VECTOR_LIST), LANES), jnp.float32)
    own[4][0, 0:padded, :] = low(stage[0:padded, :])
    adding.swap(4, 0, parts[4].depth, 0).start()
    swaps.append((4, 1, parts[4].depth))
    adding.offer(4, lambda: adding.swap(4, 0, parts[4].depth, 0).wait_recv(), start_vectors)
    adding.pump()
    pieces(W_QKV_NAME, narrow, lambda: wide[:, 0 : 3 * D], 128, 3)
    finish(stage, stage_margin(parts), out)
    adding.drain()
    for p, steps, block in swaps:
        loop(steps, lambda i: adding.swap(p, i * block, block, i).wait_send())
    for c in outs:
        c.wait()


def even_backward(place, tokens, cotangent, lengths, mats, saved, table, entries):
    rows = part_rows(entries)
    sz = Sizes(tokens, lengths)
    parts = shares(place)
    dma = pltpu.SemaphoreType.DMA
    plan = slot_plan(place, rows)
    rects = [(part, k) for part in parts for k in part.parts]
    any_spec = pl.BlockSpec(memory_space=pl.ANY)
    vmem = pl.BlockSpec(memory_space=pltpu.VMEM)
    smem = pl.BlockSpec(memory_space=pltpu.SMEM)
    bf, f32 = jnp.bfloat16, jnp.float32
    shapes = saved_shapes(sz)
    scratch = lambda name: pltpu.VMEM(*shapes[name])
    out, input_grad = pl.pallas_call(
        functools.partial(even_kernel, place, entries, sz),
        out_shape=[
            jax.ShapeDtypeStruct((rows, LANES), f32),
            jax.ShapeDtypeStruct(tokens.shape, f32),
        ],
        in_specs=[any_spec, any_spec, smem, vmem] + [any_spec] * 12,
        out_specs=[vmem, any_spec],
        scratch_shapes=[pltpu.VMEM((2, part.depth, part.half), bf) for part in parts]
        + [pltpu.VMEM((part.depth, part.half), bf) for part in parts]
        + [
            pltpu.VMEM((most_blocks(part, entries), 2, part.high, part.half), bf)
            for part in parts[:4]
        ]
        + [
            pltpu.VMEM((plan[k][1], part.parts[k][1], part.parts[k][3]), bf) for part, k in rects
        ]
        + [dma((plan[k][1],)) for _, k in rects]
        + [dma((5, place.classes, place.chips)), dma((5, 12)), dma((5, 12)), dma((4, 2))]
        + [dma((most_blocks(part, entries), 2)) for part in parts[:4]]
        + [
            pltpu.VMEM((-(-len(VECTOR_LIST) // 16), 16, LANES), bf),
            dma((32,)),
            dma((-(-len(VECTOR_LIST) // 16),)),
            dma((4,)),
            pltpu.VMEM((2 * stage_margin(parts) + rows + 32, LANES), f32),
            pltpu.VMEM(TABLE, f32),
            pltpu.VMEM((FF, D), bf),
            pltpu.VMEM((D, FF), bf),
            scratch(ACT_NAME),
            scratch(SLOPE_NAME),
            scratch(QKV_NAME),
            scratch(PROBS_NAME),
            scratch(MIX_NAME),
            scratch(MID_NAME),
            scratch(MLP_IN_NAME),
            pltpu.VMEM((sz.total, D), bf),
            pltpu.VMEM((sz.total, D), bf),
            pltpu.VMEM((sz.total, D), f32),
            pltpu.VMEM((max(8, sz.full - sz.rows), D), f32),
            pltpu.VMEM((2, 8, D), f32),
            pltpu.SemaphoreType.DMA((24 + 2 * sz.buffers,)),
            pltpu.SemaphoreType.DMA((2 * sz.buffers,)),
        ],
        compiler_params=pltpu.CompilerParams(
            collective_id=1, has_side_effects=True, vmem_limit_bytes=67 * 10**6
        ),
        name=BACKWARD_NAME,
    )(tokens, cotangent, lengths, table, *[mats[m] for m in MATRICES], *[saved[s] for s in SAVED])
    return input_grad, out.reshape(-1)[:entries]


def solution(mesh):
    place = Place(mesh)

    def shards(tokens, cotangent, params, lengths):
        mats, saved, table, out = forward(place, tokens, params, lengths)
        input_grad, grad = (even_backward if fits(place) else backward)(
            place, tokens, cotangent, lengths, mats, saved, table, params.shape[0]
        )
        return out, input_grad, grad

    rows, flat = P(AXES, None), P(AXES)
    return jax.shard_map(
        shards,
        mesh=mesh,
        in_specs=(rows, rows, flat, rows),
        out_specs=(rows, rows, flat),
        check_vma=False,
    )
```
